32 devices in a mesh: clip: 8 (over z, x), head: 4 (over y, core).
Axes of the slice: x: 2, y: 2, z: 4, core: 2. Of those that a mesh axis runs over, the one named last changes fastest.
Arguments:
- patches: bfloat16 [8, 8, 196, 768], P('clip', None, 'head'), may hold values from -6 to 6
- cls_token: bfloat16 [8, 768], P('clip'), may hold values from -6 to 6
- keep_mask: int32 [8, 8, 196], P('clip'), may hold values 0 or 1
- gain_time: float32 [768], replicated, may hold values from 0.25 to 1.75
- qkv_time: bfloat16 [768, 12, 3, 64], P(None, 'head'), may hold values from -0.3125 to 0.3125
- proj_time: bfloat16 [12, 64, 768], P('head'), may hold values from -0.3125 to 0.3125
- temporal_fc: bfloat16 [768, 768], replicated, may hold values from -0.21875 to 0.21875
- gain_space: float32 [768], replicated, may hold values from 0.25 to 1.75
- qkv_space: bfloat16 [768, 12, 3, 64], P(None, 'head'), may hold values from -0.3125 to 0.3125
- proj_space: bfloat16 [12, 64, 768], P('head'), may hold values from -0.875 to 0.875
- gain_mlp: float32 [768], replicated, may hold values from 0.25 to 1.75
- mlp_in: bfloat16 [768, 3072], P(None, 'head'), may hold values from -0.21875 to 0.21875
- mlp_out: bfloat16 [3072, 768], P('head'), may hold values from -0.109375 to 0.109375
- cotangent: bfloat16 [8, 8, 196, 768], P('clip', None, 'head'), may hold values from -6 to 6
- cls_cotangent: bfloat16 [8, 768], P('clip'), may hold values from -6 to 6
Outputs:
- output: bfloat16 [8, 8, 196, 768], P('clip', None, 'head')
- output_cls: bfloat16 [8, 768], P('clip')
- input_grad: float32 [8, 8, 196, 768], P('clip', None, 'head')
- cls_grad: float32 [8, 768], P('clip')
- gain_time_grad: float32 [768], replicated
- qkv_time_grad: float32 [768, 12, 3, 64], P(None, 'head')
- proj_time_grad: float32 [12, 64, 768], P('head')
- temporal_fc_grad: float32 [768, 768], replicated
- gain_space_grad: float32 [768], replicated
- qkv_space_grad: float32 [768, 12, 3, 64], P(None, 'head')
- proj_space_grad: float32 [12, 64, 768], P('head')
- gain_mlp_grad: float32 [768], replicated
- mlp_in_grad: float32 [768, 3072], P(None, 'head')
- mlp_out_grad: float32 [3072, 768], P('head')
The draws below stay inside these ranges and needn't reach their ends.
Inputs may be any that keep to these rules, and one draw needn't show every extreme that they name: `keep_mask`: 1 keeps the patch token of that clip, frame and position; a dropped token's rows take no branch output.
All inputs are finite; a program needn't handle non-finite values. No bound on the sum of `keep_mask` on one device may be relied on, other than what follows from the above.
Results may differ from the reference program's by a relative error of at most 0.03.
The reference program's roundings to bfloat16 on the way count: a program that leaves them out, or rounds other values in their place, can miss the bound.
Values may be sent and summed in bfloat16 or wider, within the bound.
A program may use at most 128 MiB of HBM per device.

```python
import jax
import jax.numpy as jnp
from jax import lax

D = 768
HEADS = 12
HD = 64
FF = 3072
FRAMES = 8
PATCHES = 196
CLIPS = 8


def plant(drawn, stream_key, low, top_value):
    shape = drawn.shape
    index_at = [jax.random.randint(jax.random.fold_in(stream_key, axis), (), 0, shape[axis]) for axis in range(len(shape))]
    drawn = drawn.at[tuple(index_at)].set(low)
    longest = shape.index(max(shape))
    index_at[longest] = (index_at[longest] + 1) % shape[longest]
    return drawn.at[tuple(index_at)].set(top_value)


def block_scale(stream_key, extent, cuts, low, top_value):
    level = 1.0
    for dim, parts in cuts:
        heights = jax.random.uniform(jax.random.fold_in(jax.random.fold_in(stream_key, 6), dim), (parts,), jnp.float32, low / len(cuts), top_value / len(cuts))
        level = level * jnp.repeat(jnp.exp(heights), extent[dim] // parts).reshape((-1,) + (1,) * (len(extent) - 1 - dim))
    return level


def centred(stream_key, dims, scale, most, shards=(), held_as=jnp.bfloat16):
    drawn = jax.random.normal(stream_key, dims, jnp.float32) * scale
    if len(shards) > 0:
        drawn = block_scale(stream_key, dims, shards, -0.22, 0.18) * drawn
    return jnp.clip(drawn, min=-most, max=most).astype(held_as)


def setup_inputs(seed: int = 0) -> dict:
    arg_keys = jax.random.split(jax.random.key(seed), 16)
    patches = centred(arg_keys[0], (CLIPS, FRAMES, PATCHES, D), 1.0, 6.0, ((0, 8), (2, 4)))
    cls_token = centred(arg_keys[1], (CLIPS, D), 1.0, 6.0, ((0, 8),))
    keep_mask = plant((jax.random.randint(arg_keys[2], (CLIPS, FRAMES, PATCHES), 0, 25) < 23).astype(jnp.int32), jax.random.fold_in(arg_keys[2], 1), 0, 1)
    gain_time = jnp.clip(1.0 + 0.15 * jax.random.normal(arg_keys[3], (D,), jnp.float32), 0.25, 1.75)
    qkv_time = centred(arg_keys[4], (D, HEADS, 3, HD), (D // 2) ** -0.5, 0.3125, ((1, 4),))
    proj_time = centred(arg_keys[5], (HEADS, HD, D), (D // 2) ** -0.5, 0.3125, ((0, 4),))
    temporal_fc = centred(arg_keys[6], (D, D), D ** -0.5, 0.21875)
    gain_space = jnp.clip(1.0 + 0.15 * jax.random.normal(arg_keys[7], (D,), jnp.float32), 0.25, 1.75)
    qkv_space = centred(arg_keys[8], (D, HEADS, 3, HD), (D // 2) ** -0.5, 0.3125, ((1, 4),))
    proj_space = centred(arg_keys[9], (HEADS, HD, D), (D // 16) ** -0.5, 0.875, ((0, 4),))
    gain_mlp = jnp.clip(1.0 + 0.15 * jax.random.normal(arg_keys[10], (D,), jnp.float32), 0.25, 1.75)
    mlp_in = centred(arg_keys[11], (D, FF), D ** -0.5, 0.21875, ((1, 4),))
    mlp_out = centred(arg_keys[12], (FF, D), FF ** -0.5, 0.109375, ((0, 4),))
    cotangent = centred(arg_keys[13], (CLIPS, FRAMES, PATCHES, D), 1.0, 6.0, ((0, 8), (2, 4)))
    cls_cotangent = centred(arg_keys[14], (CLIPS, D), 1.0, 6.0, ((0, 8),))
    return dict(patches=patches, cls_token=cls_token, keep_mask=keep_mask, gain_time=gain_time, qkv_time=qkv_time, proj_time=proj_time, temporal_fc=temporal_fc, gain_space=gain_space, qkv_space=qkv_space, proj_space=proj_space, gain_mlp=gain_mlp, mlp_in=mlp_in, mlp_out=mlp_out, cotangent=cotangent, cls_cotangent=cls_cotangent)


HIGH = lax.Precision.HIGHEST
EPSILON = 1e-06
NEGATIVE = -1e+30

@jax.custom_vjp
def low(v):
    return lax.optimization_barrier(v.astype(jnp.bfloat16)).astype(jnp.float32)

@jax.custom_vjp
def low_back(v):
    return v

def low_keep(v):
    return (low(v), None)

def low_pass(kept, grad):
    return (grad,)

def back_keep(v):
    return (v, None)

def back_low(kept, grad):
    return (low(grad),)
low.defvjp(low_keep, low_pass)
low_back.defvjp(back_keep, back_low)

def layer_norm(values, gain):
    center = values - lax.optimization_barrier(jnp.mean(values, axis=-1, keepdims=True))
    spread = lax.optimization_barrier(jnp.mean(center * center, axis=-1, keepdims=True))
    return center * lax.rsqrt(spread + EPSILON) * gain

def clip_forward(weights, patch_rows, cls_row, keep_rows):
    gain_time, qkv_time, proj_time, temporal_fc, gain_space, qkv_space, proj_space, gain_mlp, mlp_in, mlp_out = weights
    scaling = HD ** (-0.5)
    keep_float = keep_rows.astype(jnp.float32)[..., None]
    normed = low(layer_norm(patch_rows, gain_time))
    triple = low_back(low(jnp.dot(normed, qkv_time.reshape(D, 3 * D), precision=HIGH)))
    triple = triple.reshape(FRAMES, PATCHES, HEADS, 3, HD)
    scores = low_back(jnp.einsum('fphe,gphe->phfg', triple[..., 0, :], triple[..., 1, :], precision=HIGH) * scaling)
    allowed = (keep_rows.T[:, None, None, :] > 0) | jnp.eye(FRAMES, dtype=bool)[None, None]
    weights_time = low(jax.nn.softmax(jnp.where(allowed, scores, NEGATIVE), axis=-1))
    mixed = jnp.einsum('phfg,gphe->fphe', weights_time, triple[..., 2, :], precision=HIGH)
    mixed = low_back(low(mixed)).reshape(FRAMES, PATCHES, D)
    attended = low_back(low(jnp.dot(mixed, proj_time.reshape(D, D), precision=HIGH)))
    temporal = low_back(jnp.dot(attended, temporal_fc, precision=HIGH))
    first = patch_rows + keep_float * temporal
    normed = low(layer_norm(first, gain_space))
    cls_normed = low(layer_norm(cls_row, gain_space))
    triple = low_back(low(jnp.dot(normed, qkv_space.reshape(D, 3 * D), precision=HIGH)))
    triple = triple.reshape(FRAMES, PATCHES, HEADS, 3, HD)
    cls_triple = low_back(low(jnp.dot(cls_normed, qkv_space.reshape(D, 3 * D), precision=HIGH)))
    cls_triple = cls_triple.reshape(HEADS, 3, HD)
    joined = jnp.concatenate([jnp.broadcast_to(cls_triple[None, None], (FRAMES, 1, HEADS, 3, HD)), triple], axis=1)
    scores = low_back(jnp.einsum('fqhe,fkhe->fhqk', joined[..., 0, :], joined[..., 1, :], precision=HIGH) * scaling)
    key_ok = jnp.concatenate([jnp.ones((FRAMES, 1), dtype=bool), keep_rows > 0], axis=1)
    weights_space = low(jax.nn.softmax(jnp.where(key_ok[:, None, None, :], scores, NEGATIVE), axis=-1))
    outputs = jnp.einsum('fhqk,fkhe->fqhe', weights_space, joined[..., 2, :], precision=HIGH)
    patch_mix = low_back(low(outputs[:, 1:])).reshape(FRAMES, PATCHES, D)
    cls_mix = low_back(low(lax.optimization_barrier(jnp.mean(outputs[:, 0], axis=0)))).reshape(D)
    spatial = low_back(jnp.dot(patch_mix, proj_space.reshape(D, D), precision=HIGH))
    cls_spatial = low_back(jnp.dot(cls_mix, proj_space.reshape(D, D), precision=HIGH))
    second = first + keep_float * spatial
    cls_second = cls_row + cls_spatial
    normed = low(layer_norm(second, gain_mlp))
    cls_normed = low(layer_norm(cls_second, gain_mlp))
    hidden = low_back(jnp.dot(normed, mlp_in, precision=HIGH))
    cls_hidden = low_back(jnp.dot(cls_normed, mlp_in, precision=HIGH))
    active = low(jax.nn.gelu(hidden, approximate=False))
    cls_active = low(jax.nn.gelu(cls_hidden, approximate=False))
    block_out = low_back(jnp.dot(active, mlp_out, precision=HIGH))
    cls_block = low_back(jnp.dot(cls_active, mlp_out, precision=HIGH))
    return (second + keep_float * block_out, cls_second + cls_block)

def reference(patches, cls_token, keep_mask, gain_time, qkv_time, proj_time, temporal_fc, gain_space, qkv_space, proj_space, gain_mlp, mlp_in, mlp_out, cotangent, cls_cotangent):
    weights = (gain_time.astype(jnp.float32), qkv_time.astype(jnp.float32), proj_time.astype(jnp.float32), temporal_fc.astype(jnp.float32), gain_space.astype(jnp.float32), qkv_space.astype(jnp.float32), proj_space.astype(jnp.float32), gain_mlp.astype(jnp.float32), mlp_in.astype(jnp.float32), mlp_out.astype(jnp.float32))

    def forward(weight_set, patch_all, cls_all):

        def per_clip(members):
            return clip_forward(weight_set, members[0], members[1], members[2])
        return lax.map(jax.checkpoint(per_clip), (patch_all, cls_all, keep_mask))
    results, pullback = jax.vjp(forward, weights, patches.astype(jnp.float32), cls_token.astype(jnp.float32))
    weight_grads, patch_grad, cls_grad = pullback((cotangent.astype(jnp.float32), cls_cotangent.astype(jnp.float32)))
    return (results[0].astype(jnp.bfloat16), results[1].astype(jnp.bfloat16), patch_grad, cls_grad, weight_grads[0], weight_grads[1], weight_grads[2], weight_grads[3], weight_grads[4], weight_grads[5], weight_grads[6], weight_grads[7], weight_grads[8], weight_grads[9])
```

```python
from functools import partial

import jax
import jax.numpy as jnp
from jax import lax
from jax.experimental import pallas as pl
from jax.experimental.pallas import tpu as pltpu
from jax.sharding import PartitionSpec as P

EPSILON = 1e-06
NEGATIVE = -1e30
F32 = jnp.float32
BF16 = jnp.bfloat16


def nn(a, b):
    return lax.dot_general(a, b, (((1,), (0,)), ((), ())), preferred_element_type=F32)


def nt(a, b):
    return lax.dot_general(a, b, (((1,), (1,)), ((), ())), preferred_element_type=F32)


def tn(a, b):
    return lax.dot_general(a, b, (((0,), (0,)), ((), ())), preferred_element_type=F32)


def tiles(total, size, body):
    def step(i, carry):
        body(pl.multiple_of(i * size, size))
        return carry

    lax.fori_loop(0, total // size, step, 0)


def stats(x):
    center = x - jnp.mean(x, axis=-1, keepdims=True)
    factor = lax.rsqrt(jnp.mean(center * center, axis=-1, keepdims=True) + EPSILON)
    return center * factor, factor


def norm_back(grad, gain, scaled, factor):
    weighted = grad * gain
    inner = weighted - jnp.mean(weighted, axis=-1, keepdims=True)
    return factor * (inner - scaled * jnp.mean(weighted * scaled, axis=-1, keepdims=True))


def pair_masks():
    lane = lax.broadcasted_iota(jnp.int32, (1, 128), 1)
    return (lane < 64).astype(F32).astype(BF16), (lane >= 64).astype(F32).astype(BF16)


def stacked(x):
    low, high = pair_masks()
    return jnp.concatenate([x * low, x * high], axis=0)


def unstacked(x):
    rows = x.shape[0] // 2
    lane = lax.broadcasted_iota(jnp.int32, (1, 128), 1)
    return jnp.where(lane < 64, x[:rows], x[rows:])


def norm_rows(x_ref, gain_ref, u_ref, chunk):
    def body(r):
        rows = pl.ds(r, chunk)
        scaled, _ = stats(x_ref[rows, :])
        u_ref[rows, :] = (scaled * gain_ref[...]).astype(BF16)

    tiles(x_ref.shape[0], chunk, body)


def project_qkv(u_ref, wt_ref, qkv_ref):
    width = u_ref.shape[1]

    def body(n):
        scale = jnp.where(n < width, 0.125, 1.0)
        out = nt(u_ref[...], wt_ref[pl.ds(n, 256), :]) * scale
        qkv_ref[:, pl.ds(n, 256)] = out.astype(BF16)

    tiles(wt_ref.shape[0], 256, body)


def qkv_grad_and_back(dqkv_ref, u_ref, wt_ref, dwt_ref, du_ref):
    def grad(n):
        dwt_ref[pl.ds(n, 256), :] = tn(dqkv_ref[:, pl.ds(n, 256)], u_ref[...]).astype(BF16)

    tiles(dqkv_ref.shape[1], 256, grad)

    def back(n):
        du_ref[:, pl.ds(n, 256)] = nn(dqkv_ref[...], wt_ref[:, pl.ds(n, 256)])

    tiles(u_ref.shape[1], 256, back)


def softmax(scores):
    highest = jnp.max(scores, axis=-1, keepdims=True)
    weights = jnp.exp(scores - highest)
    return weights * (1.0 / jnp.sum(weights, axis=-1, keepdims=True))


def attention(qkv_ref, p_ref, mix_ref, groups, bias_of):
    width = mix_ref.shape[1]

    def body(c):
        hp = c // 128
        for g, (start, size) in enumerate(groups):
            rows = pl.ds(start, size)
            q = qkv_ref[rows, pl.ds(c, 128)]
            k = qkv_ref[rows, pl.ds(pl.multiple_of(width + c, 128), 128)]
            v = qkv_ref[rows, pl.ds(pl.multiple_of(2 * width + c, 128), 128)]
            prob = softmax(nt(stacked(q), k) + bias_of(g, size))
            p_ref[hp, g, : 2 * size, :size] = prob
            mix_ref[rows, pl.ds(c, 128)] = unstacked(nn(prob.astype(BF16), v)).astype(BF16)

    tiles(width, 128, body)


def attention_back(qkv_ref, p_ref, dmix_ref, dqkv_ref, groups):
    width = dmix_ref.shape[1]

    def body(c):
        hp = c // 128
        kc = pl.multiple_of(width + c, 128)
        vc = pl.multiple_of(2 * width + c, 128)
        for g, (start, size) in enumerate(groups):
            rows = pl.ds(start, size)
            q = qkv_ref[rows, pl.ds(c, 128)]
            k = qkv_ref[rows, pl.ds(kc, 128)]
            v = qkv_ref[rows, pl.ds(vc, 128)]
            up = stacked(dmix_ref[rows, pl.ds(c, 128)])
            prob = p_ref[hp, g, : 2 * size, :size]
            dprob = nt(up, v)
            delta = jnp.sum(prob * dprob, axis=-1, keepdims=True)
            dscore = (prob * (dprob - delta)).astype(BF16)
            dqkv_ref[rows, pl.ds(c, 128)] = (unstacked(nn(dscore, k)) * 0.125).astype(BF16)
            dqkv_ref[rows, pl.ds(kc, 128)] = tn(dscore, stacked(q)).astype(BF16)
            dqkv_ref[rows, pl.ds(vc, 128)] = tn(prob.astype(BF16), up).astype(BF16)

    tiles(width, 128, body)


T_ROWS = 400
T_GROUPS = ((0, 96), (96, 96), (192, 96), (288, 112))


def time_bias(krow_ref):
    def bias_of(g, size):
        row = lax.broadcasted_iota(jnp.int32, (size, size), 0)
        col = lax.broadcasted_iota(jnp.int32, (size, size), 1)
        same = (row // 8) == (col // 8)
        kept = jnp.broadcast_to(krow_ref[g, :, :size], (size, size)) > 0.0
        ok = same & (kept | (row == col))
        bias = jnp.where(ok, 0.0, NEGATIVE)
        return jnp.concatenate([bias, bias], axis=0)

    return bias_of


def to_patch_order(src_ref, dst_ref, perm_ref):
    frames, count, width = src_ref.shape
    used = frames * count
    for j in range(width // 128):
        for f in range(frames):
            perm_ref[j, pl.ds(f, count, stride=frames), :] = src_ref[f, :, j * 128 : (j + 1) * 128].astype(F32)
        dst_ref[:used, j * 128 : (j + 1) * 128] = perm_ref[j, :used, :]
    dst_ref[used:, :] = jnp.zeros((T_ROWS - used, width), F32)


def to_frame_order(src_ref, dst_ref, perm_ref):
    frames, count, width = dst_ref.shape
    for j in range(width // 128):
        perm_ref[j, :, :] = src_ref[:, j * 128 : (j + 1) * 128]
        for f in range(frames):
            out = perm_ref[j, pl.ds(f, count, stride=frames), :]
            dst_ref[f, :, j * 128 : (j + 1) * 128] = out.astype(dst_ref.dtype)


def time_forward(
    patches_ref, krow_ref, kcol_ref, gain_ref, wt_ref, proj_ref, fc_ref,
    send_ref, u_ref, qkv_ref, p_ref, mix_ref, att_ref, x_ref, first_ref, perm_ref,
):
    width = patches_ref.shape[2]
    to_patch_order(patches_ref, x_ref, perm_ref)
    norm_rows(x_ref, gain_ref, u_ref, 80)
    project_qkv(u_ref, wt_ref, qkv_ref)
    attention(qkv_ref, p_ref, mix_ref, T_GROUPS, time_bias(krow_ref))

    def project(n):
        att_ref[:, pl.ds(n, 256)] = nn(mix_ref[...], proj_ref[:, pl.ds(n, 256)]).astype(BF16)

    tiles(width, 256, project)

    def branch(n):
        cols = pl.ds(n, 256)
        first_ref[:, cols] = x_ref[:, cols] + kcol_ref[...] * nn(att_ref[...], fc_ref[:, cols])

    tiles(width, 256, branch)
    to_frame_order(first_ref, send_ref, perm_ref)


def time_backward(
    dfirst_ref, patches_ref, kcol_ref, gain_ref, wt_ref, proj_ref, fc_ref, u_ref, qkv_ref, p_ref, mix_ref, att_ref,
    dx_ref, dwt_ref, dproj_ref, dfc_ref, dgain_ref,
    x_ref, df_ref, low_ref, datt_ref, dmix_ref, dqkv_ref, du_ref, perm_ref,
):
    width = patches_ref.shape[2]
    to_patch_order(patches_ref, x_ref, perm_ref)
    to_patch_order(dfirst_ref, df_ref, perm_ref)
    low_ref[...] = (df_ref[...] * kcol_ref[...]).astype(BF16)

    def first(n):
        cols = pl.ds(n, 256)
        dfc_ref[cols, :] = tn(att_ref[:, cols], low_ref[...]).astype(BF16)
        datt_ref[:, cols] = nt(low_ref[...], fc_ref[cols, :]).astype(BF16)

    tiles(width, 256, first)

    def second(n):
        cols = pl.ds(n, 256)
        dproj_ref[cols, :] = tn(mix_ref[:, cols], datt_ref[...]).astype(BF16)
        dmix_ref[:, cols] = nt(datt_ref[...], proj_ref[cols, :]).astype(BF16)

    tiles(width, 256, second)
    attention_back(qkv_ref, p_ref, dmix_ref, dqkv_ref, T_GROUPS)
    qkv_grad_and_back(dqkv_ref, u_ref, wt_ref, dwt_ref, du_ref)
    dgain_ref[...] = jnp.zeros_like(dgain_ref)

    def finish(r):
        rows = pl.ds(r, 80)
        scaled, factor = stats(x_ref[rows, :])
        grad = du_ref[rows, :]
        dgain_ref[...] += jnp.sum(grad * scaled, axis=0, keepdims=True)
        df_ref[rows, :] += norm_back(grad, gain_ref[...], scaled, factor)

    tiles(T_ROWS, 80, finish)
    to_frame_order(df_ref, dx_ref, perm_ref)


SEG = 208
S_ROWS = 416
S_GROUPS = ((0, 208), (208, 208))


def gather_frames(got_ref, cls_row, out_ref, sources, count):
    for f in range(2):
        base = f * SEG
        for s in range(sources):
            out_ref[base + s * count : base + (s + 1) * count, :] = got_ref[2 * s + f].astype(F32)
        at = base + sources * count
        out_ref[at : at + 1, :] = cls_row[f]
        out_ref[at + 1 : base + SEG, :] = jnp.zeros((SEG - 1 - sources * count, out_ref.shape[1]), F32)


def scatter_frames(x_ref, send_ref, sources, count):
    for f in range(2):
        for s in range(sources):
            at = f * SEG + s * count
            send_ref[2 * s + f] = x_ref[at : at + count, :].astype(send_ref.dtype)


def space_bias(krow_ref):
    def bias_of(g, size):
        bias = (krow_ref[g, :, :size] - 1.0) * -NEGATIVE
        return bias

    return bias_of


def space_forward(got_ref, cls_ref, krow_ref, gain_ref, wt_ref, x_ref, u_ref, qkv_ref, p_ref, mix_ref, cls_part_ref):
    sources, count = got_ref.shape[0] // 2, got_ref.shape[1]
    cls_row = cls_ref[...].astype(F32)
    gather_frames(got_ref, (cls_row, cls_row), x_ref, sources, count)
    norm_rows(x_ref, gain_ref, u_ref, 208)
    project_qkv(u_ref, wt_ref, qkv_ref)
    width = u_ref.shape[1]
    heads = width // 64
    at = sources * count
    lane = lax.broadcasted_iota(jnp.int32, (16, width), 1) // 64
    own = (lane == lax.broadcasted_iota(jnp.int32, (16, width), 0)).astype(F32)
    total = jnp.zeros((1, width), F32)
    for f in range(2):
        q = qkv_ref[f * SEG + at : f * SEG + at + 1, :width].astype(F32)
        k = qkv_ref[f * SEG : (f + 1) * SEG, width : 2 * width]
        v = qkv_ref[f * SEG : (f + 1) * SEG, 2 * width :]
        prob = softmax(nt((own * q).astype(BF16), k) + krow_bias(krow_ref, f))
        total += jnp.sum(own * nn(prob.astype(BF16), v), axis=0, keepdims=True)
    cls_part_ref[...] = total
    attention(qkv_ref, p_ref, mix_ref, S_GROUPS, lambda g, size: krow_bias(krow_ref, g))


def krow_bias(krow_ref, g):
    return (krow_ref[g, :, :SEG] - 1.0) * (-NEGATIVE)


def space_project(mix_ref, cls_total, x_ref, kcol_ref, proj_ref, second_ref, at):
    width = mix_ref.shape[1]
    rows = mix_ref[192:208, :]
    pick = lax.broadcasted_iota(jnp.int32, (16, 1), 0) == (at - 192)
    mix_ref[192:208, :] = jnp.where(pick, jnp.broadcast_to(cls_total, (16, width)), rows.astype(F32)).astype(BF16)

    def project(n):
        cols = pl.ds(n, 256)
        second_ref[:, cols] = x_ref[:, cols] + kcol_ref[...] * nn(mix_ref[...], proj_ref[:, cols])

    tiles(width, 256, project)


def mlp_stage(
    second_ref, cot_ref, kcol_ref, once_ref, gain_ref, w1_ref, w2_ref,
    out_ref, dsecond_ref, dw1_ref, dw2_ref, dgain_ref,
    u_ref, uw_ref, dz_ref, dzw_ref, acc_ref, du_ref,
):
    def prepare(r):
        rows = pl.ds(r, 208)
        scaled, _ = stats(second_ref[rows, :])
        u = (scaled * gain_ref[...]).astype(BF16)
        u_ref[rows, :] = u
        uw_ref[rows, :] = (u.astype(F32) * once_ref[rows, :]).astype(BF16)
        dz = cot_ref[rows, :] * kcol_ref[rows, :]
        dz_ref[rows, :] = dz.astype(BF16)
        dzw_ref[rows, :] = (dz * once_ref[rows, :]).astype(BF16)

    tiles(S_ROWS, 208, prepare)
    acc_ref[...] = jnp.zeros_like(acc_ref)
    du_ref[...] = jnp.zeros_like(du_ref)
    shard = w1_ref.shape[2]
    per = shard // 256

    def step(i, carry):
        s = i // per
        n = pl.multiple_of((i % per) * 256, 256)
        cols = pl.ds(n, 256)
        w1 = w1_ref[s, :, cols]
        w2 = w2_ref[s, cols, :]
        hid = nn(u_ref[...], w1)
        phi = 0.5 + 0.5 * lax.erf(hid * 0.7071067811865476)
        act = (hid * phi).astype(BF16)
        slope = phi + hid * (0.3989422804014327 * jnp.exp(hid * hid * -0.5))
        acc_ref[...] += nn(act, w2)
        dhid = (nt(dz_ref[...], w2) * slope).astype(BF16)
        dw2_ref[s, cols, :] = tn(act, dzw_ref[...]).astype(BF16)
        dw1_ref[s, :, cols] = tn(uw_ref[...], dhid).astype(BF16)
        du_ref[...] += nt(dhid, w1)
        return carry

    lax.fori_loop(0, w1_ref.shape[0] * per, step, 0)
    dgain_ref[...] = jnp.zeros_like(dgain_ref)

    def finish(r):
        rows = pl.ds(r, 208)
        x = second_ref[rows, :]
        scaled, factor = stats(x)
        out_ref[rows, :] = x + kcol_ref[rows, :] * acc_ref[rows, :]
        grad = du_ref[rows, :]
        dgain_ref[...] += jnp.sum(grad * scaled * once_ref[rows, :], axis=0, keepdims=True)
        dsecond_ref[rows, :] = cot_ref[rows, :] + norm_back(grad, gain_ref[...], scaled, factor)

    tiles(S_ROWS, 208, finish)


def space_backward(
    dsecond_ref, kcol_ref, once_ref, gain_ref, wt_ref, proj_ref, x_ref, u_ref, qkv_ref, p_ref, mix_ref,
    dfirst_ref, dwt_ref, dproj_ref, dgain_ref, dcls_ref,
    low_ref, loww_ref, dmix_ref, dqkv_ref, du_ref, at, frames,
):
    width = mix_ref.shape[1]
    low_ref[...] = (dsecond_ref[...] * kcol_ref[...]).astype(BF16)
    loww_ref[...] = (dsecond_ref[...] * (kcol_ref[...] * once_ref[...])).astype(BF16)
    pick = lax.broadcasted_iota(jnp.int32, (16, 1), 0) == (at - 192)
    cls_grad = jnp.broadcast_to(dsecond_ref[at : at + 1, :], (16, width))
    rest = low_ref[SEG + 192 : SEG + 208, :].astype(F32)
    low_ref[SEG + 192 : SEG + 208, :] = jnp.where(pick, cls_grad, rest).astype(BF16)

    def back(n):
        cols = pl.ds(n, 256)
        dproj_ref[cols, :] = tn(mix_ref[:, cols], loww_ref[...]).astype(BF16)
        dmix_ref[:, cols] = nt(low_ref[...], proj_ref[cols, :]).astype(BF16)

    tiles(width, 256, back)
    for f in range(2):
        rows = pl.ds(f * SEG + 192, 16)
        part = dmix_ref[rows, :].astype(F32)
        dmix_ref[rows, :] = jnp.where(pick, part * (1.0 / frames), part).astype(BF16)
    attention_back(qkv_ref, p_ref, dmix_ref, dqkv_ref, S_GROUPS)
    qkv_grad_and_back(dqkv_ref, u_ref, wt_ref, dwt_ref, du_ref)
    dgain_ref[...] = jnp.zeros_like(dgain_ref)
    dcls_ref[...] = du_ref[at : at + 1, :] + du_ref[SEG + at : SEG + at + 1, :]

    def finish(r):
        rows = pl.ds(r, 208)
        scaled, factor = stats(x_ref[rows, :])
        grad = du_ref[rows, :]
        dgain_ref[...] += jnp.sum(grad * scaled, axis=0, keepdims=True)
        dfirst_ref[rows, :] = dsecond_ref[rows, :] + norm_back(grad, gain_ref[...], scaled, factor)

    tiles(S_ROWS, 208, finish)


VM = pl.BlockSpec(memory_space=pltpu.VMEM)


def call(body, outs, scratch, *args):
    return pl.pallas_call(
        body,
        out_shape=[jax.ShapeDtypeStruct(s, d) for s, d in outs],
        in_specs=[VM] * len(args),
        out_specs=[VM] * len(outs),
        scratch_shapes=[pltpu.VMEM(s, d) for s, d in scratch],
        compiler_params=pltpu.CompilerParams(vmem_limit_bytes=60 << 20),
    )(*args)


def local(
    patches, cls_token, keep_mask, gain_time, qkv_time, proj_time, temporal_fc, gain_space, qkv_space, proj_space,
    gain_mlp, mlp_in, mlp_out, cotangent, cls_cotangent,
):
    _, frames, count, width = patches.shape
    members = lax.axis_size("head")
    me = lax.axis_index("head")
    heads_here, hd = qkv_time.shape[1], qkv_time.shape[3]
    at = members * count

    def swap(x, bit):
        return lax.ppermute(x, "head", [(i, i ^ bit) for i in range(members)])

    def gather(w):
        far = swap(w, 2)
        return jnp.stack([w, swap(w, 1), far, swap(far, 1)])

    def flat_t(w):
        return jnp.transpose(w, (2, 1, 3, 0)).reshape(3, heads_here * hd, width)

    def all_t(w):
        g = gather(flat_t(w))
        return jnp.transpose(g, (1, 0, 2, 3)).reshape(3 * width, width)

    wt_time, wt_space = all_t(qkv_time), all_t(qkv_space)
    pt = gather(proj_time.reshape(-1, width)).reshape(width, width)
    ps = gather(proj_space.reshape(-1, width)).reshape(width, width)
    w1, w2 = gather(mlp_in), gather(mlp_out)
    gt, gs, gm = gain_time[None], gain_space[None], gain_mlp[None]

    keep = keep_mask[0].astype(F32)
    here = lax.dynamic_slice_in_dim(keep, me * count, count, axis=1)
    kt = jnp.pad(here.T.reshape(-1), (0, T_ROWS - frames * count))
    kt_col = kt[:, None]
    kt_row = jnp.stack([jnp.pad(kt[s : s + n], (0, 128 - n)) for s, n in T_GROUPS])[:, None, :]
    mine = lax.dynamic_slice_in_dim(keep, me * 2, 2, axis=0)
    ks_row = jnp.pad(mine, ((0, 0), (0, 256 - at))).at[:, at].set(1.0)[:, None, :]
    first_only = jnp.array([1.0, 0.0], F32)[:, None]
    ks_col = jnp.concatenate([mine, first_only, jnp.zeros((2, SEG - 1 - at), F32)], axis=1).reshape(-1, 1)
    row_id = jnp.arange(S_ROWS)
    once = jnp.where((row_id == at) & (me != 0), 0.0, 1.0).astype(F32)[:, None]

    def exchange(x):
        return lax.all_to_all(x, "head", split_axis=0, concat_axis=0, tiled=True)

    cot = exchange(cotangent[0])
    cls_cot = cls_cotangent.astype(F32)

    send, u_t, qkv_t, p_t, mix_t, att_t = call(
        lambda *r: time_forward(*r[:7], *r[7:]),
        [((frames, count, width), BF16), ((T_ROWS, width), BF16), ((T_ROWS, 3 * width), BF16),
         ((6, 4, 224, 128), F32), ((T_ROWS, width), BF16), ((T_ROWS, width), BF16)],
        [((T_ROWS, width), F32), ((T_ROWS, width), F32), ((width // 128, T_ROWS, 128), F32)],
        patches[0], kt_row, kt_col, gt, wt_time, pt, temporal_fc,
    )
    got = exchange(send)
    x_s, u_s, qkv_s, p_s, mix_s, cls_part = call(
        space_forward,
        [((S_ROWS, width), F32), ((S_ROWS, width), BF16), ((S_ROWS, 3 * width), BF16),
         ((6, 2, 416, 256), F32), ((S_ROWS, width), BF16), ((1, width), F32)],
        [],
        got, cls_token, ks_row, gs, wt_space,
    )
    part = cls_part.reshape(members, -1)
    part = part + swap(part, 1)[jnp.array([1, 0, 3, 2])]
    part = part + swap(part, 2)[jnp.array([2, 3, 0, 1])]
    cls_total = part.reshape(1, width) * (1.0 / frames)

    def mlp_body(mix_ref, tot_ref, x_ref, kcol_ref, once_ref, ps_ref, cot_ref, ccot_ref, gain_ref, w1_ref, w2_ref,
                 out_ref, ocls_ref, dsec_ref, dw1_ref, dw2_ref, dg_ref, mixo_ref,
                 second_ref, cotx_ref, u_ref, uw_ref, dz_ref, dzw_ref, acc_ref, du_ref):
        mixo_ref[...] = mix_ref[...]
        space_project(mixo_ref, tot_ref[...], x_ref, kcol_ref, ps_ref, second_ref, at)
        zero = jnp.zeros((1, width), F32)
        gather_frames(cot_ref, (ccot_ref[...], zero), cotx_ref, members, count)
        mlp_stage(second_ref, cotx_ref, kcol_ref, once_ref, gain_ref, w1_ref, w2_ref,
                  acc_ref, dsec_ref, dw1_ref, dw2_ref, dg_ref, u_ref, uw_ref, dz_ref, dzw_ref, acc_ref, du_ref)
        scatter_frames(acc_ref, out_ref, members, count)
        ocls_ref[...] = acc_ref[at : at + 1, :].astype(BF16)

    out_send, out_cls, dsecond, dw1, dw2, dg_mlp, mix_s = call(
        mlp_body,
        [((frames, count, width), BF16), ((1, width), BF16), ((S_ROWS, width), F32),
         (w1.shape, BF16), (w2.shape, BF16), ((1, width), F32), ((S_ROWS, width), BF16)],
        [((S_ROWS, width), F32), ((S_ROWS, width), F32), ((S_ROWS, width), BF16), ((S_ROWS, width), BF16),
         ((S_ROWS, width), BF16), ((S_ROWS, width), BF16), ((S_ROWS, width), F32), ((S_ROWS, width), F32)],
        mix_s, cls_total, x_s, ks_col, once, ps, cot, cls_cot, gm, w1, w2,
    )
    output = exchange(out_send)

    def sb_body(*r):
        ins, outs, scr = r[:11], r[11:17], r[17:]
        dfs_ref, dcls_ref, dwt_ref, dproj_ref, dg_ref, dc2_ref = outs
        space_backward(*ins, scr[0], dwt_ref, dproj_ref, dg_ref, dcls_ref, *scr[1:], at, frames)
        scatter_frames(scr[0], dfs_ref, members, count)
        dc2_ref[...] = ins[0][at : at + 1, :]

    df_send, dcls_part, dwt_s, dps, dg_space, dcls_second = call(
        sb_body,
        [((frames, count, width), BF16), ((1, width), F32), ((3 * width, width), BF16), ((width, width), BF16),
         ((1, width), F32), ((1, width), F32)],
        [((S_ROWS, width), F32), ((S_ROWS, width), BF16), ((S_ROWS, width), BF16), ((S_ROWS, width), BF16),
         ((S_ROWS, 3 * width), BF16), ((S_ROWS, width), F32)],
        dsecond, ks_col, once, gs, wt_space, ps, x_s, u_s, qkv_s, p_s, mix_s,
    )
    dfirst = exchange(df_send)
    du_cls = lax.psum(dcls_part, "head")
    scaled, factor = stats(cls_token.astype(F32))
    cls_grad = dcls_second + norm_back(du_cls, gs, scaled, factor)

    dx, dwt_t, dpt, dfc, dg_time = call(
        lambda *r: time_backward(*r),
        [((frames, count, width), F32), ((3 * width, width), BF16), ((width, width), BF16), ((width, width), BF16),
         ((1, width), F32)],
        [((T_ROWS, width), F32), ((T_ROWS, width), F32), ((T_ROWS, width), BF16), ((T_ROWS, width), BF16),
         ((T_ROWS, width), BF16), ((T_ROWS, 3 * width), BF16), ((T_ROWS, width), F32),
         ((width // 128, T_ROWS, 128), F32)],
        dfirst, patches[0], kt_col, gt, wt_time, pt, temporal_fc, u_t, qkv_t, p_t, mix_t, att_t,
    )

    def reduce(g):
        pair = g[0::2] + swap(g[1::2], 1)
        own = pair[0] + swap(pair[1], 2)
        return lax.psum(own, "clip").astype(F32)

    def by_shard(dwt):
        return jnp.transpose(dwt.reshape(3, members, -1, width), (1, 0, 2, 3)).reshape(members, -1, width)

    def untie(own):
        return jnp.transpose(own.reshape(3, heads_here, hd, width), (3, 1, 0, 2))

    d_qt = untie(reduce(by_shard(dwt_t)))
    d_qs = untie(reduce(by_shard(dwt_s)))
    d_pt = reduce(dpt.reshape(members, -1, width)).reshape(proj_time.shape)
    d_ps = reduce(dps.reshape(members, -1, width)).reshape(proj_space.shape)
    d_w1, d_w2 = reduce(dw1), reduce(dw2)
    d_fc = lax.psum(dfc, ("clip", "head")).astype(F32)
    d_gt, d_gs, d_gm = lax.psum((dg_time[0], dg_space[0], dg_mlp[0]), ("clip", "head"))
    return (
        output[None], out_cls, dx[None], cls_grad, d_gt, d_qt, d_pt, d_fc, d_gs, d_qs, d_ps, d_gm, d_w1, d_w2,
    )


def solution(mesh):
    rows, wide, by_head = P("clip", None, "head", None), P("clip", None), P(None, "head", None, None)
    in_specs = (
        rows, wide, P("clip", None, None), P(), by_head, P("head", None, None), P(), P(), by_head,
        P("head", None, None), P(), P(None, "head"), P("head", None), rows, wide,
    )
    out_specs = (
        rows, wide, rows, wide, P(), by_head, P("head", None, None), P(), P(), by_head,
        P("head", None, None), P(), P(None, "head"), P("head", None),
    )
    return jax.shard_map(local, mesh=mesh, in_specs=in_specs, out_specs=out_specs, check_vma=False)
```

```python
from functools import partial
from types import SimpleNamespace

import jax
import jax.numpy as jnp
from jax import lax
from jax.experimental import pallas as pl
from jax.experimental.pallas import tpu as pltpu
from jax.sharding import PartitionSpec as P

EPSILON = 1e-06
NEGATIVE = -1e30
F32 = jnp.float32
BF16 = jnp.bfloat16


def nn(a, b):
    return lax.dot_general(a, b, (((1,), (0,)), ((), ())), preferred_element_type=F32)


def nt(a, b):
    return lax.dot_general(a, b, (((1,), (1,)), ((), ())), preferred_element_type=F32)


def tn(a, b):
    return lax.dot_general(a, b, (((0,), (0,)), ((), ())), preferred_element_type=F32)


def tiles(total, size, body):
    def step(i, carry):
        body(pl.multiple_of(i * size, size))
        return carry

    lax.fori_loop(0, total // size, step, 0)


def stats(x):
    center = x - jnp.mean(x, axis=-1, keepdims=True)
    factor = lax.rsqrt(jnp.mean(center * center, axis=-1, keepdims=True) + EPSILON)
    return center * factor, factor


def norm_back(grad, gain, scaled, factor):
    weighted = grad * gain
    inner = weighted - jnp.mean(weighted, axis=-1, keepdims=True)
    return factor * (inner - scaled * jnp.mean(weighted * scaled, axis=-1, keepdims=True))


def pair_masks():
    lane = lax.broadcasted_iota(jnp.int32, (1, 128), 1)
    return (lane < 64).astype(F32).astype(BF16), (lane >= 64).astype(F32).astype(BF16)


def stacked(x):
    low, high = pair_masks()
    return jnp.concatenate([x * low, x * high], axis=0)


def unstacked(x):
    rows = x.shape[0] // 2
    lane = lax.broadcasted_iota(jnp.int32, (1, 128), 1)
    return jnp.where(lane < 64, x[:rows], x[rows:])


def norm_rows(x_ref, gain_ref, u_ref, total, chunk):
    def body(r):
        rows = pl.ds(r, chunk)
        scaled, _ = stats(x_ref[rows, :])
        u_ref[rows, :] = (scaled * gain_ref[...]).astype(BF16)

    tiles(total, chunk, body)


def project_qkv(u_ref, wt_ref, qkv_ref, rows, start, size):
    width = u_ref.shape[1]

    def body(t, carry):
        scale = jnp.where(t == 0, 0.125, 1.0)
        out = nt(u_ref[:rows, :], wt_ref[t, start : start + size, :]) * scale
        qkv_ref[:rows, pl.ds(pl.multiple_of(t * width + start, 128), size)] = out.astype(BF16)
        return carry

    lax.fori_loop(0, 3, body, 0)


def qkv_back(dqkv_ref, u_ref, wt_ref, du_ref, rows):
    width = u_ref.shape[1]

    def back(n):
        cols = pl.ds(n, 256)
        total = nn(dqkv_ref[:rows, :width], wt_ref[0, :, cols])
        total += nn(dqkv_ref[:rows, width : 2 * width], wt_ref[1, :, cols])
        total += nn(dqkv_ref[:rows, 2 * width :], wt_ref[2, :, cols])
        du_ref[:rows, cols] = total

    tiles(width, 256, back)

    def grad(i, carry):
        n = pl.multiple_of((i % 3) * 256, 256)
        cols = pl.ds(pl.multiple_of(i * 256, 256), 256)
        wt_ref[i // 3, pl.ds(n, 256), :] = tn(dqkv_ref[:rows, cols], u_ref[:rows, :]).astype(BF16)
        return carry

    lax.fori_loop(0, 9, grad, 0)


def softmax(scores):
    highest = jnp.max(scores, axis=-1, keepdims=True)
    weights = jnp.exp(scores - highest)
    return weights * (1.0 / jnp.sum(weights, axis=-1, keepdims=True))


def attention(qkv_ref, p_ref, mix_ref, groups, bias_of, first, last):
    width = mix_ref.shape[1]

    def body(hp, carry):
        qc = pl.ds(pl.multiple_of(hp * 128, 128), 128)
        kc = pl.ds(pl.multiple_of(width + hp * 128, 128), 128)
        vc = pl.ds(pl.multiple_of(2 * width + hp * 128, 128), 128)
        for g, (start, size) in enumerate(groups):
            rows = pl.ds(start, size)
            prob = softmax(nt(stacked(qkv_ref[rows, qc]), qkv_ref[rows, kc]) + bias_of(g, size))
            p_ref[hp, g, : 2 * size, :size] = prob
            mix_ref[rows, qc] = unstacked(nn(prob.astype(BF16), qkv_ref[rows, vc])).astype(BF16)
        return carry

    lax.fori_loop(first, last, body, 0)


def attention_back(qkv_ref, p_ref, dmix_ref, dqkv_ref, groups):
    width = dmix_ref.shape[1]

    def body(hp, carry):
        qc = pl.ds(pl.multiple_of(hp * 128, 128), 128)
        kc = pl.ds(pl.multiple_of(width + hp * 128, 128), 128)
        vc = pl.ds(pl.multiple_of(2 * width + hp * 128, 128), 128)
        for g, (start, size) in enumerate(groups):
            rows = pl.ds(start, size)
            up = stacked(dmix_ref[rows, qc])
            prob = p_ref[hp, g, : 2 * size, :size]
            dprob = nt(up, qkv_ref[rows, vc])
            delta = jnp.sum(prob * dprob, axis=-1, keepdims=True)
            dscore = (prob * (dprob - delta)).astype(BF16)
            dqkv_ref[rows, qc] = (unstacked(nn(dscore, qkv_ref[rows, kc])) * 0.125).astype(BF16)
            dqkv_ref[rows, kc] = tn(dscore, stacked(qkv_ref[rows, qc])).astype(BF16)
            dqkv_ref[rows, vc] = tn(prob.astype(BF16), up).astype(BF16)
        return carry

    lax.fori_loop(0, width // 128, body, 0)


T_ROWS = 400
T_GROUPS = ((0, 96), (96, 96), (192, 96), (288, 112))
SEG = 208
S_ROWS = 416
S_GROUPS = ((0, 208), (208, 208))


def time_bias(krow_ref):
    def bias_of(g, size):
        row = lax.broadcasted_iota(jnp.int32, (size, size), 0)
        col = lax.broadcasted_iota(jnp.int32, (size, size), 1)
        same = (row // 8) == (col // 8)
        kept = jnp.broadcast_to(krow_ref[g, :, :size], (size, size)) > 0.0
        ok = same & (kept | (row == col))
        bias = jnp.where(ok, 0.0, NEGATIVE)
        return jnp.concatenate([bias, bias], axis=0)

    return bias_of


def space_bias(krow_ref, g):
    return (krow_ref[g, :, :SEG] - 1.0) * (-NEGATIVE)


def to_patch_order(src_ref, dst_ref, perm_ref):
    frames, count, width = src_ref.shape
    used = frames * count
    for j in range(width // 128):
        for f in range(frames):
            perm_ref[j, pl.ds(f, count, stride=frames), :] = src_ref[f, :, j * 128 : (j + 1) * 128].astype(F32)
        dst_ref[:used, j * 128 : (j + 1) * 128] = perm_ref[j, :used, :]
    dst_ref[used:T_ROWS, :] = jnp.zeros((T_ROWS - used, width), F32)


def to_frame_order(src_ref, dst_ref, perm_ref):
    frames, count, width = dst_ref.shape
    for j in range(width // 128):
        perm_ref[j, :, :] = src_ref[:T_ROWS, j * 128 : (j + 1) * 128]
        for f in range(frames):
            out = perm_ref[j, pl.ds(f, count, stride=frames), :]
            dst_ref[f, :, j * 128 : (j + 1) * 128] = out.astype(dst_ref.dtype)


def gather_frames(got_ref, cls_row, out_ref):
    sources, count = got_ref.shape[0] // 2, got_ref.shape[1]
    for f in range(2):
        base = f * SEG
        for s in range(sources):
            out_ref[base + s * count : base + (s + 1) * count, :] = got_ref[2 * s + f].astype(F32)
        at = base + sources * count
        out_ref[at : at + 1, :] = cls_row[f]
        out_ref[at + 1 : base + SEG, :] = jnp.zeros((SEG - 1 - sources * count, out_ref.shape[1]), F32)


def scatter_frames(x_ref, send_ref):
    sources, count = send_ref.shape[0] // 2, send_ref.shape[1]
    for f in range(2):
        for s in range(sources):
            at = f * SEG + s * count
            send_ref[2 * s + f] = x_ref[at : at + count, :].astype(send_ref.dtype)


def cls_attention(qkv_ref, krow_ref, at, width):
    lane = lax.broadcasted_iota(jnp.int32, (16, width), 1) // 64
    own = (lane == lax.broadcasted_iota(jnp.int32, (16, width), 0)).astype(F32)
    total = jnp.zeros((1, width), F32)
    for f in range(2):
        q = qkv_ref[f * SEG + at : f * SEG + at + 1, :width].astype(F32)
        k = qkv_ref[f * SEG : (f + 1) * SEG, width : 2 * width]
        v = qkv_ref[f * SEG : (f + 1) * SEG, 2 * width :]
        prob = softmax(nt((own * q).astype(BF16), k) + space_bias(krow_ref, f))
        total += jnp.sum(own * nn(prob.astype(BF16), v), axis=0, keepdims=True)
    return total


def blocks_swapped(x, distance):
    width = x.shape[1]
    quarter = width // 4
    order = [i ^ distance for i in range(4)]
    return jnp.concatenate([x[:, i * quarter : (i + 1) * quarter] for i in order], axis=1)


def set_row(ref, base, at, row, dtype):
    start = base + at // 16 * 16
    pick = lax.broadcasted_iota(jnp.int32, (16, 1), 0) == at % 16
    kept = ref[start : start + 16, :].astype(F32)
    ref[start : start + 16, :] = jnp.where(pick, jnp.broadcast_to(row, kept.shape), kept).astype(dtype)


MESH = pl.DeviceIdType.MESH


def whole_step(names, frames, *refs):
    R = SimpleNamespace(**dict(zip(names, refs)))
    clip, head = lax.axis_index("clip"), lax.axis_index("head")
    side, turn = clip % 2, clip // 2 % 2
    width = R.wt_t.shape[2]
    count = R.patches.shape[1]
    at = 4 * count
    peer_c, peer_y, peer_d = (clip, head ^ 1), (clip, head ^ 2), (clip, head ^ 3)
    levels = lax.axis_size("clip").bit_length() - 1
    bits = [(clip ^ (1 << j), head) for j in range(levels)]

    pieces = (
        (R.wt_t, R.wt_t_in, 0), (R.pj_t, R.pj_t_in, 1), (R.wt_s, R.wt_s_in, 0), (R.pj_s, R.pj_s_in, 1),
        (R.w1, R.w1_in, 2), (R.w2, R.w2_in, 2),
    )

    def slot(i, s, half=None):
        ref, _, kind = pieces[i]
        if kind == 2:
            return ref.at[s] if half is None else ref.at[s, pl.ds(half * 384, 384), :]
        start, size = (s * 192, 192) if half is None else (s * 192 + half * 96, 96)
        return ref.at[:, pl.ds(start, size), :] if kind == 0 else ref.at[pl.ds(start, size), :]

    def source(i, half=None):
        _, ref, kind = pieces[i]
        if half is None:
            return ref
        if kind == 0:
            return ref.at[:, pl.ds(half * 96, 96), :]
        size = ref.shape[0] // 2
        return ref.at[pl.ds(half * size, size), :]

    def remote(src, dst, sems, index, peer):
        return pltpu.make_async_remote_copy(
            src_ref=src, dst_ref=dst, send_sem=sems[0].at[index], recv_sem=sems[1].at[index],
            device_id=peer, device_id_type=MESH,
        )

    def y_copy(i):
        return remote(source(i, side), slot(i, 2, side), (R.wy_s, R.wy_r), i, peer_y)

    def x_copy(i):
        return remote(slot(i, 2, side), slot(i, 2, side), (R.wx_s, R.wx_r), i, bits[0])

    def c_copy(i):
        return remote(source(i), slot(i, 1), (R.wc_s, R.wc_r), i, peer_c)

    def f_copy(i, other):
        half = 1 - side if other else side
        sems = (R.wg_s, R.wg_r) if other else (R.wf_s, R.wf_r)
        return remote(slot(i, 2, half), slot(i, 3, half), sems, i, peer_c)

    def own_copy(i):
        return pltpu.make_async_copy(source(i), slot(i, 0), R.wo.at[i])

    def pass_near(i):
        y_copy(i).wait_recv()
        x_copy(i).start()
        f_copy(i, False).start()

    def pass_far(i):
        x_copy(i).wait_recv()
        f_copy(i, True).start()

    def ready_near(i):
        own_copy(i).wait()
        c_copy(i).wait_recv()

    def ready_far(i):
        f_copy(i, False).wait_recv()
        f_copy(i, True).wait_recv()

    def sent(i):
        y_copy(i).wait_send()
        x_copy(i).wait_send()
        c_copy(i).wait_send()
        f_copy(i, False).wait_send()
        f_copy(i, True).wait_send()

    def exchange(k, src, dst):
        mine = pl.ds(2 * head, 2)
        copies = []
        for r, peer in ((2, peer_y), (3, peer_d), (1, peer_c)):
            there = pl.ds(2 * (head ^ r), 2)
            copies.append(remote(src.at[there], dst.at[mine], (R.ex_s, R.ex_r), 3 * k + r - 1, peer))
        copies.append(pltpu.make_async_copy(src.at[mine], dst.at[mine], R.exo.at[k]))
        return copies

    def all_start(copies):
        for copy in copies:
            copy.start()

    def all_wait(copies):
        for copy in copies:
            copy.wait()

    def sum_rows(k, buf, swapped):
        copies = [
            remote(buf.at[0], buf.at[r], (R.row_s, R.row_r), 3 * k + r - 1, peer)
            for r, peer in ((2, peer_y), (3, peer_d), (1, peer_c))
        ]
        all_start(copies)

        def finish():
            all_wait(copies)
            part = [buf[r] for r in range(4)]
            if swapped:
                part = [part[0]] + [blocks_swapped(part[r], r) for r in (1, 2, 3)]
            total = (part[0] + part[1]) + (part[2] + part[3])
            return total[0:1, :]

        return finish

    def unit(i):
        if i < 8:
            ref, n = (R.w1, i) if i < 4 else (R.w2, i - 4)
            return lambda s, start=0, size=192: ref.at[s, pl.ds(n * 192 + start, size), :]
        if i == 12:
            return lambda s, start=0, size=192: R.fc.at[pl.ds((head ^ s) * 192 + start, size), :]
        wt, pj = (R.wt_s, R.pj_s) if i < 12 else (R.wt_t, R.pj_t)
        n = i - 8 if i < 12 else i - 13
        if n == 0:
            return lambda s, start=0, size=192: pj.at[pl.ds(s * 192 + start, size), :]
        return lambda s, start=0, size=192: wt.at[n - 1, pl.ds(s * 192 + start, size), :]

    half = side * 96
    quarter = half + turn * 48

    def add(dst, src, size):
        def body(r, carry):
            rows = pl.ds(pl.multiple_of(r * 48, 48), 48)
            dst[rows, :] = dst[rows, :] + src[rows, :]
            return carry

        lax.fori_loop(0, size // 48, body, 0)

    def core_copies(i):
        u = unit(i)
        return [
            remote(u(1), R.near.at[i % 9, 0], (R.gc_s, R.gc_r), 2 * i, peer_c),
            remote(u(3), R.near.at[i % 9, 1], (R.gc_s, R.gc_r), 2 * i + 1, peer_c),
        ]

    def y_part(i):
        u = unit(i)
        return remote(u(2), u(3) if i == 12 else u(1), (R.gy_s, R.gy_r), i, peer_y)

    def landing(i, j):
        u = unit(i)
        if j == 0:
            return u(3, 0, 96)
        return u(3, 48 + 48 * j, 48) if j < 3 else u(2, 48 * (j - 3), 48)

    def bit_part(i, j):
        u = unit(i)
        if j == 0:
            src = u(0, 96 - half, 96)
        elif j == 1:
            src = u(0, half + 48 - turn * 48, 48)
        else:
            src = u(0, quarter, 48)
        return remote(src, landing(i, j), (R.gb_s, R.gb_r), i * levels + j, bits[j])

    def result(i, start, size):
        if i < 8:
            return (R.dw1 if i < 4 else R.dw2).at[pl.ds(i % 4 * 192 + start, size), :]
        if i == 12:
            return R.dfc.at[pl.ds(head * 192 + start, size), :]
        n = i - 8 if i < 12 else i - 13
        return (R.dsp if i < 12 else R.dti).at[n, pl.ds(start, size), :]

    def back_near(i):
        mine = unit(i)(0, quarter, 48)
        there = result(i, quarter, 48)
        return [
            remote(mine, there, (R.gq_s, R.gq_r), i, bits[1]),
            pltpu.make_async_copy(mine, there, R.go.at[i]),
        ]

    def back_far(i):
        rows = result(i, half, 96)
        return remote(rows, rows, (R.gh_s, R.gh_r), i, bits[0])

    def back_all(i):
        copies = []
        for r, peer in ((2, peer_y), (3, peer_d), (1, peer_c)):
            rows = R.dfc.at[pl.ds(head * 192, 192), :]
            copies.append(remote(rows, rows, (R.gf_s, R.gf_r), r - 1, peer))
        return copies

    def tell(sem, index, peer):
        pl.semaphore_signal(sem.at[index], inc=1, device_id=peer, device_id_type=MESH)

    stage = [0] * 17
    joined = [False] * 17

    def wait_core(i):
        if joined[i]:
            return
        joined[i] = True
        u = unit(i)
        all_wait(core_copies(i))
        tell(R.free_y, i, peer_y)
        for j in range(min(levels, 3)):
            tell(R.free_b, i * levels + j, bits[j])
        add(u(2), R.near.at[i % 9, 1], 192)
        add(u(0), R.near.at[i % 9, 0], 192)

    def advance(i):
        u, k = unit(i), stage[i]
        stage[i] += 1
        if k == 0:
            all_start(core_copies(i))
        elif k == 1:
            wait_core(i)
            pl.semaphore_wait(R.free_y.at[i], 1)
            y_part(i).start()
        elif k == 2:
            y_part(i).wait()
            for j in range(3, levels):
                tell(R.free_b, i * levels + j, bits[j])
            add(u(0), u(1), 192)
        elif k < 3 + levels:
            j = k - 3
            bit_part(i, j).wait()
            if j == 0:
                add(u(0, half, 96), landing(i, j), 96)
            else:
                add(u(0, quarter, 48), landing(i, j), 48)
        elif k == 3 + levels:
            all_wait(back_near(i))
            back_far(i).start()
        elif k == 4 + levels:
            back_far(i).wait()
            if i == 12:
                all_start(back_all(i))
        else:
            all_wait(back_all(i))
        if 2 <= k < 2 + levels:
            pl.semaphore_wait(R.free_b.at[i * levels + k - 2], 1)
            bit_part(i, k - 2).start()
        elif k == 2 + levels:
            all_start(back_near(i))

    last = 5 + levels

    def finish_units(between):
        while min(stage) < last:
            for i in reversed(range(17)):
                if stage[i] < last and (i == 0 or stage[i] < stage[i - 1] or stage[i - 1] >= last):
                    advance(i)
            next(between, None)
        for _ in between:
            pass
        advance(12)

    barrier = pltpu.get_barrier_semaphore()
    for peer in [peer_c, peer_y, peer_d] + bits:
        pl.semaphore_signal(barrier, inc=1, device_id=peer, device_id_type=MESH)
    pl.semaphore_wait(barrier, 3 + levels)

    load = [pltpu.make_async_copy(R.patches, R.patches_v, R.lo.at[0])]
    load.append(pltpu.make_async_copy(R.fc_in, R.fc, R.lo.at[1]))
    load[0].start()
    for i in range(4):
        y_copy(i).start()
    for i in range(4):
        own_copy(i).start()
        c_copy(i).start()
    load[1].start()
    for i in range(4, 6):
        own_copy(i).start()
        c_copy(i).start()

    rows_x, first = R.rows_x, R.rows_s
    qkv_t, p_t, mix_t, att_t, u_t = R.qkv_t, R.p_t, R.mix_t, R.att_t, R.u_t
    load[0].wait()
    to_patch_order(R.patches_v, rows_x, R.perm)
    norm_rows(rows_x, R.gain_t, u_t, T_ROWS, 80)
    ready_near(0)
    ready_near(1)
    project_qkv(u_t, R.wt_t, qkv_t, T_ROWS, 0, width // 2)
    pass_near(0)
    pass_near(1)
    attention(qkv_t, p_t, mix_t, T_GROUPS, time_bias(R.kt_row), 0, 3)
    pass_far(0)
    pass_far(1)
    ready_far(0)
    ready_far(1)
    project_qkv(u_t, R.wt_t, qkv_t, T_ROWS, width // 2, width // 2)
    attention(qkv_t, p_t, mix_t, T_GROUPS, time_bias(R.kt_row), 3, 6)
    pass_near(2)
    pass_near(3)
    load[1].wait()

    def project(n):
        cols = pl.ds(n, 256)
        att_t[:, cols] = nn(mix_t[...], R.pj_t[:, cols]).astype(BF16)

    tiles(width, 256, project)

    def branch(n):
        cols = pl.ds(n, 256)
        first[:T_ROWS, cols] = rows_x[:T_ROWS, cols] + R.kt_col[...] * nn(att_t[...], R.fc[:, cols])

    tiles(width, 256, branch)
    to_frame_order(first, R.send_a, R.perm)
    ex_first = exchange(0, R.send_a, R.got_first)
    all_start(ex_first)
    ex_cot = exchange(1, R.cot, R.got_cot)
    all_start(ex_cot)
    y_copy(4).start()
    pass_far(2)
    pass_far(3)

    qkv_s, p_s, mix_s, u_s = R.qkv_s, R.p_s, R.mix_s, R.u_s
    all_wait(ex_first)
    cls_row = R.cls[...].astype(F32)
    gather_frames(R.got_first, (cls_row, cls_row), rows_x)
    norm_rows(rows_x, R.gain_s, u_s, S_ROWS, 208)
    for i in (2, 3):
        ready_near(i)
        ready_far(i)
    project_qkv(u_s, R.wt_s, qkv_s, S_ROWS, 0, width)
    part = cls_attention(qkv_s, R.ks_row, at, width)
    R.cls_sum[0] = jnp.broadcast_to(part, (8, width))
    cls_total = sum_rows(0, R.cls_sum, True)
    y_copy(5).start()
    pass_near(4)
    attention(qkv_s, p_s, mix_s, S_GROUPS, lambda g, size: space_bias(R.ks_row, g), 0, 6)
    set_row(mix_s, 0, at, cls_total() * (1.0 / frames), BF16)
    set_row(mix_s, SEG, at, jnp.zeros((1, width), F32), BF16)
    pass_far(4)
    pass_near(5)
    second, cot = R.rows_s, R.rows_c

    def project_space(n):
        cols = pl.ds(n, 256)
        second[:, cols] = rows_x[:, cols] + R.ks_col[...] * nn(mix_s[...], R.pj_s[:, cols])

    tiles(width, 256, project_space)

    all_wait(ex_cot)
    gather_frames(R.got_cot, (R.ccot[...], jnp.zeros((1, width), F32)), cot)
    u, uw, dz, dzw = R.low_a, R.low_b, R.low_c, R.low_d
    acc, du = R.rows_a, R.rows_d
    kcol, once = R.ks_col, R.once

    def prepare(r):
        rows = pl.ds(r, 208)
        scaled, _ = stats(second[rows, :])
        low = (scaled * R.gain_m[...]).astype(BF16)
        u[rows, :] = low
        uw[rows, :] = (low.astype(F32) * once[rows, :]).astype(BF16)
        grad = cot[rows, :] * kcol[rows, :]
        dz[rows, :] = grad.astype(BF16)
        dzw[rows, :] = (grad * once[rows, :]).astype(BF16)

    tiles(S_ROWS, 208, prepare)
    acc[...] = jnp.zeros_like(acc)
    du[...] = jnp.zeros_like(du)
    w1_ref, w2_ref = R.w1, R.w2
    per = w1_ref.shape[2] // 256

    def hidden(i, carry):
        s = i // per
        cols = pl.ds(pl.multiple_of((i % per) * 256, 256), 256)
        w1 = w1_ref[s, :, cols]
        w2 = w2_ref[s, cols, :]
        hid = nn(u[...], w1)
        phi = 0.5 + 0.5 * lax.erf(hid * 0.7071067811865476)
        act = (hid * phi).astype(BF16)
        slope = phi + hid * (0.3989422804014327 * jnp.exp(hid * hid * -0.5))
        acc[...] += nn(act, w2)
        dhid = (nt(dz[...], w2) * slope).astype(BF16)
        du[...] += nt(dhid, w1)
        w2_ref[s, cols, :] = tn(act, dzw[...]).astype(BF16)
        w1_ref[s, :, cols] = tn(uw[...], dhid).astype(BF16)
        return carry

    for i in (4, 5):
        ready_near(i)
    for i in (4, 5):
        c_copy(i).wait_send()
    lax.fori_loop(0, 2 * per, hidden, 0)
    pass_far(5)
    for i in (4, 5):
        ready_far(i)
        y_copy(i).wait_send()
        x_copy(i).wait_send()
        f_copy(i, False).wait_send()
        f_copy(i, True).wait_send()
    lax.fori_loop(2 * per, 4 * per, hidden, 0)
    R.dgain_m[...] = jnp.zeros((1, width), F32)

    def finish_mlp(r):
        rows = pl.ds(r, 208)
        x = second[rows, :]
        scaled, factor = stats(x)
        acc[rows, :] = x + kcol[rows, :] * acc[rows, :]
        grad = du[rows, :]
        R.dgain_m[...] += jnp.sum(grad * scaled * once[rows, :], axis=0, keepdims=True)
        cot[rows, :] += norm_back(grad, R.gain_m[...], scaled, factor)

    tiles(S_ROWS, 208, finish_mlp)
    R.ocls[...] = acc[at : at + 1, :].astype(BF16)
    scatter_frames(acc, R.send_b)
    ex_out = exchange(2, R.send_b, R.out)
    all_start(ex_out)

    for i in range(8):
        advance(i)

    dsecond = cot
    low, loww, dmix, dqkv = R.low_a, R.low_b, R.low_c, R.dqkv
    low[...] = (dsecond[...] * kcol[...]).astype(BF16)
    loww[...] = (dsecond[...] * (kcol[...] * once[...])).astype(BF16)
    dcls_second = dsecond[at : at + 1, :]
    set_row(low, SEG, at, dcls_second, BF16)
    for i in (2, 3):
        sent(i)

    def back_space(n):
        cols = pl.ds(n, 256)
        dmix[:, cols] = nt(low[...], R.pj_s[cols, :]).astype(BF16)
        R.pj_s[cols, :] = tn(mix_s[:, cols], loww[...]).astype(BF16)

    tiles(width, 256, back_space)
    advance(0)
    advance(1)
    dcls_mix = dmix[SEG - 16 : SEG, :].astype(F32)[at - SEG + 16 : at - SEG + 17, :] * (1.0 / frames)
    set_row(dmix, 0, at, dcls_mix, BF16)
    set_row(dmix, SEG, at, dcls_mix, BF16)
    attention_back(qkv_s, p_s, dmix, dqkv, S_GROUPS)
    advance(2)
    advance(3)
    advance(0)
    qkv_back(dqkv, u_s, R.wt_s, du, S_ROWS)
    R.dcls_sum[0] = jnp.broadcast_to(du[at : at + 1, :] + du[SEG + at : SEG + at + 1, :], (8, width))
    R.dgain_s[...] = jnp.zeros((1, width), F32)
    dfirst = R.rows_a

    def finish_space(r):
        rows = pl.ds(r, 208)
        scaled, factor = stats(rows_x[rows, :])
        grad = du[rows, :]
        R.dgain_s[...] += jnp.sum(grad * scaled, axis=0, keepdims=True)
        dfirst[rows, :] = dsecond[rows, :] + norm_back(grad, R.gain_s[...], scaled, factor)

    tiles(S_ROWS, 208, finish_space)
    scatter_frames(dfirst, R.send_a)
    for i in range(4, 8):
        wait_core(i)
    ex_df = exchange(3, R.send_a, R.got_first)
    all_start(ex_df)
    dcls_total = sum_rows(1, R.dcls_sum, False)
    for i in range(4, 8):
        advance(i)
    advance(1)
    advance(0)

    df = R.rows_s
    to_patch_order(R.patches_v, rows_x, R.perm)
    all_wait(ex_df)
    for i in range(8, 12):
        advance(i)
    to_patch_order(R.got_first, df, R.perm)
    scaled, factor = stats(cls_row)
    R.dcls[...] = dcls_second + norm_back(dcls_total(), R.gain_s[...], scaled, factor)
    low, datt, dmix = R.low_a, R.low_b, R.low_c
    low[:T_ROWS, :] = (df[:T_ROWS, :] * R.kt_col[...]).astype(BF16)
    for i in (0, 1):
        sent(i)

    def back_fc(n):
        cols = pl.ds(n, 256)
        datt[:T_ROWS, cols] = nt(low[:T_ROWS, :], R.fc[cols, :]).astype(BF16)
        R.fc[cols, :] = tn(att_t[:, cols], low[:T_ROWS, :]).astype(BF16)

    tiles(width, 256, back_fc)
    advance(12)
    advance(8)

    def back_time(n):
        cols = pl.ds(n, 256)
        dmix[:T_ROWS, cols] = nt(datt[:T_ROWS, :], R.pj_t[cols, :]).astype(BF16)
        R.pj_t[cols, :] = tn(mix_t[:, cols], datt[:T_ROWS, :]).astype(BF16)

    tiles(width, 256, back_time)
    advance(13)
    advance(2)
    advance(1)
    advance(0)
    attention_back(qkv_t, p_t, dmix, dqkv, T_GROUPS)
    advance(9)
    advance(3)
    advance(2)
    advance(1)
    advance(0)
    qkv_back(dqkv, u_t, R.wt_t, du, T_ROWS)
    for i in (14, 15, 16):
        advance(i)
    advance(4)
    advance(3)
    advance(2)
    advance(1)
    advance(0)
    R.dgain_t[...] = jnp.zeros((1, width), F32)

    def finish_time(r):
        rows = pl.ds(r, 80)
        scaled, factor = stats(rows_x[rows, :])
        grad = du[rows, :]
        R.dgain_t[...] += jnp.sum(grad * scaled, axis=0, keepdims=True)
        df[rows, :] += norm_back(grad, R.gain_t[...], scaled, factor)

    tiles(T_ROWS, 80, finish_time)
    to_frame_order(df, R.dx_v, R.perm)
    store = pltpu.make_async_copy(R.dx_v, R.dx, R.lo.at[2])
    store.start()
    for n, gain in enumerate((R.dgain_t, R.dgain_s, R.dgain_m)):
        R.gains[0, n : n + 1, :] = gain[...]

    def gain_part(j):
        peer = ([peer_c, peer_y] + bits)[j]
        return remote(R.gains.at[0], R.gains.at[1 + j], (R.gg_s, R.gg_r), j, peer)

    def gain_steps():
        for j in range(2 + levels):
            gain_part(j).start()
            yield
            gain_part(j).wait()
            R.gains[0] = R.gains[0] + R.gains[1 + j]

    finish_units(gain_steps())
    R.gains_out[...] = R.gains[0]
    all_wait(ex_out)
    store.wait()


def local(
    patches, cls_token, keep_mask, gain_time, qkv_time, proj_time, temporal_fc, gain_space, qkv_space, proj_space,
    gain_mlp, mlp_in, mlp_out, cotangent, cls_cotangent,
):
    _, frames, count, width = patches.shape
    members = lax.axis_size("head")
    me = lax.axis_index("head")
    heads_here, hd = qkv_time.shape[1], qkv_time.shape[3]
    part = heads_here * hd
    at = members * count

    def flat_t(w):
        return jnp.transpose(w, (2, 1, 3, 0)).reshape(3, part, width)

    keep = keep_mask[0].astype(F32)
    here = lax.dynamic_slice_in_dim(keep, me * count, count, axis=1)
    kt = jnp.pad(here.T.reshape(-1), (0, T_ROWS - frames * count))
    kt_col = kt[:, None]
    kt_row = jnp.stack([jnp.pad(kt[s : s + n], (0, 128 - n)) for s, n in T_GROUPS])[:, None, :]
    mine = lax.dynamic_slice_in_dim(keep, me * 2, 2, axis=0)
    ks_row = jnp.pad(mine, ((0, 0), (0, 256 - at))).at[:, at].set(1.0)[:, None, :]
    first_only = jnp.array([1.0, 0.0], F32)[:, None]
    ks_col = jnp.concatenate([mine, first_only, jnp.zeros((2, SEG - 1 - at), F32)], axis=1).reshape(-1, 1)
    row_id = jnp.arange(S_ROWS)
    once = jnp.where((row_id == at) & (me != 0), 0.0, 1.0).astype(F32)[:, None]

    small = dict(
        cls=cls_token, ccot=cls_cotangent.astype(F32), gain_t=gain_time[None], gain_s=gain_space[None],
        gain_m=gain_mlp[None], kt_row=kt_row, kt_col=kt_col, ks_row=ks_row, ks_col=ks_col, once=once,
    )
    large = dict(
        patches=patches[0], cot=cotangent[0], wt_t_in=flat_t(qkv_time), pj_t_in=proj_time.reshape(-1, width),
        fc_in=temporal_fc, wt_s_in=flat_t(qkv_space), pj_s_in=proj_space.reshape(-1, width), w1_in=mlp_in, w2_in=mlp_out,
    )
    frame_rows, square, row = (frames, count, width), (width, width), (1, width)
    t_rows, s_rows = (T_ROWS, width), (S_ROWS, width)
    in_hbm = dict(
        out=(frame_rows, BF16), dx=(frame_rows, F32), dw1=(square, BF16), dw2=(square, BF16), dfc=(square, BF16),
        dsp=((4, part, width), BF16), dti=((4, part, width), BF16),
    )
    in_vmem = dict(ocls=(row, BF16), dcls=(row, F32), gains_out=((8, width), F32))
    levels = lax.axis_size("clip").bit_length() - 1
    vmem = dict(
        wt_t=((3, width, width), BF16), pj_t=(square, BF16), fc=(square, BF16), wt_s=((3, width, width), BF16),
        pj_s=(square, BF16), w1=((4, width, width), BF16), w2=((4, width, width), BF16),
        patches_v=(frame_rows, BF16), u_t=(t_rows, BF16), qkv_t=((T_ROWS, 3 * width), BF16),
        p_t=((6, 4, 224, 128), F32), mix_t=(t_rows, BF16), att_t=(t_rows, BF16),
        rows_x=(s_rows, F32), rows_s=(s_rows, F32), rows_c=(s_rows, F32), rows_a=(s_rows, F32), rows_d=(s_rows, F32),
        low_a=(s_rows, BF16), low_b=(s_rows, BF16), low_c=(s_rows, BF16), low_d=(s_rows, BF16),
        u_s=(s_rows, BF16), qkv_s=((S_ROWS, 3 * width), BF16), mix_s=(s_rows, BF16),
        p_s=((6, 2, 416, 256), F32), dqkv=((S_ROWS, 3 * width), BF16),
        perm=((width // 128, T_ROWS, 128), F32), dx_v=(frame_rows, F32), send_a=(frame_rows, BF16),
        send_b=(frame_rows, BF16), got_first=(frame_rows, BF16), got_cot=(frame_rows, BF16),
        cls_sum=((4, 8, width), F32), dcls_sum=((4, 8, width), F32),
        dgain_t=(row, F32), dgain_s=(row, F32), dgain_m=(row, F32), gains=((3 + levels, 8, width), F32),
        near=((9, 2, part, width), BF16),
    )
    pairs = dict(wy=6, wx=6, wc=6, wf=6, wg=6, ex=12, row=6, gc=34, gy=17, gb=17 * levels, gq=17, gh=17, gf=3, gg=2 + levels)
    sems = dict(wo=6, exo=4, lo=3, go=17)
    for name, n in pairs.items():
        sems[name + "_s"] = n
        sems[name + "_r"] = n
    flags = dict(free_y=17, free_b=17 * levels)
    names = [*large, *small, *in_hbm, *in_vmem, *vmem, *sems, *flags]
    hbm, vm = pl.BlockSpec(memory_space=pl.ANY), pl.BlockSpec(memory_space=pltpu.VMEM)
    output, dx, d_w1, d_w2, d_fc, d_sp, d_ti, out_cls, cls_grad, gains = pl.pallas_call(
        partial(whole_step, names, frames),
        out_shape=[jax.ShapeDtypeStruct(s, d) for s, d in [*in_hbm.values(), *in_vmem.values()]],
        in_specs=[hbm] * len(large) + [vm] * len(small),
        out_specs=[hbm] * len(in_hbm) + [vm] * len(in_vmem),
        scratch_shapes=[pltpu.VMEM(s, d) for s, d in vmem.values()]
        + [pltpu.SemaphoreType.DMA((n,)) for n in sems.values()]
        + [pltpu.SemaphoreType.REGULAR((n,)) for n in flags.values()],
        compiler_params=pltpu.CompilerParams(collective_id=0, has_side_effects=True, vmem_limit_bytes=60 << 20),
    )(*large.values(), *small.values())

    def untie(own):
        return jnp.transpose(own.astype(F32).reshape(3, heads_here, hd, width), (3, 1, 0, 2))

    return (
        output[None], out_cls, dx[None], cls_grad, gains[0], untie(d_ti[1:]), d_ti[0].astype(F32).reshape(proj_time.shape),
        d_fc.astype(F32), gains[1], untie(d_sp[1:]), d_sp[0].astype(F32).reshape(proj_space.shape), gains[2],
        d_w1.astype(F32), d_w2.astype(F32),
    )


def solution(mesh):
    rows, wide, by_head = P("clip", None, "head", None), P("clip", None), P(None, "head", None, None)
    in_specs = (
        rows, wide, P("clip", None, None), P(), by_head, P("head", None, None), P(), P(), by_head,
        P("head", None, None), P(), P(None, "head"), P("head", None), rows, wide,
    )
    out_specs = (
        rows, wide, rows, wide, P(), by_head, P("head", None, None), P(), P(), by_head,
        P("head", None, None), P(), P(None, "head"), P("head", None),
    )
    return jax.shard_map(local, mesh=mesh, in_specs=in_specs, out_specs=out_specs, check_vma=False)
```

```python
from functools import partial
from types import SimpleNamespace

import jax
import jax.numpy as jnp
from jax import lax
from jax.experimental import pallas as pl
from jax.experimental.pallas import tpu as pltpu
from jax.sharding import PartitionSpec as P

EPSILON = 1e-06
NEGATIVE = -1e30
F32 = jnp.float32
BF16 = jnp.bfloat16


def nn(a, b):
    return lax.dot_general(a, b, (((1,), (0,)), ((), ())), preferred_element_type=F32)


def nt(a, b):
    return lax.dot_general(a, b, (((1,), (1,)), ((), ())), preferred_element_type=F32)


def tn(a, b):
    return lax.dot_general(a, b, (((0,), (0,)), ((), ())), preferred_element_type=F32)


def tiles(total, size, body):
    def step(i, carry):
        body(pl.multiple_of(i * size, size))
        return carry

    lax.fori_loop(0, total // size, step, 0)


def stats(x):
    center = x - jnp.mean(x, axis=-1, keepdims=True)
    factor = lax.rsqrt(jnp.mean(center * center, axis=-1, keepdims=True) + EPSILON)
    return center * factor, factor


def norm_back(grad, gain, scaled, factor):
    weighted = grad * gain
    inner = weighted - jnp.mean(weighted, axis=-1, keepdims=True)
    return factor * (inner - scaled * jnp.mean(weighted * scaled, axis=-1, keepdims=True))


def pair_masks():
    lane = lax.broadcasted_iota(jnp.int32, (1, 128), 1)
    return (lane < 64).astype(F32).astype(BF16), (lane >= 64).astype(F32).astype(BF16)


def stacked(x):
    low, high = pair_masks()
    return jnp.concatenate([x * low, x * high], axis=0)


def unstacked(x):
    rows = x.shape[0] // 2
    lane = lax.broadcasted_iota(jnp.int32, (1, 128), 1)
    return jnp.where(lane < 64, x[:rows], x[rows:])


def norm_rows(x_ref, gain_ref, u_ref, total, chunk):
    def body(r):
        rows = pl.ds(r, chunk)
        scaled, _ = stats(x_ref[rows, :])
        u_ref[rows, :] = (scaled * gain_ref[...]).astype(BF16)

    tiles(total, chunk, body)


def project_qkv(u_ref, wt_ref, qkv_ref, rows, first, last):
    width = u_ref.shape[1]
    size = (last - first) * 64

    def body(t, carry):
        scale = jnp.where(t == 0, 0.125, 1.0)
        out = nt(u_ref[:rows, :], wt_ref[t, first:last].reshape(size, width)) * scale
        qkv_ref[:rows, pl.ds(pl.multiple_of(t * width + first * 64, 128), size)] = out.astype(BF16)
        return carry

    lax.fori_loop(0, 3, body, 0)


def columns(ref, cols):
    part = ref[:, :, cols]
    return part.reshape(part.shape[0] * part.shape[1], part.shape[2])


def rows_of(ref, n):
    part = ref[pl.ds(n // 64, 4)]
    return part.reshape(256, part.shape[2])


def qkv_back(dqkv_ref, wt_ref, du_ref, rows):
    width = du_ref.shape[1]

    def back(n):
        cols = pl.ds(n, 256)
        total = nn(dqkv_ref[:rows, :width], columns(wt_ref.at[0], cols))
        total += nn(dqkv_ref[:rows, width : 2 * width], columns(wt_ref.at[1], cols))
        total += nn(dqkv_ref[:rows, 2 * width :], columns(wt_ref.at[2], cols))
        du_ref[:rows, cols] = total

    tiles(width, 256, back)


def qkv_grad(dqkv_ref, u_ref, wt_ref, rows):
    width = u_ref.shape[1]

    def grad(i, carry):
        cols = pl.ds(pl.multiple_of(i * 256, 256), 256)
        out = tn(dqkv_ref[:rows, cols], u_ref[:rows, :]).astype(BF16)
        wt_ref[i // 3, pl.ds((i % 3) * 4, 4)] = out.reshape(4, 64, width)
        return carry

    lax.fori_loop(0, 9, grad, 0)


def softmax(scores):
    highest = jnp.max(scores, axis=-1, keepdims=True)
    weights = jnp.exp(scores - highest)
    return weights * (1.0 / jnp.sum(weights, axis=-1, keepdims=True))


def attention(qkv_ref, p_ref, mix_ref, groups, bias_of, first, last):
    width = mix_ref.shape[1]

    def body(hp, carry):
        qc = pl.ds(pl.multiple_of(hp * 128, 128), 128)
        kc = pl.ds(pl.multiple_of(width + hp * 128, 128), 128)
        vc = pl.ds(pl.multiple_of(2 * width + hp * 128, 128), 128)
        for g, (start, size) in enumerate(groups):
            rows = pl.ds(start, size)
            prob = softmax(nt(stacked(qkv_ref[rows, qc]), qkv_ref[rows, kc]) + bias_of(g, size))
            p_ref[hp, g, : 2 * size, :size] = prob
            mix_ref[rows, qc] = unstacked(nn(prob.astype(BF16), qkv_ref[rows, vc])).astype(BF16)
        return carry

    lax.fori_loop(first, last, body, 0)


def attention_back(qkv_ref, p_ref, dmix_ref, dqkv_ref, groups, first, last):
    width = dmix_ref.shape[1]

    def body(hp, carry):
        qc = pl.ds(pl.multiple_of(hp * 128, 128), 128)
        kc = pl.ds(pl.multiple_of(width + hp * 128, 128), 128)
        vc = pl.ds(pl.multiple_of(2 * width + hp * 128, 128), 128)
        for g, (start, size) in enumerate(groups):
            rows = pl.ds(start, size)
            up = stacked(dmix_ref[rows, qc])
            prob = p_ref[hp, g, : 2 * size, :size]
            dprob = nt(up, qkv_ref[rows, vc])
            delta = jnp.sum(prob * dprob, axis=-1, keepdims=True)
            dscore = (prob * (dprob - delta)).astype(BF16)
            dqkv_ref[rows, qc] = (unstacked(nn(dscore, qkv_ref[rows, kc])) * 0.125).astype(BF16)
            dqkv_ref[rows, kc] = tn(dscore, stacked(qkv_ref[rows, qc])).astype(BF16)
            dqkv_ref[rows, vc] = tn(prob.astype(BF16), up).astype(BF16)
        return carry

    lax.fori_loop(first, last, body, 0)


T_ROWS = 400
T_GROUPS = ((0, 96), (96, 96), (192, 96), (288, 112))
SEG = 208
S_ROWS = 416
S_GROUPS = ((0, 208), (208, 208))


def time_bias(kcol, size):
    row = lax.broadcasted_iota(jnp.int32, (size, size), 0)
    col = lax.broadcasted_iota(jnp.int32, (size, size), 1)
    kept = jnp.sum(jnp.where(row == col, kcol, 0.0), axis=0, keepdims=True)
    ok = ((row // 8) == (col // 8)) & ((kept > 0.0) | (row == col))
    return jnp.where(ok, 0.0, NEGATIVE)


def patch_keep(keep_ref, head, count, frames):
    total = keep_ref.shape[1]
    row = lax.broadcasted_iota(jnp.int32, (T_ROWS, total), 0)
    col = lax.broadcasted_iota(jnp.int32, (T_ROWS, total), 1)
    pick = ((row // frames + head * count == col) & (row < frames * count)).astype(F32).astype(BF16)
    by_frame = nt(pick, keep_ref[...].astype(F32).astype(BF16))
    row = lax.broadcasted_iota(jnp.int32, (T_ROWS, frames), 0)
    col = lax.broadcasted_iota(jnp.int32, (T_ROWS, frames), 1)
    return jnp.sum(jnp.where(row % frames == col, by_frame, 0.0), axis=1, keepdims=True)


def space_bias(krow_ref, g):
    return (krow_ref[g, :, :SEG] - 1.0) * (-NEGATIVE)


def to_patch_order(src_ref, dst_ref, perm_ref):
    frames, count, width = src_ref.shape
    used = frames * count
    for j in range(width // 128):
        for f in range(frames):
            perm_ref[j, pl.ds(f, count, stride=frames), :] = src_ref[f, :, j * 128 : (j + 1) * 128].astype(F32)
        dst_ref[:used, j * 128 : (j + 1) * 128] = perm_ref[j, :used, :]
    dst_ref[used:T_ROWS, :] = jnp.zeros((T_ROWS - used, width), F32)


def to_frame_order(src_ref, dst_ref, perm_ref):
    frames, count, width = dst_ref.shape
    for j in range(width // 128):
        used = frames * count
        perm_ref[j, :used, :] = src_ref[:used, j * 128 : (j + 1) * 128].astype(F32)
        for f in range(frames):
            out = perm_ref[j, pl.ds(f, count, stride=frames), :]
            dst_ref[f, :, j * 128 : (j + 1) * 128] = out.astype(dst_ref.dtype)


def gather_frames(got_ref, cls_row, out_ref):
    sources, count = got_ref.shape[0] // 2, got_ref.shape[1]
    for f in range(2):
        base = f * SEG
        for s in range(sources):
            out_ref[base + s * count : base + (s + 1) * count, :] = got_ref[2 * s + f].astype(F32)
        at = base + sources * count
        out_ref[at : at + 1, :] = cls_row[f]
        out_ref[at + 1 : base + SEG, :] = jnp.zeros((SEG - 1 - sources * count, out_ref.shape[1]), F32)


def scatter_frames(x_ref, send_ref):
    sources, count = send_ref.shape[0] // 2, send_ref.shape[1]
    for f in range(2):
        for s in range(sources):
            at = f * SEG + s * count
            send_ref[2 * s + f] = x_ref[at : at + count, :].astype(send_ref.dtype)


def cls_attention(qkv_ref, krow_ref, at, width):
    lane = lax.broadcasted_iota(jnp.int32, (16, width), 1) // 64
    own = (lane == lax.broadcasted_iota(jnp.int32, (16, width), 0)).astype(F32)
    total = jnp.zeros((1, width), F32)
    for f in range(2):
        q = qkv_ref[f * SEG + at : f * SEG + at + 1, :width].astype(F32)
        k = qkv_ref[f * SEG : (f + 1) * SEG, width : 2 * width]
        v = qkv_ref[f * SEG : (f + 1) * SEG, 2 * width :]
        prob = softmax(nt((own * q).astype(BF16), k) + space_bias(krow_ref, f))
        total += jnp.sum(own * nn(prob.astype(BF16), v), axis=0, keepdims=True)
    return total


def blocks_swapped(x, distance):
    width = x.shape[1]
    quarter = width // 4
    order = [i ^ distance for i in range(4)]
    return jnp.concatenate([x[:, i * quarter : (i + 1) * quarter] for i in order], axis=1)


def set_row(ref, base, at, row, dtype):
    start = base + at // 16 * 16
    pick = lax.broadcasted_iota(jnp.int32, (16, 1), 0) == at % 16
    kept = ref[start : start + 16, :].astype(F32)
    ref[start : start + 16, :] = jnp.where(pick, jnp.broadcast_to(row, kept.shape), kept).astype(dtype)


MESH = pl.DeviceIdType.MESH

ROUTES = (0, 2, 0, 1, 0, 0, 1, 2, 0, 0, 0, 0, 0, 0, 0)
ORDER = (
    (0, 1),
    (2, 3, 0, 1),
    (4, 5, 2, 3),
    (0, 1, 4),
    (),
    (),
    (),
    (2, 3),
    (0, 1),
    (4, 2),
    (0, 5),
    (6, 8, 9, 7, 0, 1, 2, 3, 4),
    (10, 6, 8, 15),
    (11, 0, 1, 9, 7, 10),
    (2, 3, 4, 5, 11),
    (1, 6),
    (0,),
    (2, 5, 8, 7),
    (12, 13, 14, 3),
    (12, 13, 14, 9, 16, 8, 4, 1, 2, 10, 5, 9, 16, 3, 11, 15, 7, 10, 8, 4, 6, 16, 3, 9, 5, 10, 11, 12, 6, 16,
     8, 4, 9, 5, 13, 12, 11, 16, 10, 8, 6, 5, 14, 9, 7, 16, 12, 13, 10, 11, 8, 6, 14, 16, 12, 13, 11, 9, 14,
     7, 12, 16, 10, 13, 6, 14, 11, 7, 13, 16, 10, 14, 12, 10, 7, 13, 14, 16),
)


def whole_step(names, frames, *refs):
    R = SimpleNamespace(**dict(zip(names, refs)))
    clip, head = lax.axis_index("clip"), lax.axis_index("head")
    digit = (clip % 2, clip // 2 % 2, clip // 4 % 2)
    side, turn = digit[0], digit[1]
    width = R.wt_t.shape[3]
    count = R.patches.shape[0] // frames
    at = 4 * count
    peer_c, peer_y, peer_d = (clip, head ^ 1), (clip, head ^ 2), (clip, head ^ 3)
    levels = lax.axis_size("clip").bit_length() - 1
    bits = [(clip ^ (1 << j), head) for j in range(levels)]

    def part(ref, q, n):
        return ref.at[:, pl.ds(q * 16, n * 16), :]

    def hidden_tile(w1, w2, i, q, n):
        t = (i - 8) // 2
        if i % 2:
            return w1.at[:, pl.ds(q * 16, n * 16), pl.ds(t * 256, 256)]
        return part(w2.at[pl.ds(t * 4, 4)], q, n)

    def slot(i, s, q=0, n=4):
        if i >= 8:
            return hidden_tile(R.w1.at[s], R.w2.at[s], i, q, n)
        wt, pj = (R.wt_t, R.pj_t) if i < 4 else (R.wt_s, R.pj_s)
        if i % 4 == 3:
            return part(pj.at[pl.ds(s * 3, 3)], q, n)
        return part(wt.at[:, s * 3 + i % 4], q, n)

    def source(i, q=0, n=4):
        if i >= 8:
            return hidden_tile(R.w1_in, R.w2_in, i, q, n)
        wt, pj = (R.wt_t_in, R.pj_t_in) if i < 4 else (R.wt_s_in, R.pj_s_in)
        return part(pj if i % 4 == 3 else wt.at[i % 4], q, n)

    def remote(src, dst, sems, index, peer):
        return pltpu.make_async_remote_copy(
            src_ref=src, dst_ref=dst, send_sem=sems[0].at[index], recv_sem=sems[1].at[index],
            device_id=peer, device_id_type=MESH,
        )

    mine = side + 2 * turn

    def y_copy(i):
        return remote(source(i, mine, 1), slot(i, 2, mine, 1), (R.wy_s, R.wy_r), i, peer_y)

    def clip_copies(i):
        quarter = slot(i, 2, mine, 1)
        near = (bits[0], bits[1], (clip ^ 3, head))
        return [remote(quarter, quarter, (R.wx_s, R.wx_r), 3 * i + n, peer) for n, peer in enumerate(near)]

    def c_copy(i):
        return remote(source(i), slot(i, 1), (R.wc_s, R.wc_r), i, peer_c)

    def f_copy(i):
        return remote(slot(i, 2), slot(i, 3), (R.wf_s, R.wf_r), i, peer_c)

    def own_copy(i):
        return pltpu.make_async_copy(source(i), slot(i, 0), R.wo.at[i])

    def pass_near(*pieces):
        for i in pieces:
            y_copy(i).wait_recv()
            for copy in clip_copies(i):
                copy.start()

    def pass_far(*pieces):
        for i in pieces:
            for copy in clip_copies(i):
                copy.wait_recv()
            f_copy(i).start()

    def ready_near(*pieces):
        for i in pieces:
            own_copy(i).wait()
            c_copy(i).wait_recv()

    def ready_far(*pieces):
        for i in pieces:
            f_copy(i).wait_recv()

    def sent(*pieces):
        for i in pieces:
            y_copy(i).wait_send()
            c_copy(i).wait_send()
            f_copy(i).wait_send()
            for copy in clip_copies(i):
                copy.wait_send()

    def exchange(k, src, dst):
        here = pl.ds(2 * head, 2)
        copies = []
        for r, peer in ((2, peer_y), (3, peer_d), (1, peer_c)):
            there = pl.ds(2 * (head ^ r), 2)
            copies.append(remote(src.at[there], dst.at[here], (R.ex_s, R.ex_r), 3 * k + r - 1, peer))
        copies.append(pltpu.make_async_copy(src.at[here], dst.at[here], R.exo.at[k]))
        return copies

    def all_start(copies):
        for copy in copies:
            copy.start()

    def all_wait(copies):
        for copy in copies:
            copy.wait()

    def sum_rows(k, buf, swapped):
        copies = [
            remote(buf.at[0], buf.at[r], (R.row_s, R.row_r), 3 * k + r - 1, peer)
            for r, peer in ((2, peer_y), (3, peer_d), (1, peer_c))
        ]
        all_start(copies)

        def finish():
            all_wait(copies)
            terms = [buf[r] for r in range(4)]
            if swapped:
                terms = [terms[0]] + [blocks_swapped(terms[r], r) for r in (1, 2, 3)]
            total = (terms[0] + terms[1]) + (terms[2] + terms[3])
            return total[0:1, :]

        return finish

    def unit(i):
        if i < 6:
            n = i // 2
            if i % 2:
                return lambda s, q=0, k=4: R.w1.at[s, :, pl.ds(q * 16, k * 16), pl.ds(n * 256, 256)]
            return lambda s, q=0, k=4: part(R.w2.at[s, pl.ds(n * 4, 4)], q, k)
        if i == 10:
            return lambda s, q=0, k=4: part(R.fc.at[pl.ds((head ^ s) * 3, 3)], q, k)
        wt, pj = (R.wt_s, R.pj_s) if i < 10 else (R.wt_t, R.pj_t)
        n = i - 6 if i < 10 else i - 11
        if n == 0:
            return lambda s, q=0, k=4: part(pj.at[pl.ds(s * 3, 3)], q, k)
        return lambda s, q=0, k=4: part(wt.at[:, s * 3 + n - 1], q, k)

    def result(i, q, k):
        if i < 6:
            n = i // 2
            if i % 2:
                return R.dw1.at[:, pl.ds(q * 16, k * 16), pl.ds(n * 256, 256)]
            return part(R.dw2.at[pl.ds(n * 4, 4)], q, k)
        if i == 10:
            return part(R.dfc.at[pl.ds(head * 3, 3)], q, k)
        wt, pj = (R.dwt_s, R.dpj_s) if i < 10 else (R.dwt_t, R.dpj_t)
        n = i - 6 if i < 10 else i - 11
        return part(pj if n == 0 else wt.at[n - 1], q, k)

    def near_slot(i, k):
        if i < 6:
            return (R.near_c if i % 2 else R.near_b).at[i // 2, k]
        if i < 9:
            return R.near_b.at[i - 6, k, pl.ds(0, 3)]
        return R.near_a.at[i - 9, k]

    def add(dst, src):
        def body(r, carry):
            dst[r] = dst[r] + src[r]
            return carry

        lax.fori_loop(0, dst.shape[0], body, 0)

    def steps_of(i):
        u, route = unit(i), ROUTES[i]
        a, b = (1, 2) if route == 2 else (0, 1)
        half = 2 * digit[a]
        quarter = half + digit[b]
        counts = [0, 0]

        def copy(src, dst, peer):
            counts[0] += 1
            return remote(src, dst, (R.gu_s, R.gu_r), i * 16 + counts[0] - 1, peer)

        def land(k):
            at_q = counts[1]
            counts[1] += k
            s, q = ((1, at_q) if at_q < 4 else (3, at_q - 4) if at_q < 8 else (2, at_q - 8))
            return u(s, q, k), (s, q, k)

        steps = [([copy(u(1), near_slot(i, 0), peer_c), copy(u(3), near_slot(i, 1), peer_c)],
                  [(u(2), near_slot(i, 1)), (u(0), near_slot(i, 0))], None)]
        peers = []
        kept, joined = (0, 4), False
        whole_bits = [j for j in range(levels) if j not in (a, b)]
        order = ((-1, a, b), (a, -1, b), (a, b, -1))[route]
        for bit in list(order) + whole_bits:
            copies, sums = [], []
            if bit == -1:
                spot, (s, q, k) = land(kept[1])
                copies.append(copy(u(2, *kept), u(s ^ 2, q, k) if i == 10 else spot, peer_y))
                sums.append((u(0, *kept), spot))
                joined = True
                peers.append(peer_y)
            else:
                if bit == a:
                    kept, other = (half, 2), (2 - half, 2)
                elif bit == b:
                    kept, other = (quarter, 1), (half + 1 - digit[b], 1)
                else:
                    other = kept
                for s in (0,) if joined else (0, 2):
                    spot, _ = land(other[1])
                    copies.append(copy(u(s, *other), spot, bits[bit]))
                    sums.append((u(s, *kept), spot))
                peers.append(bits[bit])
            steps.append((copies, sums, len(peers) - 1))
        mine_q, there_q, rows = u(0, quarter, 1), result(i, quarter, 1), result(i, half, 2)
        steps.append(([copy(mine_q, there_q, bits[b]), pltpu.make_async_copy(mine_q, there_q, R.go.at[i])], [], None))
        steps.append(([copy(rows, rows, bits[a])], [], None))
        if i == 10:
            ours, far = R.dfc.at[pl.ds(head * 3, 3)], R.dfc.at[pl.ds((head ^ 2) * 3, 3)]
            steps.append(([copy(ours, ours, peer_y), copy(ours, ours, peer_c)], [], None))
            steps.append(([copy(far, far, peer_c)], [], None))
        return steps, peers

    units = [None] * 15
    stage = [0] * 15

    def tell(i, first, last):
        peers = units[i][1]
        for k in range(first, min(last, len(peers))):
            pl.semaphore_signal(R.free.at[i * 8 + k], inc=1, device_id=peers[k], device_id_type=MESH)

    def land_step(i):
        steps, _ = units[i]
        copies, sums, _ = steps[stage[i] - 1]
        all_wait(copies)
        if stage[i] == 1:
            tell(i, 0, 4)
        for dst, src in sums:
            add(dst, src)
        if stage[i] == 4:
            tell(i, 4, 8)

    landed = [0] * 15

    def advance(i):
        if units[i] is None:
            units[i] = steps_of(i)
        steps, _ = units[i]
        if stage[i] > landed[i]:
            land_step(i)
            landed[i] = stage[i]
        if stage[i] < len(steps):
            copies, _, credit = steps[stage[i]]
            if credit is not None:
                pl.semaphore_wait(R.free.at[i * 8 + credit], 1)
            all_start(copies)
        stage[i] += 1

    def join_core(i):
        if stage[i] == 1 and landed[i] == 0:
            land_step(i)
            landed[i] = 1

    extra = {}

    def service(k):
        for i in ORDER[k]:
            if i < 15:
                advance(i)
            else:
                next(extra[i], None)

    def finish_units():
        while any(stage[i] < 1 + len(units[i][0]) for i in range(15)):
            for i in reversed(range(15)):
                done = [stage[j] >= 1 + len(units[j][0]) for j in (i, i - 1)]
                if not done[0] and (i == 0 or done[1] or stage[i] < stage[i - 1]):
                    advance(i)
        for steps in extra.values():
            for _ in steps:
                pass

    barrier = pltpu.get_barrier_semaphore()
    for peer in [peer_c, peer_y, peer_d, (clip ^ 3, head)] + bits:
        pl.semaphore_signal(barrier, inc=1, device_id=peer, device_id_type=MESH)
    pl.semaphore_wait(barrier, 4 + levels)

    loads = (
        (R.patches, R.patches_v.at[pl.ds(0, frames * count)]), (R.keep, R.keep_v), (R.cot, R.low_d.at[pl.ds(0, frames * count)]), (R.fc_in, R.fc),
    )
    loads = [pltpu.make_async_copy(src, dst, R.lo.at[i]) for i, (src, dst) in enumerate(loads)]
    for i in range(3):
        loads[i].start()
    for i in range(14):
        y_copy(i).start()
    for i in range(14):
        own_copy(i).start()
        c_copy(i).start()
    loads[3].start()

    rows_x, first = R.rows_x, R.rows_s
    qkv_t, p_t, mix_t, att_t, u_t = R.qkv_t, R.p_t, R.mix_t, R.att_t, R.u_t
    patches, gains = R.patches_v, R.rows_in
    gain_t, gain_s, gain_m = gains.at[0:1], gains.at[1:2], gains.at[2:3]
    used = frames * count
    loads[0].wait()
    patches[used:, :] = jnp.zeros((T_ROWS - used, width), BF16)

    def norm_time(r):
        rows = pl.ds(r, 80)
        scaled, _ = stats(patches[rows, :].astype(F32))
        u_t[rows, :] = (scaled * gain_t[...]).astype(BF16)

    tiles(T_ROWS, 80, norm_time)
    pass_near(0)
    loads[1].wait()
    keep_col = patch_keep(R.keep_v, head, count, frames)
    R.kt_col[...] = keep_col
    for g, (start, size) in enumerate(T_GROUPS):
        R.bias_t[g, :size, :size] = time_bias(keep_col[start : start + size], size)
    R.ks_row[...] = jnp.zeros_like(R.ks_row)
    lane = lax.broadcasted_iota(jnp.int32, (1, 256), 1)
    row = lax.broadcasted_iota(jnp.int32, (SEG, SEG), 0)
    col = lax.broadcasted_iota(jnp.int32, (SEG, SEG), 1)
    for f in range(2):
        R.ks_row[f, :, :at] = R.keep_v[pl.ds(2 * head + f, 1), :].astype(F32)
        open_row = jnp.where(lane == at, 1.0, R.ks_row[f])
        R.ks_row[f] = open_row
        counted = (row == col) if f == 0 else (row == col) & (col != at)
        R.ks_col[f * SEG : (f + 1) * SEG, :] = jnp.sum(jnp.where(counted, open_row[:, :SEG], 0.0), axis=1, keepdims=True)
    row = lax.broadcasted_iota(jnp.int32, (S_ROWS, 1), 0)
    R.once[...] = jnp.where((row == at) & (head != 0), 0.0, 1.0)
    loads[2].wait()
    to_frame_order(R.low_d, R.send_b, R.perm)
    ex_cot = exchange(1, R.send_b, R.got_cot)
    all_start(ex_cot)
    pass_near(1, 2, 3)

    def time_bias_of(g, size):
        bias = R.bias_t[g, :size, :size]
        return jnp.concatenate([bias, bias], axis=0)

    ready_near(0, 1, 2, 3)
    project_qkv(u_t, R.wt_t, qkv_t, T_ROWS, 0, 6)
    attention(qkv_t, p_t, mix_t, T_GROUPS, time_bias_of, 0, 3)
    pass_near(4, 5, 6, 7)
    pass_far(0, 1, 2, 3)
    ready_far(0, 1, 2, 3)
    pass_near(8, 9)
    project_qkv(u_t, R.wt_t, qkv_t, T_ROWS, 6, 12)
    attention(qkv_t, p_t, mix_t, T_GROUPS, time_bias_of, 3, 6)
    pass_near(10, 11, 12, 13)
    loads[3].wait()

    def project(n):
        cols = pl.ds(n, 256)
        att_t[:, cols] = nn(mix_t[...], columns(R.pj_t, cols)).astype(BF16)

    tiles(width, 256, project)

    def branch(n):
        cols = pl.ds(n, 256)
        first[:T_ROWS, cols] = patches[:, cols].astype(F32) + R.kt_col[...] * nn(att_t[...], columns(R.fc, cols))

    tiles(width, 256, branch)
    to_frame_order(first, R.send_a, R.perm)
    ex_first = exchange(0, R.send_a, R.got_first)
    all_start(ex_first)
    pass_far(4, 5, 6, 7)

    qkv_s, p_s, mix_s, u_s = R.qkv_s, R.p_s, R.mix_s, R.u_s
    all_wait(ex_first)
    cls_row = gains[3:4, :]
    second, cot = R.rows_s, R.rows_c
    gather_frames(R.got_first, (cls_row, cls_row), rows_x)
    norm_rows(rows_x, gain_s, u_s, S_ROWS, 208)
    ready_near(4, 5, 6, 7)
    ready_far(4, 5, 6, 7)
    project_qkv(u_s, R.wt_s, qkv_s, S_ROWS, 0, 12)
    all_wait(ex_cot)
    gather_frames(R.got_cot, (gains[4:5, :], jnp.zeros((1, width), F32)), cot)
    cls_part = cls_attention(qkv_s, R.ks_row, at, width)
    R.cls_sum[0] = jnp.broadcast_to(cls_part, (8, width))
    cls_total = sum_rows(0, R.cls_sum, True)
    attention(qkv_s, p_s, mix_s, S_GROUPS, lambda g, size: space_bias(R.ks_row, g), 0, 6)
    set_row(mix_s, 0, at, cls_total() * (1.0 / frames), BF16)
    set_row(mix_s, SEG, at, jnp.zeros((1, width), F32), BF16)
    pass_far(8, 9)

    def project_space(n):
        cols = pl.ds(n, 256)
        second[:, cols] = rows_x[:, cols] + R.ks_col[...] * nn(mix_s[...], columns(R.pj_s, cols))

    tiles(width, 256, project_space)

    u, uw, dz, dzw = R.low_a, R.low_b, R.low_c, R.low_d
    acc, du = R.rows_a, R.rows_d
    kcol, once = R.ks_col, R.once

    def prepare(r):
        rows = pl.ds(r, 208)
        scaled, _ = stats(second[rows, :])
        low = (scaled * gain_m[...]).astype(BF16)
        u[rows, :] = low
        uw[rows, :] = (low.astype(F32) * once[rows, :]).astype(BF16)
        grad = cot[rows, :] * kcol[rows, :]
        dz[rows, :] = grad.astype(BF16)
        dzw[rows, :] = (grad * once[rows, :]).astype(BF16)

    tiles(S_ROWS, 208, prepare)
    acc[...] = jnp.zeros_like(acc)
    du[...] = jnp.zeros_like(du)
    w1_ref, w2_ref = R.w1, R.w2
    def hidden(s, n):
        cols = pl.ds(n * 256, 256)
        w1 = columns(w1_ref.at[s], cols)
        w2 = rows_of(w2_ref.at[s], n * 256)
        hid = nn(u[...], w1)
        phi = 0.5 + 0.5 * lax.erf(hid * 0.7071067811865476)
        act = (hid * phi).astype(BF16)
        slope = phi + hid * (0.3989422804014327 * jnp.exp(hid * hid * -0.5))
        acc[...] += nn(act, w2)
        dhid = (nt(dz[...], w2) * slope).astype(BF16)
        du[...] += nt(dhid, w1)
        w2_ref[s, n * 4 : n * 4 + 4] = tn(act, dzw[...]).astype(BF16).reshape(4, 64, width)
        w1_ref[s, :, :, cols] = tn(uw[...], dhid).astype(BF16).reshape(width // 64, 64, 256)

    for n in range(width // 256):
        if n:
            pass_far(8 + 2 * n, 9 + 2 * n)
        ready_near(8 + 2 * n, 9 + 2 * n)
        ready_far(8 + 2 * n, 9 + 2 * n)
        sent(8 + 2 * n, 9 + 2 * n)

        def by_slot(s, carry, n=n):
            hidden(s, n)
            return carry

        lax.fori_loop(0, 4, by_slot, 0)
        service(n)
    R.dgain_m[...] = jnp.zeros((1, width), F32)

    def finish_mlp(r):
        rows = pl.ds(r, 208)
        x = second[rows, :]
        scaled, factor = stats(x)
        acc[rows, :] = x + kcol[rows, :] * acc[rows, :]
        grad = du[rows, :]
        R.dgain_m[...] += jnp.sum(grad * scaled * once[rows, :], axis=0, keepdims=True)
        cot[rows, :] += norm_back(grad, gain_m[...], scaled, factor)

    tiles(S_ROWS, 208, finish_mlp)
    R.ocls[...] = acc[at : at + 1, :].astype(BF16)
    scatter_frames(acc, R.send_b)
    ex_out = exchange(2, R.send_b, R.got_cot)

    def out_steps():
        all_start(ex_out)
        yield
        all_wait(ex_out)
        to_patch_order(R.got_cot, rows_x, R.perm)
        R.low_d[:T_ROWS, :] = rows_x[:T_ROWS, :].astype(BF16)
        store_out.start()

    used = frames * count
    store_out = pltpu.make_async_copy(R.low_d.at[pl.ds(0, used)], R.out, R.lo.at[5])
    extra[15] = out_steps()
    service(3)

    dsecond = cot
    low, loww, dmix, dqkv = R.low_a, R.low_b, R.low_c, R.dqkv
    low[...] = (dsecond[...] * kcol[...]).astype(BF16)
    loww[...] = (dsecond[...] * (kcol[...] * once[...])).astype(BF16)
    dcls_second = dsecond[at : at + 1, :]
    set_row(low, SEG, at, dcls_second, BF16)
    sent(4, 5, 6, 7)

    def back_space(n):
        cols = pl.ds(n, 256)
        dmix[:, cols] = nt(low[...], rows_of(R.pj_s, n)).astype(BF16)
        R.pj_s[pl.ds(n // 64, 4)] = tn(mix_s[:, cols], loww[...]).astype(BF16).reshape(4, 64, width)

    tiles(width, 256, back_space)
    service(4)
    dcls_mix = dmix[SEG - 16 : SEG, :].astype(F32)[at - SEG + 16 : at - SEG + 17, :] * (1.0 / frames)
    set_row(dmix, 0, at, dcls_mix, BF16)
    set_row(dmix, SEG, at, dcls_mix, BF16)
    for n in range(3):
        attention_back(qkv_s, p_s, dmix, dqkv, S_GROUPS, 2 * n, 2 * n + 2)
        service(5 + n)
    qkv_back(dqkv, R.wt_s, du, S_ROWS)
    service(8)
    qkv_grad(dqkv, u_s, R.wt_s, S_ROWS)
    service(9)
    R.dcls_sum[0] = jnp.broadcast_to(du[at : at + 1, :] + du[SEG + at : SEG + at + 1, :], (8, width))
    R.dgain_s[...] = jnp.zeros((1, width), F32)
    dfirst = R.rows_a

    def finish_space(r):
        rows = pl.ds(r, 208)
        scaled, factor = stats(rows_x[rows, :])
        grad = du[rows, :]
        R.dgain_s[...] += jnp.sum(grad * scaled, axis=0, keepdims=True)
        dfirst[rows, :] = dsecond[rows, :] + norm_back(grad, gain_s[...], scaled, factor)

    tiles(S_ROWS, 208, finish_space)
    scatter_frames(dfirst, R.send_a)
    for i in range(6):
        join_core(i)
    ex_df = exchange(3, R.send_a, R.got_first)
    all_start(ex_df)
    dcls_total = sum_rows(1, R.dcls_sum, False)
    service(10)

    df = R.rows_s
    all_wait(ex_df)
    service(11)
    to_patch_order(R.got_first, df, R.perm)
    scaled, factor = stats(cls_row)
    R.dcls[...] = dcls_second + norm_back(dcls_total(), gain_s[...], scaled, factor)
    low, datt, dmix = R.low_a, R.low_b, R.low_c
    low[:T_ROWS, :] = (df[:T_ROWS, :] * R.kt_col[...]).astype(BF16)
    sent(0, 1, 2, 3)

    def back_fc(n):
        cols = pl.ds(n, 256)
        datt[:T_ROWS, cols] = nt(low[:T_ROWS, :], rows_of(R.fc, n)).astype(BF16)
        R.fc[pl.ds(n // 64, 4)] = tn(att_t[:, cols], low[:T_ROWS, :]).astype(BF16).reshape(4, 64, width)

    tiles(width, 256, back_fc)
    service(12)

    def back_time(n):
        cols = pl.ds(n, 256)
        dmix[:T_ROWS, cols] = nt(datt[:T_ROWS, :], rows_of(R.pj_t, n)).astype(BF16)
        R.pj_t[pl.ds(n // 64, 4)] = tn(mix_t[:, cols], datt[:T_ROWS, :]).astype(BF16).reshape(4, 64, width)

    tiles(width, 256, back_time)
    service(13)
    for n in range(3):
        attention_back(qkv_t, p_t, dmix, dqkv, T_GROUPS, 2 * n, 2 * n + 2)
        service(14 + n)
    qkv_back(dqkv, R.wt_t, du, T_ROWS)
    service(17)
    qkv_grad(dqkv, u_t, R.wt_t, T_ROWS)
    service(18)
    R.dgain_t[...] = jnp.zeros((1, width), F32)

    def finish_time(r):
        rows = pl.ds(r, 80)
        scaled, factor = stats(patches[rows, :].astype(F32))
        grad = du[rows, :]
        R.dgain_t[...] += jnp.sum(grad * scaled, axis=0, keepdims=True)
        df[rows, :] += norm_back(grad, gain_t[...], scaled, factor)

    tiles(T_ROWS, 80, finish_time)
    store = pltpu.make_async_copy(df.at[pl.ds(0, used)], R.dx, R.lo.at[4])
    store.start()
    for n, gain in enumerate((R.dgain_t, R.dgain_s, R.dgain_m)):
        R.gains[0, n : n + 1, :] = gain[...]
    def gain_part(j):
        peer = ([peer_c, peer_y] + bits)[j]
        return remote(R.gains.at[0], R.gains.at[1 + j], (R.gg_s, R.gg_r), j, peer)

    def gain_steps():
        for j in range(2 + levels):
            gain_part(j).start()
            yield
            gain_part(j).wait()
            R.gains[0] = R.gains[0] + R.gains[1 + j]

    extra[16] = gain_steps()
    service(19)
    finish_units()
    R.gains_out[...] = R.gains[0]
    store.wait()
    store_out.wait()


def local(
    patches, cls_token, keep_mask, gain_time, qkv_time, proj_time, temporal_fc, gain_space, qkv_space, proj_space,
    gain_mlp, mlp_in, mlp_out, cotangent, cls_cotangent,
):
    _, frames, count, width = patches.shape
    heads_here, hd = qkv_time.shape[1], qkv_time.shape[3]

    def by_patch(x):
        return jnp.transpose(x[0], (1, 0, 2)).reshape(count * frames, width)

    def by_head(w):
        return jnp.transpose(w, (1, 2, 3, 0))

    def blocks(w):
        return w.reshape(-1, 64, width)

    zero = jnp.zeros((3, width), F32)
    rows_in = jnp.concatenate(
        [gain_time[None], gain_space[None], gain_mlp[None], cls_token.astype(F32), cls_cotangent.astype(F32), zero]
    )
    large = dict(
        patches=by_patch(patches), cot=by_patch(cotangent), keep=keep_mask[0], wt_t_in=by_head(qkv_time),
        pj_t_in=proj_time, fc_in=blocks(temporal_fc), wt_s_in=by_head(qkv_space), pj_s_in=proj_space,
        w1_in=blocks(mlp_in), w2_in=blocks(mlp_out),
    )
    small = dict(rows_in=rows_in)
    frame_rows, square, row = (frames, count, width), (width // 64, 64, width), (1, width)
    heads = (heads_here, 3, hd, width)
    t_rows, s_rows, ours = (T_ROWS, width), (S_ROWS, width), (count * frames, width)
    in_hbm = dict(
        out=(ours, BF16), dx=(ours, F32), dw1=(square, BF16), dw2=(square, BF16), dfc=(square, BF16),
        dwt_s=(heads, BF16), dpj_s=(proj_space.shape, BF16), dwt_t=(heads, BF16), dpj_t=(proj_time.shape, BF16),
    )
    in_vmem = dict(ocls=(row, BF16), dcls=(row, F32), gains_out=((8, width), F32))
    levels = lax.axis_size("clip").bit_length() - 1
    vmem = dict(
        wt_t=((3,) + square, BF16), pj_t=(square, BF16), fc=(square, BF16), wt_s=((3,) + square, BF16),
        pj_s=(square, BF16), w1=((4,) + square, BF16), w2=((4,) + square, BF16),
        patches_v=(t_rows, BF16), keep_v=(keep_mask.shape[1:], jnp.int32),
        kt_col=((T_ROWS, 1), F32), ks_row=((2, 1, 256), F32), ks_col=((S_ROWS, 1), F32), once=((S_ROWS, 1), F32),
        bias_t=((4, 112, 128), F32), u_t=(t_rows, BF16), qkv_t=((T_ROWS, 3 * width), BF16),
        p_t=((6, 4, 224, 128), F32), mix_t=(t_rows, BF16), att_t=(t_rows, BF16),
        rows_x=(s_rows, F32), rows_s=(s_rows, F32), rows_c=(s_rows, F32), rows_a=(s_rows, F32), rows_d=(s_rows, F32),
        low_a=(s_rows, BF16), low_b=(s_rows, BF16), low_c=(s_rows, BF16), low_d=(s_rows, BF16),
        u_s=(s_rows, BF16), qkv_s=((S_ROWS, 3 * width), BF16), mix_s=(s_rows, BF16),
        p_s=((6, 2, 416, 256), F32), dqkv=((S_ROWS, 3 * width), BF16),
        perm=((width // 128, T_ROWS, 128), F32), send_a=(frame_rows, BF16),
        send_b=(frame_rows, BF16), got_first=(frame_rows, BF16), got_cot=(frame_rows, BF16),
        cls_sum=((4, 8, width), F32), dcls_sum=((4, 8, width), F32),
        dgain_t=(row, F32), dgain_s=(row, F32), dgain_m=(row, F32), gains=((3 + levels, 8, width), F32),
        near_a=((6, 2, 3, 64, width), BF16), near_b=((3, 2, 4, 64, width), BF16),
        near_c=((3, 2, width // 64, 64, 256), BF16),
    )
    pairs = dict(wy=14, wx=42, wc=14, wf=14, ex=12, row=6, gu=240, gg=2 + levels)
    sems = dict(wo=14, exo=4, lo=6, go=15)
    for name, n in pairs.items():
        sems[name + "_s"] = n
        sems[name + "_r"] = n
    flags = dict(free=120)
    names = [*large, *small, *in_hbm, *in_vmem, *vmem, *sems, *flags]
    hbm, vm = pl.BlockSpec(memory_space=pl.ANY), pl.BlockSpec(memory_space=pltpu.VMEM)
    output, dx, d_w1, d_w2, d_fc, d_qs, d_ps, d_qt, d_pt, out_cls, cls_grad, gains = pl.pallas_call(
        partial(whole_step, names, frames),
        out_shape=[jax.ShapeDtypeStruct(s, d) for s, d in [*in_hbm.values(), *in_vmem.values()]],
        in_specs=[hbm] * len(large) + [vm] * len(small),
        out_specs=[hbm] * len(in_hbm) + [vm] * len(in_vmem),
        scratch_shapes=[pltpu.VMEM(s, d) for s, d in vmem.values()]
        + [pltpu.SemaphoreType.DMA((n,)) for n in sems.values()]
        + [pltpu.SemaphoreType.REGULAR((n,)) for n in flags.values()],
        compiler_params=pltpu.CompilerParams(collective_id=0, has_side_effects=True, vmem_limit_bytes=60 << 20),
    )(*large.values(), *small.values())

    def by_frame(x):
        return jnp.transpose(x.reshape(count, frames, width), (1, 0, 2))[None]

    def by_width(w):
        return jnp.transpose(w.astype(F32), (3, 0, 1, 2))

    def whole(w):
        return w.astype(F32).reshape(width, width)

    return (
        by_frame(output), out_cls, by_frame(dx), cls_grad, gains[0], by_width(d_qt), d_pt.astype(F32), whole(d_fc),
        gains[1], by_width(d_qs), d_ps.astype(F32), gains[2], whole(d_w1), whole(d_w2),
    )


def solution(mesh):
    rows, wide, by_head = P("clip", None, "head", None), P("clip", None), P(None, "head", None, None)
    in_specs = (
        rows, wide, P("clip", None, None), P(), by_head, P("head", None, None), P(), P(), by_head,
        P("head", None, None), P(), P(None, "head"), P("head", None), rows, wide,
    )
    out_specs = (
        rows, wide, rows, wide, P(), by_head, P("head", None, None), P(), P(), by_head,
        P("head", None, None), P(), P(None, "head"), P("head", None),
    )
    return jax.shard_map(local, mesh=mesh, in_specs=in_specs, out_specs=out_specs, check_vma=False)
```

```python
from functools import partial
from types import SimpleNamespace

import jax
import jax.numpy as jnp
from jax import lax
from jax.experimental import pallas as pl
from jax.experimental.pallas import tpu as pltpu
from jax.sharding import PartitionSpec as P

EPSILON = 1e-06
NEGATIVE = -1e30
F32 = jnp.float32
BF16 = jnp.bfloat16


def nn(a, b):
    return lax.dot_general(a, b, (((1,), (0,)), ((), ())), preferred_element_type=F32)


def nt(a, b):
    return lax.dot_general(a, b, (((1,), (1,)), ((), ())), preferred_element_type=F32)


def tn(a, b):
    return lax.dot_general(a, b, (((0,), (0,)), ((), ())), preferred_element_type=F32)


def tiles(total, size, body):
    def step(i, carry):
        body(pl.multiple_of(i * size, size))
        return carry

    lax.fori_loop(0, total // size, step, 0)


def stats(x):
    center = x - jnp.mean(x, axis=-1, keepdims=True)
    factor = lax.rsqrt(jnp.mean(center * center, axis=-1, keepdims=True) + EPSILON)
    return center * factor, factor


def norm_back(grad, gain, scaled, factor):
    weighted = grad * gain
    inner = weighted - jnp.mean(weighted, axis=-1, keepdims=True)
    return factor * (inner - scaled * jnp.mean(weighted * scaled, axis=-1, keepdims=True))


def pair_masks():
    lane = lax.broadcasted_iota(jnp.int32, (1, 128), 1)
    return (lane < 64).astype(F32).astype(BF16), (lane >= 64).astype(F32).astype(BF16)


def stacked(x):
    low, high = pair_masks()
    return jnp.concatenate([x * low, x * high], axis=0)


def unstacked(x):
    rows = x.shape[0] // 2
    lane = lax.broadcasted_iota(jnp.int32, (1, 128), 1)
    return jnp.where(lane < 64, x[:rows], x[rows:])


def norm_rows(x_ref, gain_ref, u_ref, total, chunk):
    def body(r):
        rows = pl.ds(r, chunk)
        scaled, _ = stats(x_ref[rows, :])
        u_ref[rows, :] = (scaled * gain_ref[...]).astype(BF16)

    tiles(total, chunk, body)


def project_qkv(u_ref, wt_ref, qkv_ref, rows, first, last):
    width = u_ref.shape[1]
    size = (last - first) * 64

    def body(t, carry):
        scale = jnp.where(t == 0, 0.125, 1.0)
        out = nt(u_ref[:rows, :], wt_ref[t, first:last].reshape(size, width)) * scale
        qkv_ref[:rows, pl.ds(pl.multiple_of(t * width + first * 64, 128), size)] = out.astype(BF16)
        return carry

    lax.fori_loop(0, 3, body, 0)


def columns(ref, cols):
    part = ref[:, :, cols]
    return part.reshape(part.shape[0] * part.shape[1], part.shape[2])


def rows_of(ref, n):
    part = ref[pl.ds(n // 64, 4)]
    return part.reshape(256, part.shape[2])


def qkv_back(dqkv_ref, wt_ref, du_ref, rows):
    width = du_ref.shape[1]

    def back(n):
        cols = pl.ds(n, 256)
        total = nn(dqkv_ref[:rows, :width], columns(wt_ref.at[0], cols))
        total += nn(dqkv_ref[:rows, width : 2 * width], columns(wt_ref.at[1], cols))
        total += nn(dqkv_ref[:rows, 2 * width :], columns(wt_ref.at[2], cols))
        du_ref[:rows, cols] = total

    tiles(width, 256, back)


def qkv_grad(dqkv_ref, u_ref, wt_ref, rows):
    width = u_ref.shape[1]

    def grad(i, carry):
        cols = pl.ds(pl.multiple_of(i * 256, 256), 256)
        out = tn(dqkv_ref[:rows, cols], u_ref[:rows, :]).astype(BF16)
        wt_ref[i // 3, pl.ds((i % 3) * 4, 4)] = out.reshape(4, 64, width)
        return carry

    lax.fori_loop(0, 9, grad, 0)


def softmax(scores):
    highest = jnp.max(scores, axis=-1, keepdims=True)
    weights = jnp.exp(scores - highest)
    return weights * (1.0 / jnp.sum(weights, axis=-1, keepdims=True))


def attention(qkv_ref, p_ref, mix_ref, groups, bias_of, first, last):
    width = mix_ref.shape[1]

    def body(hp, carry):
        qc = pl.ds(pl.multiple_of(hp * 128, 128), 128)
        kc = pl.ds(pl.multiple_of(width + hp * 128, 128), 128)
        vc = pl.ds(pl.multiple_of(2 * width + hp * 128, 128), 128)
        all_rows = [pl.ds(start, size) for start, size in groups]
        scores = [nt(stacked(qkv_ref[rows, qc]), qkv_ref[rows, kc]) for rows in all_rows]
        probs = [softmax(scores[g] + bias_of(g, size)).astype(BF16) for g, (_, size) in enumerate(groups)]
        mixes = [unstacked(nn(prob, qkv_ref[rows, vc])).astype(BF16) for prob, rows in zip(probs, all_rows)]
        for g, (_, size) in enumerate(groups):
            p_ref[hp, g, : 2 * size, :size] = probs[g]
            mix_ref[all_rows[g], qc] = mixes[g]
        return carry

    lax.fori_loop(first, last, body, 0)


def attention_back(qkv_ref, p_ref, dmix_ref, dqkv_ref, groups, first, last):
    width = dmix_ref.shape[1]

    def body(hp, carry):
        qc = pl.ds(pl.multiple_of(hp * 128, 128), 128)
        kc = pl.ds(pl.multiple_of(width + hp * 128, 128), 128)
        vc = pl.ds(pl.multiple_of(2 * width + hp * 128, 128), 128)
        all_rows = [pl.ds(start, size) for start, size in groups]
        ups = [stacked(dmix_ref[rows, qc]) for rows in all_rows]
        probs = [p_ref[hp, g, : 2 * size, :size] for g, (_, size) in enumerate(groups)]
        dprobs = [nt(up, qkv_ref[rows, vc]) for up, rows in zip(ups, all_rows)]
        dvs = [tn(prob, up).astype(BF16) for prob, up in zip(probs, ups)]
        dscores = []
        for prob, dprob in zip(probs, dprobs):
            wide = prob.astype(F32)
            delta = jnp.sum(wide * dprob, axis=-1, keepdims=True)
            dscores.append((wide * (dprob - delta)).astype(BF16))
        dqs = [(unstacked(nn(ds, qkv_ref[rows, kc])) * 0.125).astype(BF16) for ds, rows in zip(dscores, all_rows)]
        dks = [tn(ds, stacked(qkv_ref[rows, qc])).astype(BF16) for ds, rows in zip(dscores, all_rows)]
        for g, rows in enumerate(all_rows):
            dqkv_ref[rows, qc] = dqs[g]
            dqkv_ref[rows, kc] = dks[g]
            dqkv_ref[rows, vc] = dvs[g]
        return carry

    lax.fori_loop(first, last, body, 0)


T_ROWS = 400
T_GROUPS = ((0, 96), (96, 96), (192, 96), (288, 112))
SEG = 208
S_ROWS = 416
S_GROUPS = ((0, 208), (208, 208))


def time_bias(kcol, size):
    row = lax.broadcasted_iota(jnp.int32, (size, size), 0)
    col = lax.broadcasted_iota(jnp.int32, (size, size), 1)
    kept = jnp.sum(jnp.where(row == col, kcol, 0.0), axis=0, keepdims=True)
    ok = ((row // 8) == (col // 8)) & ((kept > 0.0) | (row == col))
    return jnp.where(ok, 0.0, NEGATIVE)


def patch_keep(keep_ref, head, count, frames):
    total = keep_ref.shape[1]
    row = lax.broadcasted_iota(jnp.int32, (T_ROWS, total), 0)
    col = lax.broadcasted_iota(jnp.int32, (T_ROWS, total), 1)
    pick = ((row // frames + head * count == col) & (row < frames * count)).astype(F32).astype(BF16)
    by_frame = nt(pick, keep_ref[...].astype(F32).astype(BF16))
    row = lax.broadcasted_iota(jnp.int32, (T_ROWS, frames), 0)
    col = lax.broadcasted_iota(jnp.int32, (T_ROWS, frames), 1)
    return jnp.sum(jnp.where(row % frames == col, by_frame, 0.0), axis=1, keepdims=True)


def space_bias(krow_ref, g):
    return (krow_ref[g, :, :SEG] - 1.0) * (-NEGATIVE)


def to_patch_order(src_ref, dst_ref, perm_ref):
    frames, count, width = src_ref.shape
    used = frames * count
    for j in range(width // 128):
        for f in range(frames):
            perm_ref[j, pl.ds(f, count, stride=frames), :] = src_ref[f, :, j * 128 : (j + 1) * 128].astype(F32)
        dst_ref[:used, j * 128 : (j + 1) * 128] = perm_ref[j, :used, :]
    dst_ref[used:T_ROWS, :] = jnp.zeros((T_ROWS - used, width), F32)


def to_frame_order(src_ref, dst_ref, perm_ref):
    frames, count, width = dst_ref.shape
    for j in range(width // 128):
        used = frames * count
        perm_ref[j, :used, :] = src_ref[:used, j * 128 : (j + 1) * 128].astype(F32)
        for f in range(frames):
            out = perm_ref[j, pl.ds(f, count, stride=frames), :]
            dst_ref[f, :, j * 128 : (j + 1) * 128] = out.astype(dst_ref.dtype)


def gather_frames(got_ref, cls_row, out_ref):
    sources, count = got_ref.shape[0] // 2, got_ref.shape[1]
    for f in range(2):
        base = f * SEG
        for s in range(sources):
            out_ref[base + s * count : base + (s + 1) * count, :] = got_ref[2 * s + f].astype(F32)
        at = base + sources * count
        out_ref[at : at + 1, :] = cls_row[f]
        out_ref[at + 1 : base + SEG, :] = jnp.zeros((SEG - 1 - sources * count, out_ref.shape[1]), F32)


def scatter_frames(x_ref, send_ref):
    sources, count = send_ref.shape[0] // 2, send_ref.shape[1]
    for f in range(2):
        for s in range(sources):
            at = f * SEG + s * count
            send_ref[2 * s + f] = x_ref[at : at + count, :].astype(send_ref.dtype)


def cls_attention(qkv_ref, krow_ref, at, width):
    lane = lax.broadcasted_iota(jnp.int32, (16, width), 1) // 64
    own = (lane == lax.broadcasted_iota(jnp.int32, (16, width), 0)).astype(F32)
    total = jnp.zeros((1, width), F32)
    for f in range(2):
        q = qkv_ref[f * SEG + at : f * SEG + at + 1, :width].astype(F32)
        k = qkv_ref[f * SEG : (f + 1) * SEG, width : 2 * width]
        v = qkv_ref[f * SEG : (f + 1) * SEG, 2 * width :]
        prob = softmax(nt((own * q).astype(BF16), k) + space_bias(krow_ref, f))
        total += jnp.sum(own * nn(prob.astype(BF16), v), axis=0, keepdims=True)
    return total


def blocks_swapped(x, distance):
    width = x.shape[1]
    quarter = width // 4
    order = [i ^ distance for i in range(4)]
    return jnp.concatenate([x[:, i * quarter : (i + 1) * quarter] for i in order], axis=1)


def set_row(ref, base, at, row, dtype):
    start = base + at // 16 * 16
    pick = lax.broadcasted_iota(jnp.int32, (16, 1), 0) == at % 16
    kept = ref[start : start + 16, :].astype(F32)
    ref[start : start + 16, :] = jnp.where(pick, jnp.broadcast_to(row, kept.shape), kept).astype(dtype)


MESH = pl.DeviceIdType.MESH

ROUTES = (0, 2, 0, 2, 1, 0, 0, 1, 0, 0, 0, 1, 0, 0, 0)
ORDER = (
    (0, 1),
    (2, 3, 0, 1),
    (4, 5, 2, 3),
    (4, 5, 0, 1),
    (),
    (),
    (),
    (2, 3),
    (),
    (4, 0, 1),
    (5, 2, 3, 0),
    (6, 7, 8, 9),
    (10, 6, 7, 4, 8, 5, 9, 2, 10, 1, 0, 15),
    (11, 4, 3),
    (11, 5),
    (7, 1, 2, 0),
    (3, 4),
    (12, 13, 14, 6, 5),
    (12, 13, 14, 11, 1, 2, 3, 0),
    (8, 6, 4, 5, 16, 9, 2, 1, 8, 3, 6, 10, 16, 4, 8, 15, 7, 6, 8, 5, 7, 16, 6, 9, 12, 8, 7, 10, 9, 16, 7, 6,
     13, 10, 12, 9, 10, 16, 8, 12, 14, 9, 7, 10, 11, 16, 12, 13, 11, 12, 14, 13, 11, 16, 9, 14, 13, 10, 11,
     14, 12, 16, 13, 14, 11, 10, 13, 10, 14, 16),
)


def arrivals(route, levels, everywhere):
    return 2 + (3, 4, 5)[route] + levels - 2 + 2 + (3 if everywhere else 0)


def whole_step(names, frames, *refs):
    R = SimpleNamespace(**dict(zip(names, refs)))
    clip, head = lax.axis_index("clip"), lax.axis_index("head")
    digit = (clip % 2, clip // 2 % 2, clip // 4 % 2)
    side, turn = digit[0], digit[1]
    width = R.wt_t.shape[3]
    count = R.patches.shape[0] // frames
    at = 4 * count
    peer_c, peer_y, peer_d = (clip, head ^ 1), (clip, head ^ 2), (clip, head ^ 3)
    levels = lax.axis_size("clip").bit_length() - 1
    bits = [(clip ^ (1 << j), head) for j in range(levels)]

    def part(ref, q, n):
        return ref.at[:, pl.ds(q * 16, n * 16), :]

    def hidden_tile(w1, w2, i, q, n):
        t = (i - 8) // 2
        if i % 2:
            return w1.at[:, pl.ds(q * 16, n * 16), pl.ds(t * 256, 256)]
        return part(w2.at[pl.ds(t * 4, 4)], q, n)

    def slot(i, s, q=0, n=4):
        if i >= 8:
            return hidden_tile(R.w1.at[s], R.w2.at[s], i, q, n)
        wt, pj = (R.wt_t, R.pj_t) if i < 4 else (R.wt_s, R.pj_s)
        if i % 4 == 3:
            return part(pj.at[pl.ds(s * 3, 3)], q, n)
        return part(wt.at[:, s * 3 + i % 4], q, n)

    def source(i, q=0, n=4):
        if i >= 8:
            return hidden_tile(R.w1_in, R.w2_in, i, q, n)
        wt, pj = (R.wt_t_in, R.pj_t_in) if i < 4 else (R.wt_s_in, R.pj_s_in)
        return part(pj if i % 4 == 3 else wt.at[i % 4], q, n)

    def remote(src, dst, sems, index, peer):
        return pltpu.make_async_remote_copy(
            src_ref=src, dst_ref=dst, send_sem=sems[0].at[index], recv_sem=sems[1].at[index],
            device_id=peer, device_id_type=MESH,
        )

    mine = side + 2 * turn

    def y_copy(i):
        return remote(source(i, mine, 1), slot(i, 2, mine, 1), (R.wy_s, R.wy_r), i, peer_y)

    def clip_copies(i):
        quarter = slot(i, 2, mine, 1)
        near = (bits[0], bits[1], (clip ^ 3, head))
        return [remote(quarter, quarter, (R.wx_s, R.wx_r), 3 * i + n, peer) for n, peer in enumerate(near)]

    def c_copy(i):
        return remote(source(i), slot(i, 1), (R.wc_s, R.wc_r), i, peer_c)

    def f_copy(i):
        return remote(slot(i, 2), slot(i, 3), (R.wf_s, R.wf_r), i, peer_c)

    def own_copy(i):
        return pltpu.make_async_copy(source(i), slot(i, 0), R.wo.at[i])

    def pass_near(*pieces):
        for i in pieces:
            y_copy(i).wait_recv()
            for copy in clip_copies(i):
                copy.start()

    def pass_far(*pieces):
        for i in pieces:
            for copy in clip_copies(i):
                copy.wait_recv()
            f_copy(i).start()

    def ready_near(*pieces):
        for i in pieces:
            own_copy(i).wait()
            c_copy(i).wait_recv()

    def ready_far(*pieces):
        for i in pieces:
            f_copy(i).wait_recv()

    def sent(*pieces):
        for i in pieces:
            y_copy(i).wait_send()
            c_copy(i).wait_send()
            f_copy(i).wait_send()
            for copy in clip_copies(i):
                copy.wait_send()

    def exchange(k, src, dst):
        here = pl.ds(2 * head, 2)
        copies = []
        for r, peer in ((2, peer_y), (3, peer_d), (1, peer_c)):
            there = pl.ds(2 * (head ^ r), 2)
            copies.append(remote(src.at[there], dst.at[here], (R.ex_s, R.ex_r), 3 * k + r - 1, peer))
        copies.append(pltpu.make_async_copy(src.at[here], dst.at[here], R.exo.at[k]))
        return copies

    def all_start(copies):
        for copy in copies:
            copy.start()

    def all_wait(copies):
        for copy in copies:
            copy.wait()

    def sum_rows(k, buf, swapped):
        copies = [
            remote(buf.at[0], buf.at[r], (R.row_s, R.row_r), 3 * k + r - 1, peer)
            for r, peer in ((2, peer_y), (3, peer_d), (1, peer_c))
        ]
        all_start(copies)

        def finish():
            all_wait(copies)
            terms = [buf[r] for r in range(4)]
            if swapped:
                terms = [terms[0]] + [blocks_swapped(terms[r], r) for r in (1, 2, 3)]
            total = (terms[0] + terms[1]) + (terms[2] + terms[3])
            return total[0:1, :]

        return finish

    def unit(i):
        if i < 6:
            n = i // 2
            if i % 2:
                return lambda s, q=0, k=4: R.w1.at[s, :, pl.ds(q * 16, k * 16), pl.ds(n * 256, 256)]
            return lambda s, q=0, k=4: part(R.w2.at[s, pl.ds(n * 4, 4)], q, k)
        if i == 10:
            return lambda s, q=0, k=4: part(R.fc.at[pl.ds((head ^ s) * 3, 3)], q, k)
        wt, pj = (R.wt_s, R.pj_s) if i < 10 else (R.dwt_own, R.pj_t)
        n = i - 6 if i < 10 else i - 11
        if n == 0:
            return lambda s, q=0, k=4: part(pj.at[pl.ds(s * 3, 3)], q, k)
        return lambda s, q=0, k=4: part(wt.at[:, s * 3 + n - 1], q, k)

    def result(i, q, k):
        if i < 6:
            n = i // 2
            if i % 2:
                return R.dw1.at[:, pl.ds(q * 16, k * 16), pl.ds(n * 256, 256)]
            return part(R.dw2.at[pl.ds(n * 4, 4)], q, k)
        if i == 10:
            return part(R.dfc.at[pl.ds(head * 3, 3)], q, k)
        wt, pj = (R.dwt_s, R.dpj_s) if i < 10 else (R.dwt_t, R.dpj_t)
        n = i - 6 if i < 10 else i - 11
        return part(pj if n == 0 else wt.at[n - 1], q, k)

    def near_slot(i, k):
        if i < 6:
            return (R.near_c if i % 2 else R.near_b).at[i // 2, k]
        if i < 9:
            return R.near_b.at[i - 6, k, pl.ds(0, 3)]
        return R.near_a.at[i - 9, k]

    def add(dst, src):
        def body(r, carry):
            dst[r] = dst[r] + src[r]
            return carry

        lax.fori_loop(0, dst.shape[0], body, 0)

    def steps_of(i):
        u, route = unit(i), ROUTES[i]
        a, b = (1, 2) if route == 2 else (0, 1)
        half = 2 * digit[a]
        quarter = half + digit[b]
        counts = [sum(arrivals(ROUTES[k], levels, k == 10) for k in range(i)), 0]

        def copy(src, dst, peer):
            counts[0] += 1
            return pltpu.make_async_remote_copy(
                src_ref=src, dst_ref=dst, send_sem=R.gu_s.at[i * 2 + counts[0] % 2], recv_sem=R.gu_r.at[counts[0] - 1],
                device_id=peer, device_id_type=MESH,
            )

        def land(k):
            at_q = counts[1]
            counts[1] += k
            s, q = ((1, at_q) if at_q < 4 else (3, at_q - 4) if at_q < 8 else (2, at_q - 8))
            return u(s, q, k), (s, q, k)

        steps = [([copy(u(1), near_slot(i, 0), peer_c), copy(u(3), near_slot(i, 1), peer_c)],
                  [(u(2), near_slot(i, 1)), (u(0), near_slot(i, 0))], None)]
        peers = []
        kept, joined = (0, 4), False
        whole_bits = [j for j in range(levels) if j not in (a, b)]
        order = ((-1, a, b), (a, -1, b), (a, b, -1))[route]
        for bit in list(order) + whole_bits:
            copies, sums = [], []
            if bit == -1:
                spot, (s, q, k) = land(kept[1])
                copies.append(copy(u(2, *kept), u(s ^ 2, q, k) if i == 10 else spot, peer_y))
                sums.append((u(0, *kept), spot))
                joined = True
                peers.append(peer_y)
            else:
                if bit == a:
                    kept, other = (half, 2), (2 - half, 2)
                elif bit == b:
                    kept, other = (quarter, 1), (half + 1 - digit[b], 1)
                else:
                    other = kept
                for s in (0,) if joined else (0, 2):
                    spot, _ = land(other[1])
                    copies.append(copy(u(s, *other), spot, bits[bit]))
                    sums.append((u(s, *kept), spot))
                peers.append(bits[bit])
            steps.append((copies, sums, len(peers) - 1))
        mine_q, there_q, rows = u(0, quarter, 1), result(i, quarter, 1), result(i, half, 2)
        steps.append(([copy(mine_q, there_q, bits[b]), pltpu.make_async_copy(mine_q, there_q, R.go.at[i])], [], None))
        steps.append(([copy(rows, rows, bits[a])], [], None))
        if i == 10:
            ours, far = R.dfc.at[pl.ds(head * 3, 3)], R.dfc.at[pl.ds((head ^ 2) * 3, 3)]
            steps.append(([copy(ours, ours, peer_y), copy(ours, ours, peer_c)], [], None))
            steps.append(([copy(far, far, peer_c)], [], None))
        return steps, peers

    units = [None] * 15
    stage = [0] * 15

    def tell(i, first, last):
        peers = units[i][1]
        for k in range(first, min(last, len(peers))):
            pl.semaphore_signal(R.free.at[i * (levels + 1) + k], inc=1, device_id=peers[k], device_id_type=MESH)

    def land_step(i):
        steps, _ = units[i]
        copies, sums, _ = steps[stage[i] - 1]
        all_wait(copies)
        if stage[i] == 1:
            tell(i, 0, 4)
        for dst, src in sums:
            add(dst, src)
        if stage[i] == 4:
            tell(i, 4, 8)

    landed = [0] * 15

    def advance(i):
        if units[i] is None:
            units[i] = steps_of(i)
        steps, _ = units[i]
        if stage[i] > landed[i]:
            land_step(i)
            landed[i] = stage[i]
        if stage[i] < len(steps):
            copies, _, credit = steps[stage[i]]
            if credit is not None:
                pl.semaphore_wait(R.free.at[i * (levels + 1) + credit], 1)
            all_start(copies)
        stage[i] += 1

    def join_core(i):
        if stage[i] == 1 and landed[i] == 0:
            land_step(i)
            landed[i] = 1

    extra = {}

    def service(k):
        for i in ORDER[k]:
            if i < 15:
                advance(i)
            else:
                next(extra[i], None)

    def finish_units():
        while any(stage[i] < 1 + len(units[i][0]) for i in range(15)):
            for i in reversed(range(15)):
                done = [stage[j] >= 1 + len(units[j][0]) for j in (i, i - 1)]
                if not done[0] and (i == 0 or done[1] or stage[i] < stage[i - 1]):
                    advance(i)
        for steps in extra.values():
            for _ in steps:
                pass

    barrier = pltpu.get_barrier_semaphore()
    for peer in [peer_c, peer_y, peer_d, (clip ^ 3, head)] + bits:
        pl.semaphore_signal(barrier, inc=1, device_id=peer, device_id_type=MESH)
    pl.semaphore_wait(barrier, 4 + levels)

    loads = (
        (R.patches, R.patches_v.at[pl.ds(0, frames * count)]), (R.keep, R.keep_v), (R.cot, R.low_d.at[pl.ds(0, frames * count)]), (R.fc_in, R.fc),
    )
    loads = [pltpu.make_async_copy(src, dst, R.lo.at[i]) for i, (src, dst) in enumerate(loads)]
    for i in range(3):
        loads[i].start()
    for i in range(12):
        y_copy(i).start()
    for i in range(14):
        own_copy(i).start()
        c_copy(i).start()
    loads[3].start()

    rows_x, first = R.rows_x, R.rows_s
    qkv_t, p_t, mix_t, att_t, u_t = R.qkv_t, R.p_t, R.mix_t, R.att_t, R.u_t
    patches, gains = R.patches_v, R.rows_in
    gain_t, gain_s, gain_m = gains.at[0:1], gains.at[1:2], gains.at[2:3]
    used = frames * count
    loads[0].wait()
    patches[used:, :] = jnp.zeros((T_ROWS - used, width), BF16)

    def norm_time(r):
        rows = pl.ds(r, 80)
        scaled, _ = stats(patches[rows, :].astype(F32))
        u_t[rows, :] = (scaled * gain_t[...]).astype(BF16)

    tiles(T_ROWS, 80, norm_time)
    pass_near(0)
    loads[1].wait()
    keep_col = patch_keep(R.keep_v, head, count, frames)
    R.kt_col[...] = keep_col
    for g, (start, size) in enumerate(T_GROUPS):
        R.bias_t[g, :size, :size] = time_bias(keep_col[start : start + size], size)
    R.ks_row[...] = jnp.zeros_like(R.ks_row)
    lane = lax.broadcasted_iota(jnp.int32, (1, 256), 1)
    row = lax.broadcasted_iota(jnp.int32, (SEG, SEG), 0)
    col = lax.broadcasted_iota(jnp.int32, (SEG, SEG), 1)
    for f in range(2):
        R.ks_row[f, :, :at] = R.keep_v[pl.ds(2 * head + f, 1), :].astype(F32)
        open_row = jnp.where(lane == at, 1.0, R.ks_row[f])
        R.ks_row[f] = open_row
        counted = (row == col) if f == 0 else (row == col) & (col != at)
        R.ks_col[f * SEG : (f + 1) * SEG, :] = jnp.sum(jnp.where(counted, open_row[:, :SEG], 0.0), axis=1, keepdims=True)
    row = lax.broadcasted_iota(jnp.int32, (S_ROWS, 1), 0)
    R.once[...] = jnp.where((row == at) & (head != 0), 0.0, 1.0)
    loads[2].wait()
    to_frame_order(R.low_d, R.send_b, R.perm)
    ex_cot = exchange(1, R.send_b, R.got_cot)
    pass_near(1, 2, 3)

    def time_bias_of(g, size):
        bias = R.bias_t[g, :size, :size]
        return jnp.concatenate([bias, bias], axis=0)

    ready_near(0, 1, 2, 3)
    project_qkv(u_t, R.wt_t, qkv_t, T_ROWS, 0, 6)
    attention(qkv_t, p_t, mix_t, T_GROUPS, time_bias_of, 0, 3)
    pass_near(4, 5, 6, 7)
    pass_far(0, 1, 2)
    ready_far(0, 1, 2)
    pass_far(3)
    pass_near(8, 9)
    project_qkv(u_t, R.wt_t, qkv_t, T_ROWS, 6, 12)
    attention(qkv_t, p_t, mix_t, T_GROUPS, time_bias_of, 3, 6)
    pass_near(10, 11)
    ready_far(3)
    loads[3].wait()

    def project(n):
        cols = pl.ds(n, 256)
        att_t[:, cols] = nn(mix_t[...], columns(R.pj_t, cols)).astype(BF16)

    tiles(width, 256, project)

    def branch(n):
        cols = pl.ds(n, 256)
        first[:T_ROWS, cols] = patches[:, cols].astype(F32) + R.kt_col[...] * nn(att_t[...], columns(R.fc, cols))

    tiles(width, 256, branch)
    to_frame_order(first, R.send_a, R.perm)
    ex_first = exchange(0, R.send_a, R.got_first)
    all_start(ex_first)
    for i in (12, 13):
        y_copy(i).start()
    all_start(ex_cot)
    pass_far(4, 5, 6, 7)

    qkv_s, p_s, mix_s, u_s = R.qkv_s, R.p_s, R.mix_s, R.u_s
    all_wait(ex_first)
    cls_row = gains[3:4, :]
    second, cot = R.rows_s, R.rows_c
    gather_frames(R.got_first, (cls_row, cls_row), rows_x)
    norm_rows(rows_x, gain_s, u_s, S_ROWS, 208)
    ready_near(4, 5, 6, 7)
    ready_far(4, 5, 6, 7)
    project_qkv(u_s, R.wt_s, qkv_s, S_ROWS, 0, 12)
    pass_near(12, 13)
    all_wait(ex_cot)
    gather_frames(R.got_cot, (gains[4:5, :], jnp.zeros((1, width), F32)), cot)
    cls_part = cls_attention(qkv_s, R.ks_row, at, width)
    R.cls_sum[0] = jnp.broadcast_to(cls_part, (8, width))
    cls_total = sum_rows(0, R.cls_sum, True)
    attention(qkv_s, p_s, mix_s, S_GROUPS, lambda g, size: space_bias(R.ks_row, g), 0, 6)
    set_row(mix_s, 0, at, cls_total() * (1.0 / frames), BF16)
    set_row(mix_s, SEG, at, jnp.zeros((1, width), F32), BF16)
    pass_far(8, 9)

    def project_space(n):
        cols = pl.ds(n, 256)
        second[:, cols] = rows_x[:, cols] + R.ks_col[...] * nn(mix_s[...], columns(R.pj_s, cols))

    tiles(width, 256, project_space)

    u, uw, dz, dzw = R.low_a, R.low_b, R.low_c, R.low_d
    acc, du = R.rows_a, R.rows_d
    kcol, once = R.ks_col, R.once

    def prepare(r):
        rows = pl.ds(r, 208)
        scaled, _ = stats(second[rows, :])
        low = (scaled * gain_m[...]).astype(BF16)
        u[rows, :] = low
        uw[rows, :] = (low.astype(F32) * once[rows, :]).astype(BF16)
        grad = cot[rows, :] * kcol[rows, :]
        dz[rows, :] = grad.astype(BF16)
        dzw[rows, :] = (grad * once[rows, :]).astype(BF16)

    tiles(S_ROWS, 208, prepare)
    acc[...] = jnp.zeros_like(acc)
    du[...] = jnp.zeros_like(du)
    w1_ref, w2_ref = R.w1, R.w2
    def hidden(s, n):
        cols = pl.ds(n * 256, 256)
        w1 = columns(w1_ref.at[s], cols)
        w2 = rows_of(w2_ref.at[s], n * 256)
        hid = nn(u[...], w1)
        phi = 0.5 + 0.5 * lax.erf(hid * 0.7071067811865476)
        act = (hid * phi).astype(BF16)
        slope = phi + hid * (0.3989422804014327 * jnp.exp(hid * hid * -0.5))
        acc[...] += nn(act, w2)
        dhid = (nt(dz[...], w2) * slope).astype(BF16)
        du[...] += nt(dhid, w1)
        w2_ref[s, n * 4 : n * 4 + 4] = tn(act, dzw[...]).astype(BF16).reshape(4, 64, width)
        w1_ref[s, :, :, cols] = tn(uw[...], dhid).astype(BF16).reshape(width // 64, 64, 256)

    for n in range(width // 256):
        if n:
            pass_far(8 + 2 * n, 9 + 2 * n)
        ready_near(8 + 2 * n, 9 + 2 * n)
        ready_far(8 + 2 * n, 9 + 2 * n)
        sent(8 + 2 * n, 9 + 2 * n)

        def by_slot(s, carry, n=n):
            hidden(s, n)
            return carry

        lax.fori_loop(0, 4, by_slot, 0)
        service(n)
    R.dgain_m[...] = jnp.zeros((1, width), F32)

    def finish_mlp(r):
        rows = pl.ds(r, 208)
        x = second[rows, :]
        scaled, factor = stats(x)
        acc[rows, :] = x + kcol[rows, :] * acc[rows, :]
        grad = du[rows, :]
        R.dgain_m[...] += jnp.sum(grad * scaled * once[rows, :], axis=0, keepdims=True)
        cot[rows, :] += norm_back(grad, gain_m[...], scaled, factor)

    tiles(S_ROWS, 208, finish_mlp)
    R.ocls[...] = acc[at : at + 1, :].astype(BF16)
    scatter_frames(acc, R.send_b)
    ex_out = exchange(2, R.send_b, R.got_cot)

    def out_steps():
        all_start(ex_out)
        yield
        all_wait(ex_out)
        to_patch_order(R.got_cot, rows_x, R.perm)
        R.low_d[:T_ROWS, :] = rows_x[:T_ROWS, :].astype(BF16)
        store_out.start()

    used = frames * count
    store_out = pltpu.make_async_copy(R.low_d.at[pl.ds(0, used)], R.out, R.lo.at[5])
    extra[15] = out_steps()
    service(3)

    dsecond = cot
    low, loww, dmix, dqkv = R.low_a, R.low_b, R.low_c, R.dqkv
    low[...] = (dsecond[...] * kcol[...]).astype(BF16)
    loww[...] = (dsecond[...] * (kcol[...] * once[...])).astype(BF16)
    dcls_second = dsecond[at : at + 1, :]
    set_row(low, SEG, at, dcls_second, BF16)
    sent(4, 5, 6, 7)

    def back_space(n):
        cols = pl.ds(n, 256)
        dmix[:, cols] = nt(low[...], rows_of(R.pj_s, n)).astype(BF16)

    tiles(width, 256, back_space)
    service(4)
    dcls_mix = dmix[SEG - 16 : SEG, :].astype(F32)[at - SEG + 16 : at - SEG + 17, :] * (1.0 / frames)
    set_row(dmix, 0, at, dcls_mix, BF16)
    set_row(dmix, SEG, at, dcls_mix, BF16)
    for n in range(3):
        attention_back(qkv_s, p_s, dmix, dqkv, S_GROUPS, 2 * n, 2 * n + 2)
        service(5 + n)
    qkv_back(dqkv, R.wt_s, du, S_ROWS)
    service(8)
    R.dcls_sum[0] = jnp.broadcast_to(du[at : at + 1, :] + du[SEG + at : SEG + at + 1, :], (8, width))
    R.dgain_s[...] = jnp.zeros((1, width), F32)
    dfirst = R.rows_a

    def finish_space(r):
        rows = pl.ds(r, 208)
        scaled, factor = stats(rows_x[rows, :])
        grad = du[rows, :]
        R.dgain_s[...] += jnp.sum(grad * scaled, axis=0, keepdims=True)
        dfirst[rows, :] = dsecond[rows, :] + norm_back(grad, gain_s[...], scaled, factor)

    tiles(S_ROWS, 208, finish_space)
    scatter_frames(dfirst, R.send_a)
    for i in range(6):
        join_core(i)
    ex_df = exchange(3, R.send_a, R.got_first)
    all_start(ex_df)
    dcls_total = sum_rows(1, R.dcls_sum, False)
    service(9)

    def grad_space(n):
        cols = pl.ds(n, 256)
        R.pj_s[pl.ds(n // 64, 4)] = tn(mix_s[:, cols], loww[...]).astype(BF16).reshape(4, 64, width)

    tiles(width, 256, grad_space)
    qkv_grad(dqkv, u_s, R.wt_s, S_ROWS)
    service(10)

    df = R.rows_s
    all_wait(ex_df)
    service(11)
    to_patch_order(R.got_first, df, R.perm)
    scaled, factor = stats(cls_row)
    R.dcls[...] = dcls_second + norm_back(dcls_total(), gain_s[...], scaled, factor)
    low, datt, dmix = R.low_a, R.low_b, R.low_c
    low[:T_ROWS, :] = (df[:T_ROWS, :] * R.kt_col[...]).astype(BF16)
    sent(0, 1, 2, 3)

    def back_fc(n):
        cols = pl.ds(n, 256)
        datt[:T_ROWS, cols] = nt(low[:T_ROWS, :], rows_of(R.fc, n)).astype(BF16)
        R.fc[pl.ds(n // 64, 4)] = tn(att_t[:, cols], low[:T_ROWS, :]).astype(BF16).reshape(4, 64, width)

    tiles(width, 256, back_fc)
    service(12)

    def back_time(n):
        cols = pl.ds(n, 256)
        dmix[:T_ROWS, cols] = nt(datt[:T_ROWS, :], rows_of(R.pj_t, n)).astype(BF16)
        R.pj_t[pl.ds(n // 64, 4)] = tn(mix_t[:, cols], datt[:T_ROWS, :]).astype(BF16).reshape(4, 64, width)

    tiles(width, 256, back_time)
    service(13)
    for n in range(3):
        attention_back(qkv_t, p_t, dmix, dqkv, T_GROUPS, 2 * n, 2 * n + 2)
        service(14 + n)
    qkv_grad(dqkv, u_t, R.dwt_own, T_ROWS)
    service(17)
    qkv_back(dqkv, R.wt_t, du, T_ROWS)
    service(18)
    R.dgain_t[...] = jnp.zeros((1, width), F32)

    def finish_time(r):
        rows = pl.ds(r, 80)
        scaled, factor = stats(patches[rows, :].astype(F32))
        grad = du[rows, :]
        R.dgain_t[...] += jnp.sum(grad * scaled, axis=0, keepdims=True)
        df[rows, :] += norm_back(grad, gain_t[...], scaled, factor)

    tiles(T_ROWS, 80, finish_time)
    store = pltpu.make_async_copy(df.at[pl.ds(0, used)], R.dx, R.lo.at[4])
    store.start()
    for n, gain in enumerate((R.dgain_t, R.dgain_s, R.dgain_m)):
        R.gains[0, n : n + 1, :] = gain[...]
    def gain_part(j):
        peer = ([peer_c, peer_y] + bits)[j]
        return remote(R.gains.at[0], R.gains.at[1 + j], (R.gg_s, R.gg_r), j, peer)

    def gain_steps():
        for j in range(2 + levels):
            gain_part(j).start()
            yield
            gain_part(j).wait()
            R.gains[0] = R.gains[0] + R.gains[1 + j]

    extra[16] = gain_steps()
    service(19)
    finish_units()
    R.gains_out[...] = R.gains[0]
    store.wait()
    store_out.wait()


def widen(*refs):
    half = len(refs) // 2
    for src, dst in zip(refs[:half], refs[half:]):
        dst[...] = src[...].astype(dst.dtype)


def widened(arrays):
    steps = 4
    specs = []
    for x, _ in arrays:
        rows = x.shape[0] // steps if x.shape[0] % (8 * steps) == 0 else x.shape[0]
        last = x.shape[0] // rows - 1
        specs.append(pl.BlockSpec((rows, x.shape[1]), lambda i, last=last: (jnp.minimum(i, last), 0)))
    return pl.pallas_call(
        widen,
        grid=(steps,),
        out_shape=[jax.ShapeDtypeStruct(x.shape, d) for x, d in arrays],
        in_specs=specs,
        out_specs=specs,
        compiler_params=pltpu.CompilerParams(vmem_limit_bytes=60 << 20),
    )(*[x for x, _ in arrays])


def local(
    patches, cls_token, keep_mask, gain_time, qkv_time, proj_time, temporal_fc, gain_space, qkv_space, proj_space,
    gain_mlp, mlp_in, mlp_out, cotangent, cls_cotangent,
):
    _, frames, count, width = patches.shape
    heads_here, hd = qkv_time.shape[1], qkv_time.shape[3]

    def by_patch(x):
        return jnp.transpose(x[0], (1, 0, 2)).reshape(count * frames, width)

    def by_head(w):
        return jnp.transpose(w, (1, 2, 3, 0))

    def blocks(w):
        return w.reshape(-1, 64, width)

    zero = jnp.zeros((3, width), F32)
    rows_in = jnp.concatenate(
        [gain_time[None], gain_space[None], gain_mlp[None], cls_token.astype(F32), cls_cotangent.astype(F32), zero]
    )
    large = dict(
        patches=by_patch(patches), cot=by_patch(cotangent), keep=keep_mask[0], wt_t_in=by_head(qkv_time),
        pj_t_in=proj_time, fc_in=blocks(temporal_fc), wt_s_in=by_head(qkv_space), pj_s_in=proj_space,
        w1_in=blocks(mlp_in), w2_in=blocks(mlp_out),
    )
    small = dict(rows_in=rows_in)
    frame_rows, square, row = (frames, count, width), (width // 64, 64, width), (1, width)
    heads = (heads_here, 3, hd, width)
    t_rows, s_rows, ours = (T_ROWS, width), (S_ROWS, width), (count * frames, width)
    in_hbm = dict(
        out=(ours, BF16), dx=(ours, F32), dw1=(square, BF16), dw2=(square, BF16), dfc=(square, BF16),
        dwt_s=(heads, BF16), dpj_s=(proj_space.shape, BF16), dwt_t=(heads, BF16), dpj_t=(proj_time.shape, BF16),
    )
    in_vmem = dict(ocls=(row, BF16), dcls=(row, F32), gains_out=((8, width), F32))
    levels = lax.axis_size("clip").bit_length() - 1
    vmem = dict(
        wt_t=((3,) + square, BF16), pj_t=(square, BF16), fc=(square, BF16), wt_s=((3,) + square, BF16),
        pj_s=(square, BF16), w1=((4,) + square, BF16), w2=((4,) + square, BF16),
        patches_v=(t_rows, BF16), keep_v=(keep_mask.shape[1:], jnp.int32),
        kt_col=((T_ROWS, 1), F32), ks_row=((2, 1, 256), F32), ks_col=((S_ROWS, 1), F32), once=((S_ROWS, 1), F32),
        bias_t=((4, 112, 128), F32), u_t=(t_rows, BF16), qkv_t=((T_ROWS, 3 * width), BF16),
        p_t=((6, 4, 224, 128), BF16), mix_t=(t_rows, BF16), att_t=(t_rows, BF16),
        rows_x=(s_rows, F32), rows_s=(s_rows, F32), rows_c=(s_rows, F32), rows_a=(s_rows, F32), rows_d=(s_rows, F32),
        low_a=(s_rows, BF16), low_b=(s_rows, BF16), low_c=(s_rows, BF16), low_d=(s_rows, BF16),
        u_s=(s_rows, BF16), qkv_s=((S_ROWS, 3 * width), BF16), mix_s=(s_rows, BF16),
        p_s=((6, 2, 416, 256), BF16), dwt_own=((3,) + square, BF16), dqkv=((S_ROWS, 3 * width), BF16),
        perm=((width // 128, T_ROWS, 128), F32), send_a=(frame_rows, BF16),
        send_b=(frame_rows, BF16), got_first=(frame_rows, BF16), got_cot=(frame_rows, BF16),
        cls_sum=((4, 8, width), F32), dcls_sum=((4, 8, width), F32),
        dgain_t=(row, F32), dgain_s=(row, F32), dgain_m=(row, F32), gains=((3 + levels, 8, width), F32),
        near_a=((6, 2, 3, 64, width), BF16), near_b=((3, 2, 4, 64, width), BF16),
        near_c=((3, 2, width // 64, 64, 256), BF16),
    )
    pairs = dict(wy=14, wx=42, wc=14, wf=14, ex=12, row=6, gg=2 + levels)
    sems = dict(wo=14, exo=4, lo=6, go=15)
    for name, n in pairs.items():
        sems[name + "_s"] = n
        sems[name + "_r"] = n
    sems["gu_s"] = 30
    sems["gu_r"] = sum(arrivals(ROUTES[k], levels, k == 10) for k in range(15))
    flags = dict(free=15 * (levels + 1))
    names = [*large, *small, *in_hbm, *in_vmem, *vmem, *sems, *flags]
    hbm, vm = pl.BlockSpec(memory_space=pl.ANY), pl.BlockSpec(memory_space=pltpu.VMEM)
    output, dx, d_w1, d_w2, d_fc, d_qs, d_ps, d_qt, d_pt, out_cls, cls_grad, gains = pl.pallas_call(
        partial(whole_step, names, frames),
        out_shape=[jax.ShapeDtypeStruct(s, d) for s, d in [*in_hbm.values(), *in_vmem.values()]],
        in_specs=[hbm] * len(large) + [vm] * len(small),
        out_specs=[hbm] * len(in_hbm) + [vm] * len(in_vmem),
        scratch_shapes=[pltpu.VMEM(s, d) for s, d in vmem.values()]
        + [pltpu.SemaphoreType.DMA((n,)) for n in sems.values()]
        + [pltpu.SemaphoreType.REGULAR((n,)) for n in flags.values()],
        compiler_params=pltpu.CompilerParams(collective_id=0, has_side_effects=True, vmem_limit_bytes=60 << 20),
    )(*large.values(), *small.values())

    def by_frame(x):
        return jnp.transpose(x.reshape(count, frames, width), (1, 0, 2))[None]

    def by_width(w):
        return jnp.transpose(w.reshape(heads), (3, 0, 1, 2))

    grads = [(x.reshape(-1, width), F32) for x in (dx, d_w1, d_w2, d_fc, d_qs, d_ps, d_qt, d_pt)]
    output, dx, d_w1, d_w2, d_fc, d_qs, d_ps, d_qt, d_pt = widened([(output, BF16)] + grads)
    return (
        by_frame(output), out_cls, by_frame(dx), cls_grad, gains[0], by_width(d_qt), d_pt.reshape(proj_time.shape), d_fc,
        gains[1], by_width(d_qs), d_ps.reshape(proj_space.shape), gains[2], d_w1, d_w2,
    )


def solution(mesh):
    rows, wide, by_head = P("clip", None, "head", None), P("clip", None), P(None, "head", None, None)
    in_specs = (
        rows, wide, P("clip", None, None), P(), by_head, P("head", None, None), P(), P(), by_head,
        P("head", None, None), P(), P(None, "head"), P("head", None), rows, wide,
    )
    out_specs = (
        rows, wide, rows, wide, P(), by_head, P("head", None, None), P(), P(), by_head,
        P("head", None, None), P(), P(None, "head"), P("head", None),
    )
    return jax.shard_map(local, mesh=mesh, in_specs=in_specs, out_specs=out_specs, check_vma=False)
```

```python
from functools import partial
from types import SimpleNamespace

import jax
import jax.numpy as jnp
from jax import lax
from jax.experimental import pallas as pl
from jax.experimental.pallas import tpu as pltpu
from jax.sharding import PartitionSpec as P

EPSILON = 1e-06
NEGATIVE = -1e30
F32 = jnp.float32
BF16 = jnp.bfloat16


def nn(a, b):
    return lax.dot_general(a, b, (((1,), (0,)), ((), ())), preferred_element_type=F32)


def nt(a, b):
    return lax.dot_general(a, b, (((1,), (1,)), ((), ())), preferred_element_type=F32)


def tn(a, b):
    return lax.dot_general(a, b, (((0,), (0,)), ((), ())), preferred_element_type=F32)


def tiles(total, size, body):
    def step(i, carry):
        body(pl.multiple_of(i * size, size))
        return carry

    lax.fori_loop(0, total // size, step, 0)


def stats(x):
    center = x - jnp.mean(x, axis=-1, keepdims=True)
    factor = lax.rsqrt(jnp.mean(center * center, axis=-1, keepdims=True) + EPSILON)
    return center * factor, factor


def norm_back(grad, gain, scaled, factor):
    weighted = grad * gain
    inner = weighted - jnp.mean(weighted, axis=-1, keepdims=True)
    return factor * (inner - scaled * jnp.mean(weighted * scaled, axis=-1, keepdims=True))


def pair_masks():
    lane = lax.broadcasted_iota(jnp.int32, (1, 128), 1)
    return (lane < 64).astype(F32).astype(BF16), (lane >= 64).astype(F32).astype(BF16)


def stacked(x):
    low, high = pair_masks()
    return jnp.concatenate([x * low, x * high], axis=0)


def unstacked(x):
    rows = x.shape[0] // 2
    lane = lax.broadcasted_iota(jnp.int32, (1, 128), 1)
    return jnp.where(lane < 64, x[:rows], x[rows:])


def norm_rows(x_ref, gain_ref, u_ref, total, chunk):
    def body(r):
        rows = pl.ds(r, chunk)
        scaled, _ = stats(x_ref[rows, :])
        u_ref[rows, :] = (scaled * gain_ref[...]).astype(BF16)

    tiles(total, chunk, body)


def project_qkv(u_ref, wt_ref, qkv_ref, rows, first, last):
    width = u_ref.shape[1]
    size = (last - first) * 64

    def body(t, carry):
        scale = jnp.where(t == 0, 0.125, 1.0)
        out = nt(u_ref[:rows, :], wt_ref[t, first:last].reshape(size, width)) * scale
        qkv_ref[:rows, pl.ds(pl.multiple_of(t * width + first * 64, 128), size)] = out.astype(BF16)
        return carry

    lax.fori_loop(0, 3, body, 0)


def columns(ref, cols):
    part = ref[:, :, cols]
    return part.reshape(part.shape[0] * part.shape[1], part.shape[2])


def rows_of(ref, n):
    part = ref[pl.ds(n // 64, 4)]
    return part.reshape(256, part.shape[2])


def qkv_back(dqkv_ref, wt_ref, du_ref, rows):
    width = du_ref.shape[1]

    def back(n):
        cols = pl.ds(n, 256)
        total = nn(dqkv_ref[:rows, :width], columns(wt_ref.at[0], cols))
        total += nn(dqkv_ref[:rows, width : 2 * width], columns(wt_ref.at[1], cols))
        total += nn(dqkv_ref[:rows, 2 * width :], columns(wt_ref.at[2], cols))
        du_ref[:rows, cols] = total

    tiles(width, 256, back)


def qkv_grad(dqkv_ref, u_ref, wt_ref, rows):
    width = u_ref.shape[1]

    def grad(i, carry):
        cols = pl.ds(pl.multiple_of(i * 256, 256), 256)
        out = tn(dqkv_ref[:rows, cols], u_ref[:rows, :]).astype(BF16)
        wt_ref[i // 3, pl.ds((i % 3) * 4, 4)] = out.reshape(4, 64, width)
        return carry

    lax.fori_loop(0, 9, grad, 0)


def softmax(scores):
    highest = jnp.max(scores, axis=-1, keepdims=True)
    weights = jnp.exp(scores - highest)
    return weights * (1.0 / jnp.sum(weights, axis=-1, keepdims=True))


def attention(qkv_ref, p_ref, mix_ref, groups, bias_of, first, last):
    width = mix_ref.shape[1]

    def body(hp, carry):
        qc = pl.ds(pl.multiple_of(hp * 128, 128), 128)
        kc = pl.ds(pl.multiple_of(width + hp * 128, 128), 128)
        vc = pl.ds(pl.multiple_of(2 * width + hp * 128, 128), 128)
        all_rows = [pl.ds(start, size) for start, size in groups]
        scores = [nt(stacked(qkv_ref[rows, qc]), qkv_ref[rows, kc]) for rows in all_rows]
        probs = [softmax(scores[g] + bias_of(g, size)).astype(BF16) for g, (_, size) in enumerate(groups)]
        mixes = [unstacked(nn(prob, qkv_ref[rows, vc])).astype(BF16) for prob, rows in zip(probs, all_rows)]
        for g, (_, size) in enumerate(groups):
            p_ref[hp, g, : 2 * size, :size] = probs[g]
            mix_ref[all_rows[g], qc] = mixes[g]
        return carry

    lax.fori_loop(first, last, body, 0)


def attention_back(qkv_ref, p_ref, dmix_ref, dqkv_ref, groups, first, last):
    width = dmix_ref.shape[1]

    def body(hp, carry):
        qc = pl.ds(pl.multiple_of(hp * 128, 128), 128)
        kc = pl.ds(pl.multiple_of(width + hp * 128, 128), 128)
        vc = pl.ds(pl.multiple_of(2 * width + hp * 128, 128), 128)
        all_rows = [pl.ds(start, size) for start, size in groups]
        ups = [stacked(dmix_ref[rows, qc]) for rows in all_rows]
        probs = [p_ref[hp, g, : 2 * size, :size] for g, (_, size) in enumerate(groups)]
        dprobs = [nt(up, qkv_ref[rows, vc]) for up, rows in zip(ups, all_rows)]
        dvs = [tn(prob, up).astype(BF16) for prob, up in zip(probs, ups)]
        dscores = []
        for prob, dprob in zip(probs, dprobs):
            wide = prob.astype(F32)
            delta = jnp.sum(wide * dprob, axis=-1, keepdims=True)
            dscores.append((wide * (dprob - delta)).astype(BF16))
        dqs = [(unstacked(nn(ds, qkv_ref[rows, kc])) * 0.125).astype(BF16) for ds, rows in zip(dscores, all_rows)]
        dks = [tn(ds, stacked(qkv_ref[rows, qc])).astype(BF16) for ds, rows in zip(dscores, all_rows)]
        for g, rows in enumerate(all_rows):
            dqkv_ref[rows, qc] = dqs[g]
            dqkv_ref[rows, kc] = dks[g]
            dqkv_ref[rows, vc] = dvs[g]
        return carry

    lax.fori_loop(first, last, body, 0)


T_ROWS = 400
T_GROUPS = ((0, 96), (96, 96), (192, 96), (288, 112))
SEG = 208
S_ROWS = 416
S_GROUPS = ((0, 208), (208, 208))


def time_bias(kcol, size):
    row = lax.broadcasted_iota(jnp.int32, (size, size), 0)
    col = lax.broadcasted_iota(jnp.int32, (size, size), 1)
    kept = jnp.sum(jnp.where(row == col, kcol, 0.0), axis=0, keepdims=True)
    ok = ((row // 8) == (col // 8)) & ((kept > 0.0) | (row == col))
    return jnp.where(ok, 0.0, NEGATIVE)


def patch_keep(keep_ref, head, count, frames):
    total = keep_ref.shape[1]
    row = lax.broadcasted_iota(jnp.int32, (T_ROWS, total), 0)
    col = lax.broadcasted_iota(jnp.int32, (T_ROWS, total), 1)
    pick = ((row // frames + head * count == col) & (row < frames * count)).astype(F32).astype(BF16)
    by_frame = nt(pick, keep_ref[...].astype(F32).astype(BF16))
    row = lax.broadcasted_iota(jnp.int32, (T_ROWS, frames), 0)
    col = lax.broadcasted_iota(jnp.int32, (T_ROWS, frames), 1)
    return jnp.sum(jnp.where(row % frames == col, by_frame, 0.0), axis=1, keepdims=True)


def space_bias(krow_ref, g):
    return (krow_ref[g, :, :SEG] - 1.0) * (-NEGATIVE)


def to_patch_order(src_ref, dst_ref, perm_ref):
    frames, count, width = src_ref.shape
    used = frames * count
    for j in range(width // 128):
        for f in range(frames):
            perm_ref[j, pl.ds(f, count, stride=frames), :] = src_ref[f, :, j * 128 : (j + 1) * 128].astype(F32)
        dst_ref[:used, j * 128 : (j + 1) * 128] = perm_ref[j, :used, :]
    dst_ref[used:T_ROWS, :] = jnp.zeros((T_ROWS - used, width), F32)


def to_frame_order(src_ref, dst_ref, perm_ref):
    frames, count, width = dst_ref.shape
    for j in range(width // 128):
        used = frames * count
        perm_ref[j, :used, :] = src_ref[:used, j * 128 : (j + 1) * 128].astype(F32)
        for f in range(frames):
            out = perm_ref[j, pl.ds(f, count, stride=frames), :]
            dst_ref[f, :, j * 128 : (j + 1) * 128] = out.astype(dst_ref.dtype)


def gather_frames(got_ref, cls_row, out_ref):
    sources, count = got_ref.shape[0] // 2, got_ref.shape[1]
    for f in range(2):
        base = f * SEG
        for s in range(sources):
            out_ref[base + s * count : base + (s + 1) * count, :] = got_ref[2 * s + f].astype(F32)
        at = base + sources * count
        out_ref[at : at + 1, :] = cls_row[f]
        out_ref[at + 1 : base + SEG, :] = jnp.zeros((SEG - 1 - sources * count, out_ref.shape[1]), F32)


def scatter_frames(x_ref, send_ref):
    sources, count = send_ref.shape[0] // 2, send_ref.shape[1]
    for f in range(2):
        for s in range(sources):
            at = f * SEG + s * count
            send_ref[2 * s + f] = x_ref[at : at + count, :].astype(send_ref.dtype)


def cls_attention(qkv_ref, krow_ref, at, width):
    lane = lax.broadcasted_iota(jnp.int32, (16, width), 1) // 64
    own = (lane == lax.broadcasted_iota(jnp.int32, (16, width), 0)).astype(F32)
    total = jnp.zeros((1, width), F32)
    for f in range(2):
        q = qkv_ref[f * SEG + at : f * SEG + at + 1, :width].astype(F32)
        k = qkv_ref[f * SEG : (f + 1) * SEG, width : 2 * width]
        v = qkv_ref[f * SEG : (f + 1) * SEG, 2 * width :]
        prob = softmax(nt((own * q).astype(BF16), k) + space_bias(krow_ref, f))
        total += jnp.sum(own * nn(prob.astype(BF16), v), axis=0, keepdims=True)
    return total


def blocks_swapped(x, distance):
    width = x.shape[1]
    quarter = width // 4
    order = [i ^ distance for i in range(4)]
    return jnp.concatenate([x[:, i * quarter : (i + 1) * quarter] for i in order], axis=1)


def set_row(ref, base, at, row, dtype):
    start = base + at // 16 * 16
    pick = lax.broadcasted_iota(jnp.int32, (16, 1), 0) == at % 16
    kept = ref[start : start + 16, :].astype(F32)
    ref[start : start + 16, :] = jnp.where(pick, jnp.broadcast_to(row, kept.shape), kept).astype(dtype)


MESH = pl.DeviceIdType.MESH

ROUTES = (0, 0, 1, 0, 2, 1, 1, 0, 0, 1, 0, 0, 0, 0, 0)
ORDER = (
    (0, 1),
    (2, 3, 0, 1),
    (4, 5, 2, 3),
    (0, 4, 5),
    (),
    (),
    (1,),
    (),
    (0, 4),
    (2, 3),
    (0, 5),
    (6, 7, 8, 9, 1, 4),
    (10, 0, 3, 2, 6, 7, 1, 8, 9, 5, 10, 0, 4, 15),
    (11, 3),
    (2, 6, 1, 5, 11),
    (3, 9, 7),
    (0, 1, 2),
    (12, 13, 14, 3, 4, 5, 7, 8, 2),
    (1, 6, 4, 3, 12, 5, 13, 7, 8, 14, 10, 6, 11),
    (9, 8, 7, 2, 16, 6, 10, 12, 4, 9, 5, 11, 16, 8, 7, 15, 13, 6, 12, 10, 9, 16, 7, 11, 14, 8, 13, 12, 10, 16,
     6, 9, 11, 14, 13, 12, 8, 16, 10, 11, 9, 14, 13, 10, 12, 16, 14, 11, 13, 12, 14, 10, 13, 16, 10, 14),
)


def arrivals(route, levels, everywhere):
    return 2 + (3, 4, 5)[route] + levels - 2 + 2 + (3 if everywhere else 0)


def whole_step(names, frames, *refs):
    R = SimpleNamespace(**dict(zip(names, refs)))
    clip, head = lax.axis_index("clip"), lax.axis_index("head")
    digit = (clip % 2, clip // 2 % 2, clip // 4 % 2)
    side, turn = digit[0], digit[1]
    width = R.wt_t.shape[3]
    count = R.patches.shape[0] // frames
    at = 4 * count
    peer_c, peer_y, peer_d = (clip, head ^ 1), (clip, head ^ 2), (clip, head ^ 3)
    levels = lax.axis_size("clip").bit_length() - 1
    bits = [(clip ^ (1 << j), head) for j in range(levels)]

    def part(ref, q, n):
        return ref.at[:, pl.ds(q * 16, n * 16), :]

    def hidden_tile(w1, w2, i, q, n):
        t = (i - 8) // 2
        if i % 2:
            return w1.at[:, pl.ds(q * 16, n * 16), pl.ds(t * 256, 256)]
        return part(w2.at[pl.ds(t * 4, 4)], q, n)

    def slot(i, s, q=0, n=4):
        if i >= 8:
            return hidden_tile(R.w1.at[s], R.w2.at[s], i, q, n)
        wt, pj = (R.wt_t, R.pj_t) if i < 4 else (R.wt_s, R.pj_s)
        if i % 4 == 3:
            return part(pj.at[pl.ds(s * 3, 3)], q, n)
        return part(wt.at[:, s * 3 + i % 4], q, n)

    def source(i, q=0, n=4):
        if i >= 8:
            return hidden_tile(R.w1_in, R.w2_in, i, q, n)
        wt, pj = (R.wt_t_in, R.pj_t_in) if i < 4 else (R.wt_s_in, R.pj_s_in)
        return part(pj if i % 4 == 3 else wt.at[i % 4], q, n)

    def remote(src, dst, sems, index, peer):
        return pltpu.make_async_remote_copy(
            src_ref=src, dst_ref=dst, send_sem=sems[0].at[index], recv_sem=sems[1].at[index],
            device_id=peer, device_id_type=MESH,
        )

    mine = side + 2 * turn

    def y_copy(i):
        return remote(source(i, mine, 1), slot(i, 2, mine, 1), (R.wy_s, R.wy_r), i, peer_y)

    def clip_copies(i):
        quarter = slot(i, 2, mine, 1)
        near = (bits[0], bits[1], (clip ^ 3, head))
        return [remote(quarter, quarter, (R.wx_s, R.wx_r), 3 * i + n, peer) for n, peer in enumerate(near)]

    def c_copy(i):
        return remote(source(i), slot(i, 1), (R.wc_s, R.wc_r), i, peer_c)

    def f_copy(i):
        return remote(slot(i, 2), slot(i, 3), (R.wf_s, R.wf_r), i, peer_c)

    def own_copy(i):
        return pltpu.make_async_copy(source(i), slot(i, 0), R.wo.at[i])

    def pass_near(*pieces):
        for i in pieces:
            y_copy(i).wait_recv()
            for copy in clip_copies(i):
                copy.start()

    def pass_far(*pieces):
        for i in pieces:
            for copy in clip_copies(i):
                copy.wait_recv()
            f_copy(i).start()

    def ready_near(*pieces):
        for i in pieces:
            own_copy(i).wait()
            c_copy(i).wait_recv()

    def ready_far(*pieces):
        for i in pieces:
            f_copy(i).wait_recv()

    def sent(*pieces):
        for i in pieces:
            y_copy(i).wait_send()
            c_copy(i).wait_send()
            f_copy(i).wait_send()
            for copy in clip_copies(i):
                copy.wait_send()

    def exchange(k, src, dst):
        here = pl.ds(2 * head, 2)
        copies = []
        for r, peer in ((2, peer_y), (3, peer_d), (1, peer_c)):
            there = pl.ds(2 * (head ^ r), 2)
            copies.append(remote(src.at[there], dst.at[here], (R.ex_s, R.ex_r), 3 * k + r - 1, peer))
        copies.append(pltpu.make_async_copy(src.at[here], dst.at[here], R.exo.at[k]))
        return copies

    def all_start(copies):
        for copy in copies:
            copy.start()

    def all_wait(copies):
        for copy in copies:
            copy.wait()

    def sum_rows(k, buf, swapped):
        copies = [
            remote(buf.at[0], buf.at[r], (R.row_s, R.row_r), 3 * k + r - 1, peer)
            for r, peer in ((2, peer_y), (3, peer_d), (1, peer_c))
        ]
        all_start(copies)

        def finish():
            all_wait(copies)
            terms = [buf[r] for r in range(4)]
            if swapped:
                terms = [terms[0]] + [blocks_swapped(terms[r], r) for r in (1, 2, 3)]
            total = (terms[0] + terms[1]) + (terms[2] + terms[3])
            return total[0:1, :]

        return finish

    def unit(i):
        if i < 6:
            n = i // 2
            if i % 2:
                return lambda s, q=0, k=4: R.w1.at[s, :, pl.ds(q * 16, k * 16), pl.ds(n * 256, 256)]
            return lambda s, q=0, k=4: part(R.w2.at[s, pl.ds(n * 4, 4)], q, k)
        if i == 10:
            return lambda s, q=0, k=4: part(R.fc.at[pl.ds((head ^ s) * 3, 3)], q, k)
        wt, pj = (R.wt_s, R.pj_s) if i < 10 else (R.dwt_own, R.pj_t)
        n = i - 6 if i < 10 else i - 11
        if n == 0:
            return lambda s, q=0, k=4: part(pj.at[pl.ds(s * 3, 3)], q, k)
        return lambda s, q=0, k=4: part(wt.at[:, s * 3 + n - 1], q, k)

    def result(i, q, k):
        if i < 6:
            n = i // 2
            if i % 2:
                return R.dw1.at[:, pl.ds(q * 16, k * 16), pl.ds(n * 256, 256)]
            return part(R.dw2.at[pl.ds(n * 4, 4)], q, k)
        if i == 10:
            return part(R.dfc.at[pl.ds(head * 3, 3)], q, k)
        wt, pj = (R.dwt_s, R.dpj_s) if i < 10 else (R.dwt_t, R.dpj_t)
        n = i - 6 if i < 10 else i - 11
        return part(pj if n == 0 else wt.at[n - 1], q, k)

    def near_slot(i, k):
        if i < 6:
            return (R.near_c if i % 2 else R.near_b).at[i // 2, k]
        if i < 9:
            return R.near_b.at[i - 6, k, pl.ds(0, 3)]
        return R.near_a.at[i - 9, k]

    def add(dst, src):
        def body(r, carry):
            dst[r] = dst[r] + src[r]
            return carry

        lax.fori_loop(0, dst.shape[0], body, 0)

    def steps_of(i):
        u, route = unit(i), ROUTES[i]
        a, b = (1, 2) if route == 2 else (0, 1)
        half = 2 * digit[a]
        quarter = half + digit[b]
        counts = [sum(arrivals(ROUTES[k], levels, k == 10) for k in range(i)), 0]

        def copy(src, dst, peer):
            counts[0] += 1
            return pltpu.make_async_remote_copy(
                src_ref=src, dst_ref=dst, send_sem=R.gu_s.at[i * 2 + counts[0] % 2], recv_sem=R.gu_r.at[counts[0] - 1],
                device_id=peer, device_id_type=MESH,
            )

        def land(k):
            at_q = counts[1]
            counts[1] += k
            s, q = ((1, at_q) if at_q < 4 else (3, at_q - 4) if at_q < 8 else (2, at_q - 8))
            return u(s, q, k), (s, q, k)

        steps = [([copy(u(1), near_slot(i, 0), peer_c), copy(u(3), near_slot(i, 1), peer_c)],
                  [(u(2), near_slot(i, 1)), (u(0), near_slot(i, 0))], None)]
        peers = []
        kept, joined = (0, 4), False
        whole_bits = [j for j in range(levels) if j not in (a, b)]
        order = ((-1, a, b), (a, -1, b), (a, b, -1))[route]
        for bit in list(order) + whole_bits:
            copies, sums = [], []
            if bit == -1:
                spot, (s, q, k) = land(kept[1])
                copies.append(copy(u(2, *kept), u(s ^ 2, q, k) if i == 10 else spot, peer_y))
                sums.append((u(0, *kept), spot))
                joined = True
                peers.append(peer_y)
            else:
                if bit == a:
                    kept, other = (half, 2), (2 - half, 2)
                elif bit == b:
                    kept, other = (quarter, 1), (half + 1 - digit[b], 1)
                else:
                    other = kept
                for s in (0,) if joined else (0, 2):
                    spot, _ = land(other[1])
                    copies.append(copy(u(s, *other), spot, bits[bit]))
                    sums.append((u(s, *kept), spot))
                peers.append(bits[bit])
            steps.append((copies, sums, len(peers) - 1))
        mine_q, there_q, rows = u(0, quarter, 1), result(i, quarter, 1), result(i, half, 2)
        steps.append(([copy(mine_q, there_q, bits[b]), pltpu.make_async_copy(mine_q, there_q, R.go.at[i])], [], None))
        steps.append(([copy(rows, rows, bits[a])], [], None))
        if i == 10:
            ours, far = R.dfc.at[pl.ds(head * 3, 3)], R.dfc.at[pl.ds((head ^ 2) * 3, 3)]
            steps.append(([copy(ours, ours, peer_y), copy(ours, ours, peer_c)], [], None))
            steps.append(([copy(far, far, peer_c)], [], None))
        return steps, peers

    units = [None] * 15
    stage = [0] * 15

    def tell(i, first, last):
        peers = units[i][1]
        for k in range(first, min(last, len(peers))):
            pl.semaphore_signal(R.free.at[i * (levels + 1) + k], inc=1, device_id=peers[k], device_id_type=MESH)

    def land_step(i):
        steps, _ = units[i]
        copies, sums, _ = steps[stage[i] - 1]
        all_wait(copies)
        if stage[i] == 1:
            tell(i, 0, 4)
        for dst, src in sums:
            add(dst, src)
        if stage[i] == 4:
            tell(i, 4, 8)

    landed = [0] * 15

    def advance(i):
        if units[i] is None:
            units[i] = steps_of(i)
        steps, _ = units[i]
        if stage[i] > landed[i]:
            land_step(i)
            landed[i] = stage[i]
        if stage[i] < len(steps):
            copies, _, credit = steps[stage[i]]
            if credit is not None:
                pl.semaphore_wait(R.free.at[i * (levels + 1) + credit], 1)
            all_start(copies)
        stage[i] += 1

    def join_core(i):
        if stage[i] == 1 and landed[i] == 0:
            land_step(i)
            landed[i] = 1

    extra = {}

    def service(k):
        for i in ORDER[k]:
            if i < 15:
                advance(i)
            else:
                next(extra[i], None)

    def finish_units():
        while any(stage[i] < 1 + len(units[i][0]) for i in range(15)):
            for i in reversed(range(15)):
                done = [stage[j] >= 1 + len(units[j][0]) for j in (i, i - 1)]
                if not done[0] and (i == 0 or done[1] or stage[i] < stage[i - 1]):
                    advance(i)
        for steps in extra.values():
            for _ in steps:
                pass

    barrier = pltpu.get_barrier_semaphore()
    for peer in [peer_c, peer_y, peer_d, (clip ^ 3, head)] + bits:
        pl.semaphore_signal(barrier, inc=1, device_id=peer, device_id_type=MESH)
    pl.semaphore_wait(barrier, 4 + levels)

    loads = (
        (R.patches, R.patches_v.at[pl.ds(0, frames * count)]), (R.keep, R.keep_v), (R.cot, R.low_d.at[pl.ds(0, frames * count)]), (R.fc_in, R.fc),
    )
    loads = [pltpu.make_async_copy(src, dst, R.lo.at[i]) for i, (src, dst) in enumerate(loads)]
    for i in range(3):
        loads[i].start()
    for i in range(12):
        y_copy(i).start()
    for i in range(14):
        own_copy(i).start()
        c_copy(i).start()
    loads[3].start()

    rows_x, first = R.rows_x, R.rows_s
    qkv_t, p_t, mix_t, att_t, u_t = R.qkv_t, R.p_t, R.mix_t, R.att_t, R.u_t
    patches, gains = R.patches_v, R.rows_in
    for n, row in enumerate((R.gain_t, R.gain_s, R.gain_m)):
        gains[n : n + 1, :] = row[...].reshape(1, width)
    gains[3:4, :] = R.cls[...].astype(F32)
    gains[4:5, :] = R.ccot[...].astype(F32)
    gain_t, gain_s, gain_m = gains.at[0:1], gains.at[1:2], gains.at[2:3]
    used = frames * count
    loads[0].wait()
    patches[used:, :] = jnp.zeros((T_ROWS - used, width), BF16)

    def norm_time(r):
        rows = pl.ds(r, 80)
        scaled, _ = stats(patches[rows, :].astype(F32))
        u_t[rows, :] = (scaled * gain_t[...]).astype(BF16)

    tiles(T_ROWS, 80, norm_time)
    pass_near(0)
    loads[1].wait()
    keep_col = patch_keep(R.keep_v, head, count, frames)
    R.kt_col[...] = keep_col
    for g, (start, size) in enumerate(T_GROUPS):
        R.bias_t[g, :size, :size] = time_bias(keep_col[start : start + size], size)
    R.ks_row[...] = jnp.zeros_like(R.ks_row)
    lane = lax.broadcasted_iota(jnp.int32, (1, 256), 1)
    row = lax.broadcasted_iota(jnp.int32, (SEG, SEG), 0)
    col = lax.broadcasted_iota(jnp.int32, (SEG, SEG), 1)
    for f in range(2):
        R.ks_row[f, :, :at] = R.keep_v[pl.ds(2 * head + f, 1), :].astype(F32)
        open_row = jnp.where(lane == at, 1.0, R.ks_row[f])
        R.ks_row[f] = open_row
        counted = (row == col) if f == 0 else (row == col) & (col != at)
        R.ks_col[f * SEG : (f + 1) * SEG, :] = jnp.sum(jnp.where(counted, open_row[:, :SEG], 0.0), axis=1, keepdims=True)
    row = lax.broadcasted_iota(jnp.int32, (S_ROWS, 1), 0)
    R.once[...] = jnp.where((row == at) & (head != 0), 0.0, 1.0)
    loads[2].wait()
    to_frame_order(R.low_d, R.send_b, R.perm)
    ex_cot = exchange(1, R.send_b, R.got_cot)
    pass_near(1, 2, 3)

    def time_bias_of(g, size):
        bias = R.bias_t[g, :size, :size]
        return jnp.concatenate([bias, bias], axis=0)

    ready_near(0, 1, 2, 3)
    project_qkv(u_t, R.wt_t, qkv_t, T_ROWS, 0, 6)
    attention(qkv_t, p_t, mix_t, T_GROUPS, time_bias_of, 0, 3)
    pass_near(4, 5, 6, 7)
    pass_far(0, 1, 2)
    ready_far(0, 1, 2)
    pass_far(3)
    pass_near(8, 9)
    project_qkv(u_t, R.wt_t, qkv_t, T_ROWS, 6, 12)
    attention(qkv_t, p_t, mix_t, T_GROUPS, time_bias_of, 3, 6)
    pass_near(10, 11)
    ready_far(3)
    loads[3].wait()

    def project(n):
        cols = pl.ds(n, 256)
        att_t[:, cols] = nn(mix_t[...], columns(R.pj_t, cols)).astype(BF16)

    tiles(width, 256, project)

    def branch(n):
        cols = pl.ds(n, 256)
        first[:T_ROWS, cols] = patches[:, cols].astype(F32) + R.kt_col[...] * nn(att_t[...], columns(R.fc, cols))

    tiles(width, 256, branch)
    to_frame_order(first, R.send_a, R.perm)
    ex_first = exchange(0, R.send_a, R.got_first)
    all_start(ex_first)
    for i in (12, 13):
        y_copy(i).start()
    all_start(ex_cot)
    pass_far(4, 5, 6, 7)

    qkv_s, p_s, mix_s, u_s = R.qkv_s, R.p_s, R.mix_s, R.u_s
    all_wait(ex_first)
    cls_row = gains[3:4, :]
    second, cot = R.rows_s, R.rows_c
    gather_frames(R.got_first, (cls_row, cls_row), rows_x)
    norm_rows(rows_x, gain_s, u_s, S_ROWS, 208)
    ready_near(4, 5, 6, 7)
    ready_far(4, 5, 6, 7)
    project_qkv(u_s, R.wt_s, qkv_s, S_ROWS, 0, 12)
    pass_near(12, 13)
    all_wait(ex_cot)
    gather_frames(R.got_cot, (gains[4:5, :], jnp.zeros((1, width), F32)), cot)
    cls_part = cls_attention(qkv_s, R.ks_row, at, width)
    R.cls_sum[0] = jnp.broadcast_to(cls_part, (8, width))
    cls_total = sum_rows(0, R.cls_sum, True)
    attention(qkv_s, p_s, mix_s, S_GROUPS, lambda g, size: space_bias(R.ks_row, g), 0, 6)
    set_row(mix_s, 0, at, cls_total() * (1.0 / frames), BF16)
    set_row(mix_s, SEG, at, jnp.zeros((1, width), F32), BF16)
    pass_far(8, 9)

    def project_space(n):
        cols = pl.ds(n, 256)
        second[:, cols] = rows_x[:, cols] + R.ks_col[...] * nn(mix_s[...], columns(R.pj_s, cols))

    tiles(width, 256, project_space)

    u, uw, dz, dzw = R.low_a, R.low_b, R.low_c, R.low_d
    acc, du = R.rows_a, R.rows_d
    kcol, once = R.ks_col, R.once

    def prepare(r):
        rows = pl.ds(r, 208)
        scaled, _ = stats(second[rows, :])
        low = (scaled * gain_m[...]).astype(BF16)
        u[rows, :] = low
        uw[rows, :] = (low.astype(F32) * once[rows, :]).astype(BF16)
        grad = cot[rows, :] * kcol[rows, :]
        dz[rows, :] = grad.astype(BF16)
        dzw[rows, :] = (grad * once[rows, :]).astype(BF16)

    tiles(S_ROWS, 208, prepare)
    acc[...] = jnp.zeros_like(acc)
    du[...] = jnp.zeros_like(du)
    w1_ref, w2_ref = R.w1, R.w2
    def hidden(s, n):
        cols = pl.ds(n * 256, 256)
        w1 = columns(w1_ref.at[s], cols)
        w2 = rows_of(w2_ref.at[s], n * 256)
        hid = nn(u[...], w1)
        phi = 0.5 + 0.5 * lax.erf(hid * 0.7071067811865476)
        act = (hid * phi).astype(BF16)
        slope = phi + hid * (0.3989422804014327 * jnp.exp(hid * hid * -0.5))
        acc[...] += nn(act, w2)
        dhid = (nt(dz[...], w2) * slope).astype(BF16)
        du[...] += nt(dhid, w1)
        w2_ref[s, n * 4 : n * 4 + 4] = tn(act, dzw[...]).astype(BF16).reshape(4, 64, width)
        w1_ref[s, :, :, cols] = tn(uw[...], dhid).astype(BF16).reshape(width // 64, 64, 256)

    for n in range(width // 256):
        if n:
            pass_far(8 + 2 * n, 9 + 2 * n)
        ready_near(8 + 2 * n, 9 + 2 * n)
        ready_far(8 + 2 * n, 9 + 2 * n)
        sent(8 + 2 * n, 9 + 2 * n)

        def by_slot(s, carry, n=n):
            hidden(s, n)
            return carry

        lax.fori_loop(0, 4, by_slot, 0)
        service(n)
    R.dgain_m[...] = jnp.zeros((1, width), F32)

    def finish_mlp(r):
        rows = pl.ds(r, 208)
        x = second[rows, :]
        scaled, factor = stats(x)
        acc[rows, :] = x + kcol[rows, :] * acc[rows, :]
        grad = du[rows, :]
        R.dgain_m[...] += jnp.sum(grad * scaled * once[rows, :], axis=0, keepdims=True)
        cot[rows, :] += norm_back(grad, gain_m[...], scaled, factor)

    tiles(S_ROWS, 208, finish_mlp)
    R.ocls[...] = acc[at : at + 1, :].astype(BF16)
    scatter_frames(acc, R.send_b)
    ex_out = exchange(2, R.send_b, R.got_cot)

    def out_steps():
        all_start(ex_out)
        yield
        all_wait(ex_out)
        to_patch_order(R.got_cot, rows_x, R.perm)
        R.low_d[:T_ROWS, :] = rows_x[:T_ROWS, :].astype(BF16)
        store_out.start()

    used = frames * count
    store_out = pltpu.make_async_copy(R.low_d.at[pl.ds(0, used)], R.out, R.lo.at[5])
    extra[15] = out_steps()
    service(3)

    dsecond = cot
    low, loww, dmix, dqkv = R.low_a, R.low_b, R.low_c, R.dqkv
    low[...] = (dsecond[...] * kcol[...]).astype(BF16)
    loww[...] = (dsecond[...] * (kcol[...] * once[...])).astype(BF16)
    dcls_second = dsecond[at : at + 1, :]
    set_row(low, SEG, at, dcls_second, BF16)
    sent(4, 5, 6, 7)

    def back_space(n):
        cols = pl.ds(n, 256)
        dmix[:, cols] = nt(low[...], rows_of(R.pj_s, n)).astype(BF16)

    tiles(width, 256, back_space)
    service(4)
    dcls_mix = dmix[SEG - 16 : SEG, :].astype(F32)[at - SEG + 16 : at - SEG + 17, :] * (1.0 / frames)
    set_row(dmix, 0, at, dcls_mix, BF16)
    set_row(dmix, SEG, at, dcls_mix, BF16)
    for n in range(3):
        attention_back(qkv_s, p_s, dmix, dqkv, S_GROUPS, 2 * n, 2 * n + 2)
        service(5 + n)
    qkv_back(dqkv, R.wt_s, du, S_ROWS)
    service(8)
    R.dcls_sum[0] = jnp.broadcast_to(du[at : at + 1, :] + du[SEG + at : SEG + at + 1, :], (8, width))
    R.dgain_s[...] = jnp.zeros((1, width), F32)
    dfirst = R.rows_a

    def finish_space(r):
        rows = pl.ds(r, 208)
        scaled, factor = stats(rows_x[rows, :])
        grad = du[rows, :]
        R.dgain_s[...] += jnp.sum(grad * scaled, axis=0, keepdims=True)
        dfirst[rows, :] = dsecond[rows, :] + norm_back(grad, gain_s[...], scaled, factor)

    tiles(S_ROWS, 208, finish_space)
    scatter_frames(dfirst, R.send_a)
    for i in range(6):
        join_core(i)
    ex_df = exchange(3, R.send_a, R.got_first)
    all_start(ex_df)
    dcls_total = sum_rows(1, R.dcls_sum, False)
    service(9)

    def grad_space(n):
        cols = pl.ds(n, 256)
        R.pj_s[pl.ds(n // 64, 4)] = tn(mix_s[:, cols], loww[...]).astype(BF16).reshape(4, 64, width)

    tiles(width, 256, grad_space)
    qkv_grad(dqkv, u_s, R.wt_s, S_ROWS)
    service(10)

    df = R.rows_s
    all_wait(ex_df)
    service(11)
    to_patch_order(R.got_first, df, R.perm)
    scaled, factor = stats(cls_row)
    R.dcls[...] = dcls_second + norm_back(dcls_total(), gain_s[...], scaled, factor)
    low, datt, dmix = R.low_a, R.low_b, R.low_c
    low[:T_ROWS, :] = (df[:T_ROWS, :] * R.kt_col[...]).astype(BF16)
    sent(0, 1, 2, 3)

    def back_fc(n):
        cols = pl.ds(n, 256)
        datt[:T_ROWS, cols] = nt(low[:T_ROWS, :], rows_of(R.fc, n)).astype(BF16)
        R.fc[pl.ds(n // 64, 4)] = tn(att_t[:, cols], low[:T_ROWS, :]).astype(BF16).reshape(4, 64, width)

    tiles(width, 256, back_fc)
    service(12)

    def back_time(n):
        cols = pl.ds(n, 256)
        dmix[:T_ROWS, cols] = nt(datt[:T_ROWS, :], rows_of(R.pj_t, n)).astype(BF16)
        R.pj_t[pl.ds(n // 64, 4)] = tn(mix_t[:, cols], datt[:T_ROWS, :]).astype(BF16).reshape(4, 64, width)

    tiles(width, 256, back_time)
    service(13)
    for n in range(3):
        attention_back(qkv_t, p_t, dmix, dqkv, T_GROUPS, 2 * n, 2 * n + 2)
        service(14 + n)
    qkv_grad(dqkv, u_t, R.dwt_own, T_ROWS)
    service(17)
    qkv_back(dqkv, R.wt_t, du, T_ROWS)
    service(18)
    R.dgain_t[...] = jnp.zeros((1, width), F32)

    def finish_time(r):
        rows = pl.ds(r, 80)
        scaled, factor = stats(patches[rows, :].astype(F32))
        grad = du[rows, :]
        R.dgain_t[...] += jnp.sum(grad * scaled, axis=0, keepdims=True)
        df[rows, :] += norm_back(grad, gain_t[...], scaled, factor)

    tiles(T_ROWS, 80, finish_time)
    store = pltpu.make_async_copy(df.at[pl.ds(0, used)], R.dx, R.lo.at[4])
    store.start()
    for n, gain in enumerate((R.dgain_t, R.dgain_s, R.dgain_m)):
        R.gains[0, n : n + 1, :] = gain[...]
    def gain_part(j):
        peer = ([peer_c, peer_y] + bits)[j]
        return remote(R.gains.at[0], R.gains.at[1 + j], (R.gg_s, R.gg_r), j, peer)

    def gain_steps():
        for j in range(2 + levels):
            gain_part(j).start()
            yield
            gain_part(j).wait()
            R.gains[0] = R.gains[0] + R.gains[1 + j]

    extra[16] = gain_steps()
    service(19)
    finish_units()
    R.gains_out[...] = R.gains[0]
    store.wait()
    store_out.wait()


def widen(*refs):
    half = len(refs) // 2
    for src, dst in zip(refs[:half], refs[half:]):
        dst[...] = src[...].astype(dst.dtype)


def widened(arrays):
    steps = 4
    specs = []
    for x, _ in arrays:
        rows = x.shape[0] // steps if x.shape[0] % (8 * steps) == 0 else x.shape[0]
        last = x.shape[0] // rows - 1
        specs.append(pl.BlockSpec((rows, x.shape[1]), lambda i, last=last: (jnp.minimum(i, last), 0)))
    return pl.pallas_call(
        widen,
        grid=(steps,),
        out_shape=[jax.ShapeDtypeStruct(x.shape, d) for x, d in arrays],
        in_specs=specs,
        out_specs=specs,
        compiler_params=pltpu.CompilerParams(vmem_limit_bytes=60 << 20),
    )(*[x for x, _ in arrays])


def local(
    patches, cls_token, keep_mask, gain_time, qkv_time, proj_time, temporal_fc, gain_space, qkv_space, proj_space,
    gain_mlp, mlp_in, mlp_out, cotangent, cls_cotangent,
):
    _, frames, count, width = patches.shape
    heads_here, hd = qkv_time.shape[1], qkv_time.shape[3]

    def by_patch(x):
        return jnp.transpose(x[0], (1, 0, 2)).reshape(count * frames, width)

    def by_head(w):
        return jnp.transpose(w, (1, 2, 3, 0))

    def blocks(w):
        return w.reshape(-1, 64, width)

    large = dict(
        patches=by_patch(patches), cot=by_patch(cotangent), keep=keep_mask[0], wt_t_in=by_head(qkv_time),
        pj_t_in=proj_time, fc_in=blocks(temporal_fc), wt_s_in=by_head(qkv_space), pj_s_in=proj_space,
        w1_in=blocks(mlp_in), w2_in=blocks(mlp_out),
    )
    small = dict(gain_t=gain_time, gain_s=gain_space, gain_m=gain_mlp, cls=cls_token, ccot=cls_cotangent)
    frame_rows, square, row = (frames, count, width), (width // 64, 64, width), (1, width)
    heads = (heads_here, 3, hd, width)
    t_rows, s_rows, ours = (T_ROWS, width), (S_ROWS, width), (count * frames, width)
    in_hbm = dict(
        out=(ours, BF16), dx=(ours, F32), dw1=(square, BF16), dw2=(square, BF16), dfc=(square, BF16),
        dwt_s=(heads, BF16), dpj_s=(proj_space.shape, BF16), dwt_t=(heads, BF16), dpj_t=(proj_time.shape, BF16),
    )
    in_vmem = dict(ocls=(row, BF16), dcls=(row, F32), gains_out=((8, width), F32))
    levels = lax.axis_size("clip").bit_length() - 1
    vmem = dict(
        wt_t=((3,) + square, BF16), pj_t=(square, BF16), fc=(square, BF16), wt_s=((3,) + square, BF16),
        pj_s=(square, BF16), w1=((4,) + square, BF16), w2=((4,) + square, BF16),
        rows_in=((8, width), F32), patches_v=(t_rows, BF16), keep_v=(keep_mask.shape[1:], jnp.int32),
        kt_col=((T_ROWS, 1), F32), ks_row=((2, 1, 256), F32), ks_col=((S_ROWS, 1), F32), once=((S_ROWS, 1), F32),
        bias_t=((4, 112, 128), F32), u_t=(t_rows, BF16), qkv_t=((T_ROWS, 3 * width), BF16),
        p_t=((6, 4, 224, 128), BF16), mix_t=(t_rows, BF16), att_t=(t_rows, BF16),
        rows_x=(s_rows, F32), rows_s=(s_rows, F32), rows_c=(s_rows, F32), rows_a=(s_rows, F32), rows_d=(s_rows, F32),
        low_a=(s_rows, BF16), low_b=(s_rows, BF16), low_c=(s_rows, BF16), low_d=(s_rows, BF16),
        u_s=(s_rows, BF16), qkv_s=((S_ROWS, 3 * width), BF16), mix_s=(s_rows, BF16),
        p_s=((6, 2, 416, 256), BF16), dwt_own=((3,) + square, BF16), dqkv=((S_ROWS, 3 * width), BF16),
        perm=((width // 128, T_ROWS, 128), F32), send_a=(frame_rows, BF16),
        send_b=(frame_rows, BF16), got_first=(frame_rows, BF16), got_cot=(frame_rows, BF16),
        cls_sum=((4, 8, width), F32), dcls_sum=((4, 8, width), F32),
        dgain_t=(row, F32), dgain_s=(row, F32), dgain_m=(row, F32), gains=((3 + levels, 8, width), F32),
        near_a=((6, 2, 3, 64, width), BF16), near_b=((3, 2, 4, 64, width), BF16),
        near_c=((3, 2, width // 64, 64, 256), BF16),
    )
    pairs = dict(wy=14, wx=42, wc=14, wf=14, ex=12, row=6, gg=2 + levels)
    sems = dict(wo=14, exo=4, lo=6, go=15)
    for name, n in pairs.items():
        sems[name + "_s"] = n
        sems[name + "_r"] = n
    sems["gu_s"] = 30
    sems["gu_r"] = sum(arrivals(ROUTES[k], levels, k == 10) for k in range(15))
    flags = dict(free=15 * (levels + 1))
    names = [*large, *small, *in_hbm, *in_vmem, *vmem, *sems, *flags]
    hbm, vm = pl.BlockSpec(memory_space=pl.ANY), pl.BlockSpec(memory_space=pltpu.VMEM)
    output, dx, d_w1, d_w2, d_fc, d_qs, d_ps, d_qt, d_pt, out_cls, cls_grad, gains = pl.pallas_call(
        partial(whole_step, names, frames),
        out_shape=[jax.ShapeDtypeStruct(s, d) for s, d in [*in_hbm.values(), *in_vmem.values()]],
        in_specs=[hbm] * len(large) + [vm] * len(small),
        out_specs=[hbm] * len(in_hbm) + [vm] * len(in_vmem),
        scratch_shapes=[pltpu.VMEM(s, d) for s, d in vmem.values()]
        + [pltpu.SemaphoreType.DMA((n,)) for n in sems.values()]
        + [pltpu.SemaphoreType.REGULAR((n,)) for n in flags.values()],
        compiler_params=pltpu.CompilerParams(collective_id=0, has_side_effects=True, vmem_limit_bytes=60 << 20),
    )(*large.values(), *small.values())

    def by_frame(x):
        return jnp.transpose(x.reshape(count, frames, width), (1, 0, 2))[None]

    def by_width(w):
        return jnp.transpose(w.reshape(heads), (3, 0, 1, 2))

    grads = [(x.reshape(-1, width), F32) for x in (dx, d_w1, d_w2, d_fc, d_qs, d_ps, d_qt, d_pt)]
    output, dx, d_w1, d_w2, d_fc, d_qs, d_ps, d_qt, d_pt = widened([(output, BF16)] + grads)
    return (
        by_frame(output), out_cls, by_frame(dx), cls_grad, gains[0], by_width(d_qt), d_pt.reshape(proj_time.shape), d_fc,
        gains[1], by_width(d_qs), d_ps.reshape(proj_space.shape), gains[2], d_w1, d_w2,
    )


def solution(mesh):
    rows, wide, by_head = P("clip", None, "head", None), P("clip", None), P(None, "head", None, None)
    in_specs = (
        rows, wide, P("clip", None, None), P(), by_head, P("head", None, None), P(), P(), by_head,
        P("head", None, None), P(), P(None, "head"), P("head", None), rows, wide,
    )
    out_specs = (
        rows, wide, rows, wide, P(), by_head, P("head", None, None), P(), P(), by_head,
        P("head", None, None), P(), P(None, "head"), P("head", None),
    )
    return jax.shard_map(local, mesh=mesh, in_specs=in_specs, out_specs=out_specs, check_vma=False)
```

```python
from functools import partial
from types import SimpleNamespace

import jax
import jax.numpy as jnp
from jax import lax
from jax.experimental import pallas as pl
from jax.experimental.pallas import tpu as pltpu
from jax.sharding import PartitionSpec as P

EPSILON = 1e-06
NEGATIVE = -1e30
F32 = jnp.float32
BF16 = jnp.bfloat16


def nn(a, b):
    return lax.dot_general(a, b, (((1,), (0,)), ((), ())), preferred_element_type=F32)


def nt(a, b):
    return lax.dot_general(a, b, (((1,), (1,)), ((), ())), preferred_element_type=F32)


def tn(a, b):
    return lax.dot_general(a, b, (((0,), (0,)), ((), ())), preferred_element_type=F32)


def tiles(total, size, body):
    def step(i, carry):
        body(pl.multiple_of(i * size, size))
        return carry

    lax.fori_loop(0, total // size, step, 0)


def stats(x):
    center = x - jnp.mean(x, axis=-1, keepdims=True)
    factor = lax.rsqrt(jnp.mean(center * center, axis=-1, keepdims=True) + EPSILON)
    return center * factor, factor


def norm_back(grad, gain, scaled, factor):
    weighted = grad * gain
    inner = weighted - jnp.mean(weighted, axis=-1, keepdims=True)
    return factor * (inner - scaled * jnp.mean(weighted * scaled, axis=-1, keepdims=True))


def pair_masks():
    lane = lax.broadcasted_iota(jnp.int32, (1, 128), 1)
    return (lane < 64).astype(F32).astype(BF16), (lane >= 64).astype(F32).astype(BF16)


def stacked(x):
    low, high = pair_masks()
    return jnp.concatenate([x * low, x * high], axis=0)


def unstacked(x):
    rows = x.shape[0] // 2
    lane = lax.broadcasted_iota(jnp.int32, (1, 128), 1)
    return jnp.where(lane < 64, x[:rows], x[rows:])


def norm_rows(x_ref, gain_ref, u_ref, total, chunk):
    def body(r):
        rows = pl.ds(r, chunk)
        scaled, _ = stats(x_ref[rows, :])
        u_ref[rows, :] = (scaled * gain_ref[...]).astype(BF16)

    tiles(total, chunk, body)


def project_qkv(u_ref, wt_ref, qkv_ref, rows, first, last):
    width = u_ref.shape[1]
    size = (last - first) * 64

    def body(t, carry):
        scale = jnp.where(t == 0, 0.125, 1.0)
        out = nt(u_ref[:rows, :], wt_ref[t, first:last].reshape(size, width)) * scale
        qkv_ref[:rows, pl.ds(pl.multiple_of(t * width + first * 64, 128), size)] = out.astype(BF16)
        return carry

    lax.fori_loop(0, 3, body, 0)


def columns(ref, cols):
    part = ref[:, :, cols]
    return part.reshape(part.shape[0] * part.shape[1], part.shape[2])


def rows_of(ref, n):
    part = ref[pl.ds(n // 64, 4)]
    return part.reshape(256, part.shape[2])


def qkv_back(dqkv_ref, wt_ref, du_ref, rows):
    width = du_ref.shape[1]

    def back(n):
        cols = pl.ds(n, 256)
        total = nn(dqkv_ref[:rows, :width], columns(wt_ref.at[0], cols))
        total += nn(dqkv_ref[:rows, width : 2 * width], columns(wt_ref.at[1], cols))
        total += nn(dqkv_ref[:rows, 2 * width :], columns(wt_ref.at[2], cols))
        du_ref[:rows, cols] = total

    tiles(width, 256, back)


def qkv_grad(dqkv_ref, u_ref, wt_ref, rows):
    width = u_ref.shape[1]

    def grad(i, carry):
        cols = pl.ds(pl.multiple_of(i * 256, 256), 256)
        out = tn(dqkv_ref[:rows, cols], u_ref[:rows, :]).astype(BF16)
        wt_ref[i // 3, pl.ds((i % 3) * 4, 4)] = out.reshape(4, 64, width)
        return carry

    lax.fori_loop(0, 9, grad, 0)


def softmax(scores):
    highest = jnp.max(scores, axis=-1, keepdims=True)
    weights = jnp.exp(scores - highest)
    return weights * (1.0 / jnp.sum(weights, axis=-1, keepdims=True))


def attention(qkv_ref, p_ref, mix_ref, groups, bias_of, first, last):
    width = mix_ref.shape[1]

    def body(hp, carry):
        qc = pl.ds(pl.multiple_of(hp * 128, 128), 128)
        kc = pl.ds(pl.multiple_of(width + hp * 128, 128), 128)
        vc = pl.ds(pl.multiple_of(2 * width + hp * 128, 128), 128)
        all_rows = [pl.ds(start, size) for start, size in groups]
        scores = [nt(stacked(qkv_ref[rows, qc]), qkv_ref[rows, kc]) for rows in all_rows]
        probs = [softmax(scores[g] + bias_of(g, size)).astype(BF16) for g, (_, size) in enumerate(groups)]
        mixes = [unstacked(nn(prob, qkv_ref[rows, vc])).astype(BF16) for prob, rows in zip(probs, all_rows)]
        for g, (_, size) in enumerate(groups):
            p_ref[hp, g, : 2 * size, :size] = probs[g]
            mix_ref[all_rows[g], qc] = mixes[g]
        return carry

    lax.fori_loop(first, last, body, 0)


def attention_back(qkv_ref, p_ref, dmix_ref, dqkv_ref, groups, first, last):
    width = dmix_ref.shape[1]

    def body(hp, carry):
        qc = pl.ds(pl.multiple_of(hp * 128, 128), 128)
        kc = pl.ds(pl.multiple_of(width + hp * 128, 128), 128)
        vc = pl.ds(pl.multiple_of(2 * width + hp * 128, 128), 128)
        all_rows = [pl.ds(start, size) for start, size in groups]
        ups = [stacked(dmix_ref[rows, qc]) for rows in all_rows]
        probs = [p_ref[hp, g, : 2 * size, :size] for g, (_, size) in enumerate(groups)]
        dprobs = [nt(up, qkv_ref[rows, vc]) for up, rows in zip(ups, all_rows)]
        dvs = [tn(prob, up).astype(BF16) for prob, up in zip(probs, ups)]
        dscores = []
        for prob, dprob in zip(probs, dprobs):
            wide = prob.astype(F32)
            delta = jnp.sum(wide * dprob, axis=-1, keepdims=True)
            dscores.append((wide * (dprob - delta)).astype(BF16))
        dqs = [(unstacked(nn(ds, qkv_ref[rows, kc])) * 0.125).astype(BF16) for ds, rows in zip(dscores, all_rows)]
        dks = [tn(ds, stacked(qkv_ref[rows, qc])).astype(BF16) for ds, rows in zip(dscores, all_rows)]
        for g, rows in enumerate(all_rows):
            dqkv_ref[rows, qc] = dqs[g]
            dqkv_ref[rows, kc] = dks[g]
            dqkv_ref[rows, vc] = dvs[g]
        return carry

    lax.fori_loop(first, last, body, 0)


T_ROWS = 400
T_GROUPS = ((0, 96), (96, 96), (192, 96), (288, 112))
SEG = 208
S_ROWS = 416
S_GROUPS = ((0, 208), (208, 208))


def time_bias(kcol, size):
    row = lax.broadcasted_iota(jnp.int32, (size, size), 0)
    col = lax.broadcasted_iota(jnp.int32, (size, size), 1)
    kept = jnp.sum(jnp.where(row == col, kcol, 0.0), axis=0, keepdims=True)
    ok = ((row // 8) == (col // 8)) & ((kept > 0.0) | (row == col))
    return jnp.where(ok, 0.0, NEGATIVE)


def patch_keep(keep_ref, head, count, frames):
    total = keep_ref.shape[1]
    row = lax.broadcasted_iota(jnp.int32, (T_ROWS, total), 0)
    col = lax.broadcasted_iota(jnp.int32, (T_ROWS, total), 1)
    pick = ((row // frames + head * count == col) & (row < frames * count)).astype(F32).astype(BF16)
    by_frame = nt(pick, keep_ref[...].astype(F32).astype(BF16))
    row = lax.broadcasted_iota(jnp.int32, (T_ROWS, frames), 0)
    col = lax.broadcasted_iota(jnp.int32, (T_ROWS, frames), 1)
    return jnp.sum(jnp.where(row % frames == col, by_frame, 0.0), axis=1, keepdims=True)


def space_bias(krow_ref, g):
    return (krow_ref[g, :, :SEG] - 1.0) * (-NEGATIVE)


def to_patch_order(src_ref, dst_ref, perm_ref):
    frames, count, width = src_ref.shape
    used = frames * count
    for j in range(width // 128):
        for f in range(frames):
            perm_ref[j, pl.ds(f, count, stride=frames), :] = src_ref[f, :, j * 128 : (j + 1) * 128].astype(F32)
        dst_ref[:used, j * 128 : (j + 1) * 128] = perm_ref[j, :used, :]
    dst_ref[used:T_ROWS, :] = jnp.zeros((T_ROWS - used, width), F32)


def to_frame_order(src_ref, dst_ref, perm_ref):
    frames, count, width = dst_ref.shape
    for j in range(width // 128):
        used = frames * count
        perm_ref[j, :used, :] = src_ref[:used, j * 128 : (j + 1) * 128].astype(F32)
        for f in range(frames):
            out = perm_ref[j, pl.ds(f, count, stride=frames), :]
            dst_ref[f, :, j * 128 : (j + 1) * 128] = out.astype(dst_ref.dtype)


def gather_frames(got_ref, cls_row, out_ref):
    sources, count = got_ref.shape[0] // 2, got_ref.shape[1]
    for f in range(2):
        base = f * SEG
        for s in range(sources):
            out_ref[base + s * count : base + (s + 1) * count, :] = got_ref[2 * s + f].astype(F32)
        at = base + sources * count
        out_ref[at : at + 1, :] = cls_row[f]
        out_ref[at + 1 : base + SEG, :] = jnp.zeros((SEG - 1 - sources * count, out_ref.shape[1]), F32)


def scatter_frames(x_ref, send_ref):
    sources, count = send_ref.shape[0] // 2, send_ref.shape[1]
    for f in range(2):
        for s in range(sources):
            at = f * SEG + s * count
            send_ref[2 * s + f] = x_ref[at : at + count, :].astype(send_ref.dtype)


def cls_attention(qkv_ref, krow_ref, at, width):
    lane = lax.broadcasted_iota(jnp.int32, (16, width), 1) // 64
    own = (lane == lax.broadcasted_iota(jnp.int32, (16, width), 0)).astype(F32)
    total = jnp.zeros((1, width), F32)
    for f in range(2):
        q = qkv_ref[f * SEG + at : f * SEG + at + 1, :width].astype(F32)
        k = qkv_ref[f * SEG : (f + 1) * SEG, width : 2 * width]
        v = qkv_ref[f * SEG : (f + 1) * SEG, 2 * width :]
        prob = softmax(nt((own * q).astype(BF16), k) + space_bias(krow_ref, f))
        total += jnp.sum(own * nn(prob.astype(BF16), v), axis=0, keepdims=True)
    return total


def blocks_swapped(x, distance):
    width = x.shape[1]
    quarter = width // 4
    order = [i ^ distance for i in range(4)]
    return jnp.concatenate([x[:, i * quarter : (i + 1) * quarter] for i in order], axis=1)


def set_row(ref, base, at, row, dtype):
    start = base + at // 16 * 16
    pick = lax.broadcasted_iota(jnp.int32, (16, 1), 0) == at % 16
    kept = ref[start : start + 16, :].astype(F32)
    ref[start : start + 16, :] = jnp.where(pick, jnp.broadcast_to(row, kept.shape), kept).astype(dtype)


MESH = pl.DeviceIdType.MESH

ROUTES = (0, 0, 1, 0, 2, 1, 1, 0, 0, 1, 0, 0, 0, 0, 0)
ORDER = (
    (0, 1),
    (2, 3, 0, 1),
    (4, 5, 2, 3),
    (0, 4, 5),
    (),
    (),
    (1,),
    (),
    (0, 4),
    (2, 3),
    (0, 5),
    (6, 7, 8, 9, 1, 4),
    (10, 0, 3, 2, 6, 7, 1, 8, 9, 5, 10, 0, 4, 15),
    (11, 3),
    (2, 6, 1, 5, 11),
    (3, 9, 7),
    (0, 1, 2),
    (12, 13, 14, 3, 4, 5, 7, 8, 2),
    (1, 6, 4, 3, 12, 5, 13, 7, 8, 14, 10, 6, 11),
    (9, 8, 7, 2, 16, 6, 10, 12, 4, 9, 5, 11, 16, 8, 7, 15, 13, 6, 12, 10, 9, 16, 7, 11, 14, 8, 13, 12, 10, 16,
     6, 9, 11, 14, 13, 12, 8, 16, 10, 11, 9, 14, 13, 10, 12, 16, 14, 11, 13, 12, 14, 10, 13, 16, 10, 14),
)


def arrivals(route, levels, everywhere):
    return 2 + (3, 4, 5)[route] + levels - 2 + 2 + (3 if everywhere else 0)


def whole_step(names, frames, *refs):
    R = SimpleNamespace(**dict(zip(names, refs)))
    clip, head = lax.axis_index("clip"), lax.axis_index("head")
    digit = (clip % 2, clip // 2 % 2, clip // 4 % 2)
    side, turn = digit[0], digit[1]
    width = R.wt_t.shape[3]
    count = R.patches.shape[0] // frames
    at = 4 * count
    peer_c, peer_y, peer_d = (clip, head ^ 1), (clip, head ^ 2), (clip, head ^ 3)
    levels = lax.axis_size("clip").bit_length() - 1
    bits = [(clip ^ (1 << j), head) for j in range(levels)]

    def part(ref, q, n):
        return ref.at[:, pl.ds(q * 16, n * 16), :]

    def hidden_tile(w1, w2, i, q, n):
        t = (i - 8) // 2
        if i % 2:
            return w1.at[:, pl.ds(q * 16, n * 16), pl.ds(t * 256, 256)]
        return part(w2.at[pl.ds(t * 4, 4)], q, n)

    def slot(i, s, q=0, n=4):
        if i >= 8:
            return hidden_tile(R.w1.at[s], R.w2.at[s], i, q, n)
        wt, pj = (R.wt_t, R.pj_t) if i < 4 else (R.wt_s, R.pj_s)
        if i % 4 == 3:
            return part(pj.at[pl.ds(s * 3, 3)], q, n)
        return part(wt.at[:, s * 3 + i % 4], q, n)

    def source(i, q=0, n=4):
        if i >= 8:
            return hidden_tile(R.w1_in, R.w2_in, i, q, n)
        wt, pj = (R.wt_t_in, R.pj_t_in) if i < 4 else (R.wt_s_in, R.pj_s_in)
        return part(pj if i % 4 == 3 else wt.at[i % 4], q, n)

    def remote(src, dst, sems, index, peer):
        return pltpu.make_async_remote_copy(
            src_ref=src, dst_ref=dst, send_sem=sems[0].at[index], recv_sem=sems[1].at[index],
            device_id=peer, device_id_type=MESH,
        )

    mine = side + 2 * turn

    def y_copy(i):
        return remote(source(i, mine, 1), slot(i, 2, mine, 1), (R.wy_s, R.wy_r), i, peer_y)

    def clip_copies(i):
        quarter = slot(i, 2, mine, 1)
        near = (bits[0], bits[1], (clip ^ 3, head))
        return [remote(quarter, quarter, (R.wx_s, R.wx_r), 3 * i + n, peer) for n, peer in enumerate(near)]

    def c_copy(i):
        return remote(source(i), slot(i, 1), (R.wc_s, R.wc_r), i, peer_c)

    def f_copy(i):
        return remote(slot(i, 2), slot(i, 3), (R.wf_s, R.wf_r), i, peer_c)

    def own_copy(i):
        return pltpu.make_async_copy(source(i), slot(i, 0), R.wo.at[i])

    def pass_near(*pieces):
        for i in pieces:
            y_copy(i).wait_recv()
            for copy in clip_copies(i):
                copy.start()

    def pass_far(*pieces):
        for i in pieces:
            for copy in clip_copies(i):
                copy.wait_recv()
            f_copy(i).start()

    def ready_near(*pieces):
        for i in pieces:
            own_copy(i).wait()
            c_copy(i).wait_recv()

    def ready_far(*pieces):
        for i in pieces:
            f_copy(i).wait_recv()

    def sent(*pieces):
        for i in pieces:
            y_copy(i).wait_send()
            c_copy(i).wait_send()
            f_copy(i).wait_send()
            for copy in clip_copies(i):
                copy.wait_send()

    def exchange(k, src, dst):
        here = pl.ds(2 * head, 2)
        copies = []
        for r, peer in ((2, peer_y), (3, peer_d), (1, peer_c)):
            there = pl.ds(2 * (head ^ r), 2)
            copies.append(remote(src.at[there], dst.at[here], (R.ex_s, R.ex_r), 3 * k + r - 1, peer))
        copies.append(pltpu.make_async_copy(src.at[here], dst.at[here], R.exo.at[k]))
        return copies

    def all_start(copies):
        for copy in copies:
            copy.start()

    def all_wait(copies):
        for copy in copies:
            copy.wait()

    def sum_rows(k, buf, swapped):
        copies = [
            remote(buf.at[0], buf.at[r], (R.row_s, R.row_r), 3 * k + r - 1, peer)
            for r, peer in ((2, peer_y), (3, peer_d), (1, peer_c))
        ]
        all_start(copies)

        def finish():
            all_wait(copies)
            terms = [buf[r] for r in range(4)]
            if swapped:
                terms = [terms[0]] + [blocks_swapped(terms[r], r) for r in (1, 2, 3)]
            total = (terms[0] + terms[1]) + (terms[2] + terms[3])
            return total[0:1, :]

        return finish

    def unit(i):
        if i < 6:
            n = i // 2
            if i % 2:
                return lambda s, q=0, k=4: R.w1.at[s, :, pl.ds(q * 16, k * 16), pl.ds(n * 256, 256)]
            return lambda s, q=0, k=4: part(R.w2.at[s, pl.ds(n * 4, 4)], q, k)
        if i == 10:
            return lambda s, q=0, k=4: part(R.fc.at[pl.ds((head ^ s) * 3, 3)], q, k)
        wt, pj = (R.wt_s, R.pj_s) if i < 10 else (R.dwt_own, R.pj_t)
        n = i - 6 if i < 10 else i - 11
        if n == 0:
            return lambda s, q=0, k=4: part(pj.at[pl.ds(s * 3, 3)], q, k)
        return lambda s, q=0, k=4: part(wt.at[:, s * 3 + n - 1], q, k)

    def result(i, q, k):
        if i < 6:
            n = i // 2
            if i % 2:
                return R.dw1.at[:, pl.ds(q * 16, k * 16), pl.ds(n * 256, 256)]
            return part(R.dw2.at[pl.ds(n * 4, 4)], q, k)
        if i == 10:
            return part(R.dfc.at[pl.ds(head * 3, 3)], q, k)
        wt, pj = (R.dwt_s, R.dpj_s) if i < 10 else (R.dwt_t, R.dpj_t)
        n = i - 6 if i < 10 else i - 11
        return part(pj if n == 0 else wt.at[n - 1], q, k)

    def near_slot(i, k):
        if i < 6:
            return (R.near_c if i % 2 else R.near_b).at[i // 2, k]
        if i < 9:
            return R.near_b.at[i - 6, k, pl.ds(0, 3)]
        return R.near_a.at[i - 9, k]

    def add(dst, src):
        def body(r, carry):
            dst[r] = dst[r] + src[r]
            return carry

        lax.fori_loop(0, dst.shape[0], body, 0)

    def steps_of(i):
        u, route = unit(i), ROUTES[i]
        a, b = (1, 2) if route == 2 else (0, 1)
        half = 2 * digit[a]
        quarter = half + digit[b]
        counts = [sum(arrivals(ROUTES[k], levels, k == 10) for k in range(i)), 0]

        def copy(src, dst, peer):
            counts[0] += 1
            return pltpu.make_async_remote_copy(
                src_ref=src, dst_ref=dst, send_sem=R.gu_s.at[i * 2 + counts[0] % 2], recv_sem=R.gu_r.at[counts[0] - 1],
                device_id=peer, device_id_type=MESH,
            )

        def land(k):
            at_q = counts[1]
            counts[1] += k
            s, q = ((1, at_q) if at_q < 4 else (3, at_q - 4) if at_q < 8 else (2, at_q - 8))
            return u(s, q, k), (s, q, k)

        steps = [([copy(u(1), near_slot(i, 0), peer_c), copy(u(3), near_slot(i, 1), peer_c)],
                  [(u(2), near_slot(i, 1)), (u(0), near_slot(i, 0))], None)]
        peers = []
        kept, joined = (0, 4), False
        whole_bits = [j for j in range(levels) if j not in (a, b)]
        order = ((-1, a, b), (a, -1, b), (a, b, -1))[route]
        for bit in list(order) + whole_bits:
            copies, sums = [], []
            if bit == -1:
                spot, (s, q, k) = land(kept[1])
                copies.append(copy(u(2, *kept), u(s ^ 2, q, k) if i == 10 else spot, peer_y))
                sums.append((u(0, *kept), spot))
                joined = True
                peers.append(peer_y)
            else:
                if bit == a:
                    kept, other = (half, 2), (2 - half, 2)
                elif bit == b:
                    kept, other = (quarter, 1), (half + 1 - digit[b], 1)
                else:
                    other = kept
                for s in (0,) if joined else (0, 2):
                    spot, _ = land(other[1])
                    copies.append(copy(u(s, *other), spot, bits[bit]))
                    sums.append((u(s, *kept), spot))
                peers.append(bits[bit])
            steps.append((copies, sums, len(peers) - 1))
        mine_q, there_q, rows = u(0, quarter, 1), result(i, quarter, 1), result(i, half, 2)
        steps.append(([copy(mine_q, there_q, bits[b]), pltpu.make_async_copy(mine_q, there_q, R.go.at[i])], [], None))
        steps.append(([copy(rows, rows, bits[a])], [], None))
        if i == 10:
            ours, far = R.dfc.at[pl.ds(head * 3, 3)], R.dfc.at[pl.ds((head ^ 2) * 3, 3)]
            steps.append(([copy(ours, ours, peer_y), copy(ours, ours, peer_c)], [], None))
            steps.append(([copy(far, far, peer_c)], [], None))
        return steps, peers

    units = [None] * 15
    stage = [0] * 15

    def tell(i, first, last):
        peers = units[i][1]
        for k in range(first, min(last, len(peers))):
            pl.semaphore_signal(R.free.at[i * (levels + 1) + k], inc=1, device_id=peers[k], device_id_type=MESH)

    def land_step(i):
        steps, _ = units[i]
        copies, sums, _ = steps[stage[i] - 1]
        all_wait(copies)
        if stage[i] == 1:
            tell(i, 0, 4)
        for dst, src in sums:
            add(dst, src)
        if stage[i] == 4:
            tell(i, 4, 8)

    landed = [0] * 15

    def advance(i):
        if units[i] is None:
            units[i] = steps_of(i)
        steps, _ = units[i]
        if stage[i] > landed[i]:
            land_step(i)
            landed[i] = stage[i]
        if stage[i] < len(steps):
            copies, _, credit = steps[stage[i]]
            if credit is not None:
                pl.semaphore_wait(R.free.at[i * (levels + 1) + credit], 1)
            all_start(copies)
        stage[i] += 1

    def join_core(i):
        if stage[i] == 1 and landed[i] == 0:
            land_step(i)
            landed[i] = 1

    extra = {}

    def service(k):
        for i in ORDER[k]:
            if i < 15:
                advance(i)
            else:
                next(extra[i], None)

    def finish_units():
        while any(stage[i] < 1 + len(units[i][0]) for i in range(15)):
            for i in reversed(range(15)):
                done = [stage[j] >= 1 + len(units[j][0]) for j in (i, i - 1)]
                if not done[0] and (i == 0 or done[1] or stage[i] < stage[i - 1]):
                    advance(i)
        for steps in extra.values():
            for _ in steps:
                pass

    barrier = pltpu.get_barrier_semaphore()
    for peer in [peer_c, peer_y, peer_d, (clip ^ 3, head)] + bits:
        pl.semaphore_signal(barrier, inc=1, device_id=peer, device_id_type=MESH)
    pl.semaphore_wait(barrier, 4 + levels)

    loads = (
        (R.patches, R.patches_v.at[pl.ds(0, frames * count)]), (R.keep, R.keep_v), (R.cot, R.low_d.at[pl.ds(0, frames * count)]), (R.fc_in, R.fc),
    )
    loads = [pltpu.make_async_copy(src, dst, R.lo.at[i]) for i, (src, dst) in enumerate(loads)]
    for i in range(3):
        loads[i].start()
    for i in range(12):
        y_copy(i).start()
    for i in range(14):
        own_copy(i).start()
        c_copy(i).start()
    loads[3].start()

    rows_x, first = R.rows_x, R.rows_s
    qkv_t, p_t, mix_t, att_t, u_t = R.qkv_t, R.p_t, R.mix_t, R.att_t, R.u_t
    patches, gains = R.patches_v, R.rows_in
    for n, row in enumerate((R.gain_t, R.gain_s, R.gain_m)):
        gains[n : n + 1, :] = row[...].reshape(1, width)
    gains[3:4, :] = R.cls[...].astype(F32)
    gains[4:5, :] = R.ccot[...].astype(F32)
    gain_t, gain_s, gain_m = gains.at[0:1], gains.at[1:2], gains.at[2:3]
    used = frames * count
    loads[0].wait()
    patches[used:, :] = jnp.zeros((T_ROWS - used, width), BF16)

    def norm_time(r):
        rows = pl.ds(r, 80)
        scaled, _ = stats(patches[rows, :].astype(F32))
        u_t[rows, :] = (scaled * gain_t[...]).astype(BF16)

    tiles(T_ROWS, 80, norm_time)
    pass_near(0)
    loads[1].wait()
    keep_col = patch_keep(R.keep_v, head, count, frames)
    R.kt_col[...] = keep_col
    for g, (start, size) in enumerate(T_GROUPS):
        R.bias_t[g, :size, :size] = time_bias(keep_col[start : start + size], size)
    R.ks_row[...] = jnp.zeros_like(R.ks_row)
    lane = lax.broadcasted_iota(jnp.int32, (1, 256), 1)
    row = lax.broadcasted_iota(jnp.int32, (SEG, SEG), 0)
    col = lax.broadcasted_iota(jnp.int32, (SEG, SEG), 1)
    for f in range(2):
        R.ks_row[f, :, :at] = R.keep_v[pl.ds(2 * head + f, 1), :].astype(F32)
        open_row = jnp.where(lane == at, 1.0, R.ks_row[f])
        R.ks_row[f] = open_row
        counted = (row == col) if f == 0 else (row == col) & (col != at)
        R.ks_col[f * SEG : (f + 1) * SEG, :] = jnp.sum(jnp.where(counted, open_row[:, :SEG], 0.0), axis=1, keepdims=True)
    row = lax.broadcasted_iota(jnp.int32, (S_ROWS, 1), 0)
    R.once[...] = jnp.where((row == at) & (head != 0), 0.0, 1.0)
    loads[2].wait()
    to_frame_order(R.low_d, R.send_b, R.perm)
    ex_cot = exchange(1, R.send_b, R.got_cot)
    pass_near(1, 2, 3)

    def time_bias_of(g, size):
        bias = R.bias_t[g, :size, :size]
        return jnp.concatenate([bias, bias], axis=0)

    ready_near(0, 1, 2, 3)
    project_qkv(u_t, R.wt_t, qkv_t, T_ROWS, 0, 6)
    attention(qkv_t, p_t, mix_t, T_GROUPS, time_bias_of, 0, 3)
    pass_near(4, 5, 6, 7)
    pass_far(0, 1, 2)
    ready_far(0, 1, 2)
    pass_far(3)
    pass_near(8, 9)
    project_qkv(u_t, R.wt_t, qkv_t, T_ROWS, 6, 12)
    attention(qkv_t, p_t, mix_t, T_GROUPS, time_bias_of, 3, 6)
    pass_near(10, 11)
    ready_far(3)
    loads[3].wait()

    def project(n):
        cols = pl.ds(n, 256)
        att_t[:, cols] = nn(mix_t[...], columns(R.pj_t, cols)).astype(BF16)

    tiles(width, 256, project)

    def branch(n):
        cols = pl.ds(n, 256)
        first[:T_ROWS, cols] = patches[:, cols].astype(F32) + R.kt_col[...] * nn(att_t[...], columns(R.fc, cols))

    tiles(width, 256, branch)
    to_frame_order(first, R.send_a, R.perm)
    ex_first = exchange(0, R.send_a, R.got_first)
    all_start(ex_first)
    for i in (12, 13):
        y_copy(i).start()
    all_start(ex_cot)
    pass_far(4, 5, 6, 7)

    qkv_s, p_s, mix_s, u_s = R.qkv_s, R.p_s, R.mix_s, R.u_s
    all_wait(ex_first)
    cls_row = gains[3:4, :]
    second, cot = R.rows_s, R.rows_c
    gather_frames(R.got_first, (cls_row, cls_row), rows_x)
    norm_rows(rows_x, gain_s, u_s, S_ROWS, 208)
    ready_near(4, 5, 6, 7)
    ready_far(4, 5, 6, 7)
    project_qkv(u_s, R.wt_s, qkv_s, S_ROWS, 0, 12)
    pass_near(12, 13)
    all_wait(ex_cot)
    gather_frames(R.got_cot, (gains[4:5, :], jnp.zeros((1, width), F32)), cot)
    cls_part = cls_attention(qkv_s, R.ks_row, at, width)
    R.cls_sum[0] = jnp.broadcast_to(cls_part, (8, width))
    cls_total = sum_rows(0, R.cls_sum, True)
    attention(qkv_s, p_s, mix_s, S_GROUPS, lambda g, size: space_bias(R.ks_row, g), 0, 6)
    set_row(mix_s, 0, at, cls_total() * (1.0 / frames), BF16)
    set_row(mix_s, SEG, at, jnp.zeros((1, width), F32), BF16)
    pass_far(8, 9)

    def project_space(n):
        cols = pl.ds(n, 256)
        second[:, cols] = rows_x[:, cols] + R.ks_col[...] * nn(mix_s[...], columns(R.pj_s, cols))

    tiles(width, 256, project_space)

    u, uw, dz, dzw = R.low_a, R.low_b, R.low_c, R.low_d
    acc, du = R.rows_a, R.rows_d
    kcol, once = R.ks_col, R.once

    def prepare(r):
        rows = pl.ds(r, 208)
        scaled, _ = stats(second[rows, :])
        low = (scaled * gain_m[...]).astype(BF16)
        u[rows, :] = low
        uw[rows, :] = (low.astype(F32) * once[rows, :]).astype(BF16)
        grad = cot[rows, :] * kcol[rows, :]
        dz[rows, :] = grad.astype(BF16)
        dzw[rows, :] = (grad * once[rows, :]).astype(BF16)

    tiles(S_ROWS, 208, prepare)
    acc[...] = jnp.zeros_like(acc)
    du[...] = jnp.zeros_like(du)
    w1_ref, w2_ref = R.w1, R.w2
    def hidden(s, n):
        cols = pl.ds(n * 256, 256)
        w1 = columns(w1_ref.at[s], cols)
        w2 = rows_of(w2_ref.at[s], n * 256)
        hid = nn(u[...], w1)
        phi = 0.5 + 0.5 * lax.erf(hid * 0.7071067811865476)
        act = (hid * phi).astype(BF16)
        slope = phi + hid * (0.3989422804014327 * jnp.exp(hid * hid * -0.5))
        acc[...] += nn(act, w2)
        dhid = (nt(dz[...], w2) * slope).astype(BF16)
        du[...] += nt(dhid, w1)
        w2_ref[s, n * 4 : n * 4 + 4] = tn(act, dzw[...]).astype(BF16).reshape(4, 64, width)
        w1_ref[s, :, :, cols] = tn(uw[...], dhid).astype(BF16).reshape(width // 64, 64, 256)

    for n in range(width // 256):
        if n:
            pass_far(8 + 2 * n, 9 + 2 * n)
        ready_near(8 + 2 * n, 9 + 2 * n)
        ready_far(8 + 2 * n, 9 + 2 * n)
        sent(8 + 2 * n, 9 + 2 * n)

        def by_slot(s, carry, n=n):
            hidden(s, n)
            return carry

        lax.fori_loop(0, 4, by_slot, 0)
        service(n)
    R.dgain_m[...] = jnp.zeros((1, width), F32)

    def finish_mlp(r):
        rows = pl.ds(r, 208)
        x = second[rows, :]
        scaled, factor = stats(x)
        acc[rows, :] = x + kcol[rows, :] * acc[rows, :]
        grad = du[rows, :]
        R.dgain_m[...] += jnp.sum(grad * scaled * once[rows, :], axis=0, keepdims=True)
        cot[rows, :] += norm_back(grad, gain_m[...], scaled, factor)

    tiles(S_ROWS, 208, finish_mlp)
    R.ocls[...] = acc[at : at + 1, :].astype(BF16)
    scatter_frames(acc, R.send_b)
    ex_out = exchange(2, R.send_b, R.got_cot)

    def out_steps():
        all_start(ex_out)
        yield
        all_wait(ex_out)
        to_patch_order(R.got_cot, rows_x, R.perm)
        R.low_d[:T_ROWS, :] = rows_x[:T_ROWS, :].astype(BF16)
        store_out.start()

    used = frames * count
    store_out = pltpu.make_async_copy(R.low_d.at[pl.ds(0, used)], R.out, R.lo.at[5])
    extra[15] = out_steps()
    service(3)

    dsecond = cot
    low, loww, dmix, dqkv = R.low_a, R.low_b, R.low_c, R.dqkv
    low[...] = (dsecond[...] * kcol[...]).astype(BF16)
    loww[...] = (dsecond[...] * (kcol[...] * once[...])).astype(BF16)
    dcls_second = dsecond[at : at + 1, :]
    set_row(low, SEG, at, dcls_second, BF16)
    sent(4, 5, 6, 7)

    def back_space(n):
        cols = pl.ds(n, 256)
        dmix[:, cols] = nt(low[...], rows_of(R.pj_s, n)).astype(BF16)

    tiles(width, 256, back_space)
    service(4)
    dcls_mix = dmix[SEG - 16 : SEG, :].astype(F32)[at - SEG + 16 : at - SEG + 17, :] * (1.0 / frames)
    set_row(dmix, 0, at, dcls_mix, BF16)
    set_row(dmix, SEG, at, dcls_mix, BF16)
    for n in range(3):
        attention_back(qkv_s, p_s, dmix, dqkv, S_GROUPS, 2 * n, 2 * n + 2)
        service(5 + n)
    qkv_back(dqkv, R.wt_s, du, S_ROWS)
    service(8)
    R.dcls_sum[0] = jnp.broadcast_to(du[at : at + 1, :] + du[SEG + at : SEG + at + 1, :], (8, width))
    R.dgain_s[...] = jnp.zeros((1, width), F32)
    dfirst = R.rows_a

    def finish_space(r):
        rows = pl.ds(r, 208)
        scaled, factor = stats(rows_x[rows, :])
        grad = du[rows, :]
        R.dgain_s[...] += jnp.sum(grad * scaled, axis=0, keepdims=True)
        dfirst[rows, :] = dsecond[rows, :] + norm_back(grad, gain_s[...], scaled, factor)

    tiles(S_ROWS, 208, finish_space)
    scatter_frames(dfirst, R.send_a)
    for i in range(6):
        join_core(i)
    ex_df = exchange(3, R.send_a, R.got_first)
    all_start(ex_df)
    dcls_total = sum_rows(1, R.dcls_sum, False)
    service(9)

    def grad_space(n):
        cols = pl.ds(n, 256)
        R.pj_s[pl.ds(n // 64, 4)] = tn(mix_s[:, cols], loww[...]).astype(BF16).reshape(4, 64, width)

    tiles(width, 256, grad_space)
    qkv_grad(dqkv, u_s, R.wt_s, S_ROWS)
    service(10)

    df = R.rows_s
    all_wait(ex_df)
    service(11)
    to_patch_order(R.got_first, df, R.perm)
    scaled, factor = stats(cls_row)
    R.dcls[...] = dcls_second + norm_back(dcls_total(), gain_s[...], scaled, factor)
    low, datt, dmix = R.low_a, R.low_b, R.low_c
    low[:T_ROWS, :] = (df[:T_ROWS, :] * R.kt_col[...]).astype(BF16)
    sent(0, 1, 2, 3)

    def back_fc(n):
        cols = pl.ds(n, 256)
        datt[:T_ROWS, cols] = nt(low[:T_ROWS, :], rows_of(R.fc, n)).astype(BF16)
        R.fc[pl.ds(n // 64, 4)] = tn(att_t[:, cols], low[:T_ROWS, :]).astype(BF16).reshape(4, 64, width)

    tiles(width, 256, back_fc)
    service(12)

    def back_time(n):
        cols = pl.ds(n, 256)
        dmix[:T_ROWS, cols] = nt(datt[:T_ROWS, :], rows_of(R.pj_t, n)).astype(BF16)
        R.pj_t[pl.ds(n // 64, 4)] = tn(mix_t[:, cols], datt[:T_ROWS, :]).astype(BF16).reshape(4, 64, width)

    tiles(width, 256, back_time)
    service(13)
    for n in range(3):
        attention_back(qkv_t, p_t, dmix, dqkv, T_GROUPS, 2 * n, 2 * n + 2)
        service(14 + n)
    qkv_grad(dqkv, u_t, R.dwt_own, T_ROWS)
    service(17)
    qkv_back(dqkv, R.wt_t, du, T_ROWS)
    service(18)
    R.dgain_t[...] = jnp.zeros((1, width), F32)

    def finish_time(r):
        rows = pl.ds(r, 80)
        scaled, factor = stats(patches[rows, :].astype(F32))
        grad = du[rows, :]
        R.dgain_t[...] += jnp.sum(grad * scaled, axis=0, keepdims=True)
        df[rows, :] += norm_back(grad, gain_t[...], scaled, factor)

    tiles(T_ROWS, 80, finish_time)
    store = pltpu.make_async_copy(df.at[pl.ds(0, used)], R.dx, R.lo.at[4])
    store.start()
    for n, gain in enumerate((R.dgain_t, R.dgain_s, R.dgain_m)):
        R.gains[0, n : n + 1, :] = gain[...]
    def gain_part(j):
        peer = ([peer_c, peer_y] + bits)[j]
        return remote(R.gains.at[0], R.gains.at[1 + j], (R.gg_s, R.gg_r), j, peer)

    def gain_steps():
        for j in range(2 + levels):
            gain_part(j).start()
            yield
            gain_part(j).wait()
            R.gains[0] = R.gains[0] + R.gains[1 + j]

    extra[16] = gain_steps()
    service(19)
    finish_units()
    for n, ref in enumerate((R.g_t, R.g_s, R.g_m)):
        ref[...] = R.gains[0, n : n + 1, :].reshape(width)
    store.wait()
    store_out.wait()


def widen(*refs):
    half = len(refs) // 2
    for src, dst in zip(refs[:half], refs[half:]):
        dst[...] = src[...].astype(dst.dtype)


def widened(arrays):
    steps = 4
    specs = []
    for x, _ in arrays:
        if x.ndim == 1 or x.shape[0] == 1:
            specs.append(pl.BlockSpec(x.shape, lambda i, n=x.ndim: (0,) * n))
            continue
        rows = x.shape[0] // steps if x.shape[0] % (8 * steps) == 0 else x.shape[0]
        last = x.shape[0] // rows - 1
        specs.append(pl.BlockSpec((rows, x.shape[1]), lambda i, last=last: (jnp.minimum(i, last), 0)))
    return pl.pallas_call(
        widen,
        grid=(steps,),
        out_shape=[jax.ShapeDtypeStruct(x.shape, d) for x, d in arrays],
        in_specs=specs,
        out_specs=specs,
        compiler_params=pltpu.CompilerParams(vmem_limit_bytes=60 << 20),
    )(*[x for x, _ in arrays])


def local(
    patches, cls_token, keep_mask, gain_time, qkv_time, proj_time, temporal_fc, gain_space, qkv_space, proj_space,
    gain_mlp, mlp_in, mlp_out, cotangent, cls_cotangent,
):
    _, frames, count, width = patches.shape
    heads_here, hd = qkv_time.shape[1], qkv_time.shape[3]

    def by_patch(x):
        return jnp.transpose(x[0], (1, 0, 2)).reshape(count * frames, width)

    def by_head(w):
        return jnp.transpose(w, (1, 2, 3, 0))

    def blocks(w):
        return w.reshape(-1, 64, width)

    large = dict(
        patches=by_patch(patches), cot=by_patch(cotangent), keep=keep_mask[0], wt_t_in=by_head(qkv_time),
        pj_t_in=proj_time, fc_in=blocks(temporal_fc), wt_s_in=by_head(qkv_space), pj_s_in=proj_space,
        w1_in=blocks(mlp_in), w2_in=blocks(mlp_out),
    )
    small = dict(gain_t=gain_time, gain_s=gain_space, gain_m=gain_mlp, cls=cls_token, ccot=cls_cotangent)
    frame_rows, square, row = (frames, count, width), (width // 64, 64, width), (1, width)
    heads = (heads_here, 3, hd, width)
    t_rows, s_rows, ours = (T_ROWS, width), (S_ROWS, width), (count * frames, width)
    in_hbm = dict(
        out=(ours, BF16), dx=(ours, F32), dw1=(square, BF16), dw2=(square, BF16), dfc=(square, BF16),
        dwt_s=(heads, BF16), dpj_s=(proj_space.shape, BF16), dwt_t=(heads, BF16), dpj_t=(proj_time.shape, BF16),
    )
    in_vmem = dict(ocls=(row, BF16), dcls=(row, F32), g_t=((width,), F32), g_s=((width,), F32), g_m=((width,), F32))
    levels = lax.axis_size("clip").bit_length() - 1
    vmem = dict(
        wt_t=((3,) + square, BF16), pj_t=(square, BF16), fc=(square, BF16), wt_s=((3,) + square, BF16),
        pj_s=(square, BF16), w1=((4,) + square, BF16), w2=((4,) + square, BF16),
        rows_in=((8, width), F32), patches_v=(t_rows, BF16), keep_v=(keep_mask.shape[1:], jnp.int32),
        kt_col=((T_ROWS, 1), F32), ks_row=((2, 1, 256), F32), ks_col=((S_ROWS, 1), F32), once=((S_ROWS, 1), F32),
        bias_t=((4, 112, 128), F32), u_t=(t_rows, BF16), qkv_t=((T_ROWS, 3 * width), BF16),
        p_t=((6, 4, 224, 128), BF16), mix_t=(t_rows, BF16), att_t=(t_rows, BF16),
        rows_x=(s_rows, F32), rows_s=(s_rows, F32), rows_c=(s_rows, F32), rows_a=(s_rows, F32), rows_d=(s_rows, F32),
        low_a=(s_rows, BF16), low_b=(s_rows, BF16), low_c=(s_rows, BF16), low_d=(s_rows, BF16),
        u_s=(s_rows, BF16), qkv_s=((S_ROWS, 3 * width), BF16), mix_s=(s_rows, BF16),
        p_s=((6, 2, 416, 256), BF16), dwt_own=((3,) + square, BF16), dqkv=((S_ROWS, 3 * width), BF16),
        perm=((width // 128, T_ROWS, 128), F32), send_a=(frame_rows, BF16),
        send_b=(frame_rows, BF16), got_first=(frame_rows, BF16), got_cot=(frame_rows, BF16),
        cls_sum=((4, 8, width), F32), dcls_sum=((4, 8, width), F32),
        dgain_t=(row, F32), dgain_s=(row, F32), dgain_m=(row, F32), gains=((3 + levels, 8, width), F32),
        near_a=((6, 2, 3, 64, width), BF16), near_b=((3, 2, 4, 64, width), BF16),
        near_c=((3, 2, width // 64, 64, 256), BF16),
    )
    pairs = dict(wy=14, wx=42, wc=14, wf=14, ex=12, row=6, gg=2 + levels)
    sems = dict(wo=14, exo=4, lo=6, go=15)
    for name, n in pairs.items():
        sems[name + "_s"] = n
        sems[name + "_r"] = n
    sems["gu_s"] = 30
    sems["gu_r"] = sum(arrivals(ROUTES[k], levels, k == 10) for k in range(15))
    flags = dict(free=15 * (levels + 1))
    names = [*large, *small, *in_hbm, *in_vmem, *vmem, *sems, *flags]
    hbm, vm = pl.BlockSpec(memory_space=pl.ANY), pl.BlockSpec(memory_space=pltpu.VMEM)
    output, dx, d_w1, d_w2, d_fc, d_qs, d_ps, d_qt, d_pt, out_cls, cls_grad, *gains = pl.pallas_call(
        partial(whole_step, names, frames),
        out_shape=[jax.ShapeDtypeStruct(s, d) for s, d in [*in_hbm.values(), *in_vmem.values()]],
        in_specs=[hbm] * len(large) + [vm] * len(small),
        out_specs=[hbm] * len(in_hbm) + [vm] * len(in_vmem),
        scratch_shapes=[pltpu.VMEM(s, d) for s, d in vmem.values()]
        + [pltpu.SemaphoreType.DMA((n,)) for n in sems.values()]
        + [pltpu.SemaphoreType.REGULAR((n,)) for n in flags.values()],
        compiler_params=pltpu.CompilerParams(collective_id=0, has_side_effects=True, vmem_limit_bytes=60 << 20),
    )(*large.values(), *small.values())

    def by_frame(x):
        return jnp.transpose(x.reshape(count, frames, width), (1, 0, 2))[None]

    def by_width(w):
        return jnp.transpose(w.reshape(heads), (3, 0, 1, 2))

    grads = [(x.reshape(-1, width), F32) for x in (dx, d_w1, d_w2, d_fc, d_qs, d_ps, d_qt, d_pt)]
    rest = [(out_cls, BF16), (cls_grad, F32)] + [(x, F32) for x in gains]
    output, dx, d_w1, d_w2, d_fc, d_qs, d_ps, d_qt, d_pt, out_cls, cls_grad, *gains = widened([(output, BF16)] + grads + rest)
    return (
        by_frame(output), out_cls, by_frame(dx), cls_grad, gains[0], by_width(d_qt), d_pt.reshape(proj_time.shape), d_fc,
        gains[1], by_width(d_qs), d_ps.reshape(proj_space.shape), gains[2], d_w1, d_w2,
    )


def solution(mesh):
    rows, wide, by_head = P("clip", None, "head", None), P("clip", None), P(None, "head", None, None)
    in_specs = (
        rows, wide, P("clip", None, None), P(), by_head, P("head", None, None), P(), P(), by_head,
        P("head", None, None), P(), P(None, "head"), P("head", None), rows, wide,
    )
    out_specs = (
        rows, wide, rows, wide, P(), by_head, P("head", None, None), P(), P(), by_head,
        P("head", None, None), P(), P(None, "head"), P("head", None),
    )
    return jax.shard_map(local, mesh=mesh, in_specs=in_specs, out_specs=out_specs, check_vma=False)
```
